512 devices in a mesh: tile: 128 (over x, z, core), mode: 4 (over y).
Axes of the slice: x: 4, y: 4, z: 16, core: 2. Of those that a mesh axis runs over, the one named last changes fastest.
Arguments:
- obj_x: float32 [2, 4096, 512], P(None, 'tile', 'mode'), may hold values from -6 to 6
- dual_u: float32 [2, 4096, 512], P(None, 'tile', 'mode'), may hold values from -6 to 6
- probes: float32 [4, 2, 256, 256], P('mode'), may hold values from -4 to 4
- intensity: float32 [128, 256, 256], P('tile'), may hold values from 0.1 to 4
- corners: int32 [2, 128], replicated, may hold values from 0 to 3840, as said below
- owner: int32 [128], replicated, may hold values from 0 to 127, as said below
- w_in: bfloat16 [9, 48, 2], replicated, may hold values from -1.5 to 1.5
- b_in: float32 [48], replicated, may hold values from -3 to 3
- w_down: bfloat16 [4, 48, 48], replicated, may hold values from -0.4375 to 0.4375
- b_down: float32 [48], replicated, may hold values from -3 to 3
- w_mid: bfloat16 [9, 48, 48], replicated, may hold values from -0.3125 to 0.3125
- b_mid: float32 [48], replicated, may hold values from -3 to 3
- w_out: bfloat16 [9, 2, 48], replicated, may hold values from -0.3125 to 0.3125
- b_out: float32 [2], replicated, may hold values from -3 to 3
Outputs:
- obj_next: float32 [2, 4096, 512], P(None, 'tile', 'mode')
- aux_next: float32 [2, 4096, 512], P(None, 'tile', 'mode')
- dual_next: float32 [2, 4096, 512], P(None, 'tile', 'mode')
- misfit: float32 [128], P('tile')
The draws below stay inside these ranges and needn't reach their ends.
Inputs may be any that keep to these rules, and one draw needn't show every extreme that they name: Row corners lie in 0 to 3840 and column corners in 0 to 256; the upper ends are reached in every draw. Every index of tile owns between 1 and 1 positions and some owns exactly 1; of the positions of one owner at most 1 have patterns that touch one block of 32 object rows held by one index of tile, and in every draw some owner and block reach 1.
All inputs are finite; a program needn't handle non-finite values.
Results may differ from the reference program's by a relative error of at most 0.01.
Values may be sent and summed in bfloat16 or wider, within the bound.
No kernel may reach another device: no remote copies, remote signals or barrier semaphores. Data moves between devices by JAX's collectives and lax.ppermute only.
A program may use at most 128 MiB of HBM per device.

```python
import math
import jax
import jax.numpy as jnp
from jax import lax

PATCH = 256
CHANNELS = 48
TR = 32
POS_DEV = 1
MODES = 4
OBJ_H = 4096
OBJ_W = 512
NPOS = 128
OWN_MOST = 1
NB = 11
SLOTS = 128
N_TILE = 128


def scan_layout(key):
    base = jax.random.fold_in(key, 11)
    keys = jax.random.split(base, 7)
    order = jax.random.permutation(keys[0], N_TILE)
    extra = jax.random.randint(keys[1], (N_TILE // 2,), 0, POS_DEV)
    extra = extra.at[0].set(POS_DEV - 1)
    loads_pair = jnp.stack([POS_DEV + extra, POS_DEV - extra], axis=1).reshape(-1)
    loads = jnp.zeros((N_TILE,), jnp.int32).at[order].set(loads_pair.astype(jnp.int32))
    slot_ids = jnp.arange(N_TILE * OWN_MOST, dtype=jnp.int32)
    slot_dev = slot_ids // OWN_MOST
    slot_rank = slot_ids % OWN_MOST
    in_use = slot_rank < loads[slot_dev]
    scores = jax.random.permutation(keys[2], N_TILE * OWN_MOST).astype(jnp.int32)
    scores = jnp.where(in_use, scores, N_TILE * OWN_MOST + slot_ids)
    picked = jnp.argsort(scores, stable=True)[:NPOS]
    owners = slot_dev[picked]
    ranks = slot_rank[picked]
    spacing = PATCH + 2 * TR
    shift = jax.random.randint(keys[3], (N_TILE,), 0, NB)
    offset = jax.random.randint(keys[4], (N_TILE,), 0, spacing)
    jitter = jax.random.randint(keys[5], (NPOS,), 0, TR)
    band = (ranks * NB // OWN_MOST + shift[owners]) % NB
    rows = jnp.minimum(band * spacing + offset[owners] + jitter, OBJ_H - PATCH).astype(jnp.int32)
    lowest = jnp.argmax(rows)
    rows = rows.at[lowest].set(OBJ_H - PATCH)
    cols = jax.random.randint(keys[6], (NPOS,), 0, OBJ_W - PATCH + 1).astype(jnp.int32)
    cols = cols.at[0].set(OBJ_W - PATCH)
    return (jnp.stack([rows, cols]).astype(jnp.int32), owners.astype(jnp.int32))


def draw_corners(key, part):
    placed, owners = scan_layout(key)
    return placed


def draw_owner(key, part):
    placed, owners = scan_layout(key)
    return owners


def steps_of(key, dims, cuts, least, high):
    def one(axis_at, shards_of):
        steps = jax.random.uniform(jax.random.fold_in(jax.random.fold_in(key, 6), axis_at), (shards_of,), jnp.float32, least / len(cuts), high / len(cuts))
        return jnp.repeat(jnp.exp(steps), dims[axis_at] // shards_of).reshape((-1,) + (1,) * (len(dims) - axis_at - 1))

    loudness = one(*cuts[0])
    for cut in cuts[1:]:
        loudness = loudness * one(*cut)
    return loudness


def noise(key, extent, scale, most, cuts=(), kind=jnp.bfloat16):
    array = jax.random.normal(key, extent, jnp.float32) * scale
    if len(cuts) > 0:
        array = steps_of(key, extent, cuts, -0.22, 0.18) * array
    return jnp.clip(array, min=-most, max=most).astype(kind)


def setup_inputs(seed: int = 0) -> dict:
    splits = jax.random.split(jax.random.key(seed), 15)
    obj_x = noise(splits[0], (2, OBJ_H, OBJ_W), 1.0, 6.0, ((1, 128), (2, 4)), jnp.float32)
    dual_u = noise(splits[1], (2, OBJ_H, OBJ_W), 0.5, 6.0, ((1, 128), (2, 4)), jnp.float32)
    probes = noise(splits[2], (MODES, 2, PATCH, PATCH), 0.25, 4.0, ((0, 4),), jnp.float32)
    intensity = jnp.clip(jnp.exp(math.log(4.0) - 3.6888794 * jax.random.uniform(splits[3], (SLOTS, PATCH, PATCH), jnp.float32) ** steps_of(splits[3], (SLOTS, PATCH, PATCH), ((0, 128),), -0.2, 0.2)), 0.1, 4.0)
    corners = draw_corners(jax.random.fold_in(splits[14], 71), 0)
    owner = draw_owner(jax.random.fold_in(splits[14], 71), 0)
    w_in = noise(splits[6], (9, CHANNELS, 2), 18 ** -0.5, 1.5)
    b_in = noise(splits[7], (CHANNELS,), 0.5, 3.0, (), jnp.float32)
    w_down = noise(splits[8], (4, CHANNELS, CHANNELS), (4 * CHANNELS) ** -0.5, 0.4375)
    b_down = noise(splits[9], (CHANNELS,), 0.5, 3.0, (), jnp.float32)
    w_mid = noise(splits[10], (9, CHANNELS, CHANNELS), (9 * CHANNELS) ** -0.5, 0.3125)
    b_mid = noise(splits[11], (CHANNELS,), 0.5, 3.0, (), jnp.float32)
    w_out = noise(splits[12], (9, 2, CHANNELS), (9 * CHANNELS) ** -0.5, 0.3125)
    b_out = noise(splits[13], (2,), 0.5, 3.0, (), jnp.float32)
    return dict(obj_x=obj_x, dual_u=dual_u, probes=probes, intensity=intensity, corners=corners, owner=owner, w_in=w_in, b_in=b_in, w_down=w_down, b_down=b_down, w_mid=w_mid, b_mid=b_mid, w_out=w_out, b_out=b_out)


rho_weight = 2.0
floor_level = 0.25

def conv_same(act, weight):
    height = act.shape[1]
    width = act.shape[2]
    padded = jnp.pad(act.astype(jnp.float32), ((0, 0), (1, 1), (1, 1)))
    kernel = weight.astype(jnp.float32)
    total = jnp.zeros((kernel.shape[1], height, width), jnp.float32)
    for tap in range(9):
        shift_row = tap // 3
        shift_col = tap % 3
        window = padded[:, shift_row:shift_row + height, shift_col:shift_col + width]
        total = total + jnp.einsum('oc,chw->ohw', kernel[tap], window)
    return total

def through_low(values):
    lowered = values.astype(jnp.bfloat16)
    return lax.optimization_barrier(lowered).astype(jnp.float32)

def reference(obj_x, dual_u, probes, intensity, corners, owner, w_in, b_in, w_down, b_down, w_mid, b_mid, w_out, b_out):
    height_all = obj_x.shape[1]
    width_all = obj_x.shape[2]
    pos_count = owner.shape[0]
    chans = w_in.shape[1]
    indices = jnp.arange(pos_count, dtype=jnp.int32)
    earlier = (owner[:, None] == owner[None, :]) & (indices[None, :] < indices[:, None])
    slot_of = (owner * OWN_MOST + lax.optimization_barrier(jnp.sum(earlier.astype(jnp.int32), axis=1))).astype(jnp.int32)
    base = obj_x + dual_u
    base_low = base.astype(jnp.bfloat16)
    first_map = jax.nn.relu(conv_same(base_low, w_in) + b_in[:, None, None]).astype(jnp.bfloat16)
    pairs = first_map.astype(jnp.float32).reshape(chans, height_all // 2, 2, width_all // 2, 2)
    down_kernel = w_down.astype(jnp.float32).reshape(2, 2, chans, chans)
    second_map = jax.nn.relu(jnp.einsum('ijoc,chiwj->ohw', down_kernel, pairs) + b_down[:, None, None]).astype(jnp.bfloat16)
    third_map = jax.nn.relu(conv_same(second_map, w_mid) + b_mid[:, None, None]).astype(jnp.bfloat16)
    upsampled = jnp.repeat(jnp.repeat(third_map.astype(jnp.float32), 2, axis=1), 2, axis=2)
    fourth_map = (upsampled + first_map.astype(jnp.float32)).astype(jnp.bfloat16)
    aux_next = base - (conv_same(fourth_map, w_out) + b_out[:, None, None])
    obj_low = obj_x.astype(jnp.bfloat16)
    probe_re = probes[:, 0]
    probe_im = probes[:, 1]
    probe_power = lax.optimization_barrier(jnp.sum(probe_re * probe_re + probe_im * probe_im, axis=0))
    anchor = jnp.zeros((), jnp.int32)

    def one_position(index):
        row = corners[0, index]
        col = corners[1, index]
        patch = lax.dynamic_slice(obj_low, (anchor, row, col), (2, PATCH, PATCH)).astype(jnp.float32)
        wave = probe_re * patch[0] - probe_im * patch[1] + 1j * (probe_re * patch[1] + probe_im * patch[0])
        far = jnp.fft.fft2(wave, norm='ortho')
        power = lax.optimization_barrier(jnp.sum(far.real * far.real + far.imag * far.imag, axis=0))
        measured = jnp.sqrt(intensity[slot_of[index]])
        amp_error = jnp.mean((jnp.sqrt(power) - measured) ** 2)
        scale = measured / jnp.sqrt(jnp.maximum(power, floor_level))
        back = jnp.fft.ifft2(far * scale, norm='ortho')
        grad_re = lax.optimization_barrier(jnp.sum(through_low(probe_re * back.real + probe_im * back.imag), axis=0))
        grad_im = lax.optimization_barrier(jnp.sum(through_low(probe_re * back.imag - probe_im * back.real), axis=0))
        return (jnp.stack([grad_re, grad_im]), amp_error)
    grads, errors = lax.map(one_position, indices)

    def add_one(acc, index):
        row = corners[0, index]
        col = corners[1, index]
        update = jnp.concatenate([grads[index], probe_power[None]], axis=0)
        old = lax.dynamic_slice(acc, (anchor, row, col), (3, PATCH, PATCH))
        return (lax.dynamic_update_slice(acc, old + update, (anchor, row, col)), index)
    totals, unused = lax.scan(add_one, jnp.zeros((3, height_all, width_all), jnp.float32), indices)
    obj_next = (totals[:2] + rho_weight * (aux_next - dual_u)) / (totals[2] + rho_weight)
    dual_next = dual_u + obj_next - aux_next
    misfit = jnp.zeros((SLOTS,), jnp.float32).at[slot_of].set(errors)
    return (obj_next, aux_next, dual_next, misfit)
```

```python
import math

import jax
import jax.numpy as jnp
import numpy as np
from jax import lax
from jax.experimental import pallas as pl
from jax.experimental.pallas import tpu as pltpu
from jax.sharding import Mesh, PartitionSpec as P

HALO = 6
NX, NZ, NC, NM = 4, 16, 2, 4
PATCH = 256
ROWS = 32
COLS = 128
STRIPS = PATCH // ROWS + 1
HALF = (STRIPS + 1) // 2

rho_weight = 2.0
floor_level = 0.25
f32 = jnp.float32
bf16 = jnp.bfloat16
TILE_AXES = ("x", "z", "core")


def shifted(value, axes, step):
    count = math.prod(lax.axis_size(a) for a in axes)
    pairs = [(i, i + step) for i in range(count) if 0 <= i + step < count]
    return lax.ppermute(value, axes, pairs)


def extended_2(value, sides, width):
    for axes, dim in sides:
        length = value.shape[dim]
        last = lax.slice_in_dim(value, length - width, length, axis=dim)
        first = lax.slice_in_dim(value, 0, width, axis=dim)
        before = shifted(last, axes, 1)
        after = shifted(first, axes, -1)
        value = jnp.concatenate([before, value, after], axis=dim)
    return value

def vmem_spec():
    return pl.BlockSpec(memory_space=pltpu.VMEM)


def smem_spec():
    return pl.BlockSpec(memory_space=pltpu.SMEM)


def ids(meta):
    return meta[2, 0], meta[2, 1], meta[2, 2], meta[2, 3]


def first_strip(s0, core):
    return s0 + ((s0 + core) & 1)


def pack_kernel(meta, near, out):
    x, z, core, mode = ids(meta)
    for target in range(NX * NC):
        tx, tc = target // NC, target % NC
        tile = tx * (NZ * NC) + z * NC + tc
        begin = first_strip(meta[0, tile] // ROWS, core)
        for j in range(HALF):
            slot = ((begin + 2 * j) % (NZ * NC)) // NC
            out[target, j] = near[slot]


def window_kernel(meta, got, out, tall):
    x, z, core, mode = ids(meta)
    row = meta[0, x * (NZ * NC) + z * NC + core]
    s0 = row // ROWS
    for i in range(STRIPS):
        strip = s0 + i
        source = jnp.minimum(strip // (NZ * NC), NX - 1) * NC + (strip & 1)
        block = got[source, i // 2].astype(f32)
        tall[0, pl.ds(i * ROWS, ROWS)] = block[:ROWS]
        tall[1, pl.ds(i * ROWS, ROWS)] = block[ROWS:]
    offset = row - s0 * ROWS
    for plane in range(2):
        out[plane] = tall[plane, pl.ds(offset, PATCH)].astype(bf16)


def dot(a, b):
    return jnp.dot(a, b, preferred_element_type=f32)


def wave_kernel(meta, wins, probe0, probe1, probe2, probe3, intensity, table, out, err, far_all, tall):
    x, z, core, mode = ids(meta)
    mine = x * (NZ * NC) + z * NC + core
    row = meta[0, mine]
    col = meta[1, mine]
    s0 = row // ROWS
    offset = row - s0 * ROWS
    t_re = table[0]
    t_im = table[1]
    t_neg = -t_im
    left = jnp.concatenate(
        [jnp.concatenate([t_re, t_neg], axis=1), jnp.concatenate([t_im, t_re], axis=1)], axis=0
    )
    right = jnp.concatenate(
        [jnp.concatenate([t_re, t_im], axis=1), jnp.concatenate([t_neg, t_re], axis=1)], axis=0
    )
    full = jnp.concatenate(
        [jnp.concatenate([wins[m, p] for m in range(NM)], axis=1) for p in range(2)], axis=0
    )
    src = lax.broadcasted_iota(jnp.int32, (NM * COLS, PATCH), 0)
    dst = lax.broadcasted_iota(jnp.int32, (NM * COLS, PATCH), 1)
    take = jnp.where(src == dst + col, 1.0, 0.0).astype(bf16)
    patch = dot(full, take)
    obj_re = patch[:PATCH]
    obj_im = patch[PATCH:]
    probes = (probe0, probe1, probe2, probe3)
    power = jnp.zeros((PATCH, PATCH), f32)
    for m in range(NM):
        p_re = probes[m][0].astype(f32)
        p_im = probes[m][1].astype(f32)
        wave = jnp.concatenate(
            [(p_re * obj_re - p_im * obj_im).astype(bf16), (p_re * obj_im + p_im * obj_re).astype(bf16)],
            axis=0,
        )
        half = dot(left, wave).astype(bf16)
        far = dot(jnp.concatenate([half[:PATCH], half[PATCH:]], axis=1), right)
        far_all[m] = far
        power = power + far[:, :PATCH] * far[:, :PATCH] + far[:, PATCH:] * far[:, PATCH:]
    measured = jnp.sqrt(intensity[0])
    gap = jnp.sqrt(power) - measured
    err[...] = jnp.sum(gap * gap, keepdims=True) * (1.0 / (PATCH * PATCH))
    scale = measured / jnp.sqrt(jnp.maximum(power, floor_level))
    b_src = lax.broadcasted_iota(jnp.int32, (PATCH, COLS), 0)
    b_dst = lax.broadcasted_iota(jnp.int32, (PATCH, COLS), 1)
    keep = jnp.where(b_src == b_dst + (mode * COLS - col), 1.0, 0.0).astype(bf16)
    k_re = dot(t_re, keep).astype(bf16)
    k_im = dot(t_im, keep).astype(bf16)
    back_right = jnp.concatenate(
        [jnp.concatenate([k_re, -k_im], axis=1), jnp.concatenate([k_im, k_re], axis=1)], axis=0
    )
    sum_re = jnp.zeros((PATCH, COLS), f32)
    sum_im = jnp.zeros((PATCH, COLS), f32)
    for m in range(NM):
        far = far_all[m]
        scaled = jnp.concatenate(
            [(far[:, :PATCH] * scale).astype(bf16), (far[:, PATCH:] * scale).astype(bf16)], axis=1
        )
        half = dot(scaled, back_right).astype(bf16)
        back = dot(right, jnp.concatenate([half[:, :COLS], half[:, COLS:]], axis=0))
        back_re = back[:PATCH]
        back_im = back[PATCH:]
        q_re = dot(probes[m][0], keep)
        q_im = dot(probes[m][1], keep)
        sum_re = sum_re + (q_re * back_re + q_im * back_im)
        sum_im = sum_im + (q_re * back_im - q_im * back_re)
    tall[...] = jnp.zeros(tall.shape, f32)
    tall[0, pl.ds(offset, PATCH)] = sum_re
    tall[1, pl.ds(offset, PATCH)] = sum_im
    out[...] = jnp.zeros(out.shape, bf16)
    for i in range(STRIPS):
        strip = s0 + i
        target = jnp.minimum(strip // (NZ * NC), NX - 1) * NC + (strip & 1)
        piece = [tall[p, pl.ds(i * ROWS, ROWS)] for p in range(2)]
        out[target, i // 2] = jnp.concatenate(piece, axis=0).astype(bf16)


def gather_kernel(meta, got, out, acc):
    x, z, core, mode = ids(meta)
    acc[...] = jnp.zeros(acc.shape, f32)
    for source in range(NX * NC):
        sx, sc = source // NC, source % NC
        begin = first_strip(meta[0, sx * (NZ * NC) + z * NC + sc] // ROWS, core)
        for j in range(HALF):
            slot = ((begin + 2 * j) % (NZ * NC)) // NC
            acc[slot] = acc[slot] + got[source, j].astype(f32)
    out[...] = acc[...].astype(bf16)


def weight_kernel(meta, probe0, probe1, probe2, probe3, out, padded):
    x, z, core, mode = ids(meta)
    row0 = (x * (NZ * NC) + z * NC + core) * ROWS
    col0 = mode * COLS
    total = jnp.zeros((PATCH, PATCH), f32)
    for probe in (probe0, probe1, probe2, probe3):
        p_re = probe[0].astype(f32)
        p_im = probe[1].astype(f32)
        total = total + p_re * p_re + p_im * p_im
    padded[...] = jnp.zeros(padded.shape, f32)
    for half in range(PATCH // COLS):
        padded[1 + half, pl.ds(ROWS, PATCH)] = total[:, half * COLS : (half + 1) * COLS]
    out[...] = jnp.zeros(out.shape, f32)

    def add(k, carry):
        down = row0 - meta[0, k] + ROWS
        over = col0 - meta[1, k] + COLS
        hit = (down > 0) & (down < PATCH + ROWS) & (over > 0) & (over < PATCH + COLS)

        @pl.when(hit)
        def _():
            rows = jnp.concatenate([padded[q, pl.ds(down, ROWS)] for q in range(4)], axis=1)
            moved = pltpu.roll(rows, PATCH + 2 * COLS - over, 1)
            out[...] = out[...] + moved[:, :COLS]

        return carry

    lax.fori_loop(0, meta.shape[1], add, 0)


def dft_table():
    grid = np.arange(PATCH)[:, None] * np.arange(PATCH)[None, :] % PATCH
    angle = 2.0 * np.pi / PATCH * grid
    factor = 1.0 / math.sqrt(PATCH)
    table = np.stack([np.cos(angle) * factor, -np.sin(angle) * factor])
    return jnp.asarray(table.astype(np.float32)).astype(bf16)


CY, CX = (ROWS + 2 * HALO) // 2, (COLS + 2 * HALO) // 2
FLAT = CY * 128
CHUNK = 256
PHASES = ((0, 0), (0, 1), (1, 0), (1, 1))
SHIFTS = tuple((dy, dx) for dy in (-1, 0, 1) for dx in (-1, 0, 1))


def split_tables():
    first = np.zeros((9, 2, 4, 72), np.float32)
    last = np.zeros((9, 36, 4), np.float32)
    for tap in range(9):
        for ij, (i, j) in enumerate(PHASES):
            r, c = i + tap // 3 - 1, j + tap % 3 - 1
            p, q, dy, dx = r & 1, c & 1, r >> 1, c >> 1
            s = (dy + 1) * 3 + dx + 1
            for ch in range(2):
                first[tap, ch, ij, s * 8 + q * 4 + ch * 2 + p] = 1
            last[tap, s * 4 + ij, p * 2 + q] = 1
    return jnp.asarray(first).astype(bf16), jnp.asarray(last).astype(bf16)


def moved(value, dy, dx):
    if dx:
        value = pltpu.roll(value, (-dx) % FLAT, 1)
    if dy == 1:
        value = jnp.concatenate([value[:, 128:], value[:, :128]], axis=1)
    if dy == -1:
        value = jnp.concatenate([value[:, FLAT - 128 :], value[:, : FLAT - 128]], axis=1)
    return value


def denoise_kernel(
    meta,
    b_out,
    ext,
    first_w,
    first_b,
    down_w,
    down_b,
    mid_w,
    mid_b,
    last_w,
    out,
    halves,
    planes,
    taps1,
    maps,
    coarse,
    taps2,
    fourth,
    parts,
    inter,
):
    x, z, core, mode = ids(meta)
    chans = coarse.shape[0]
    height = ROWS + 2 * HALO
    width = COLS + 2 * HALO
    src = lax.broadcasted_iota(jnp.int32, (width, 256), 0)
    dst = lax.broadcasted_iota(jnp.int32, (width, 256), 1)
    lane = dst & 127
    even_odd = jnp.where((src == 2 * lane + (dst >> 7)) & (lane < CX), 1.0, 0.0).astype(bf16)
    for ch in range(2):
        row = dot(ext[ch], even_odd)
        for q in range(2):
            halves[q, pl.ds(ch * height, height)] = row[:, q * 128 : (q + 1) * 128]
    for y in range(CY):
        pieces = [
            halves[q, pl.ds(ch * height + 2 * y, 2)] for q in range(2) for ch in range(2)
        ]
        planes[:, pl.ds(y * 128, 128)] = jnp.concatenate(pieces, axis=0)
    full = planes[...]
    taps1[...] = jnp.concatenate([moved(full, dy, dx) for dy, dx in SHIFTS], axis=0).astype(bf16)

    row0 = (x * (NZ * NC) + z * NC + core) * ROWS - HALO
    col0 = mode * COLS - HALO
    height_all, width_all = NX * NZ * NC * ROWS, NM * COLS

    def masks(start):
        spot = lax.broadcasted_iota(jnp.int32, (1, CHUNK), 1) + start
        rows = row0 + 2 * (spot >> 7)
        cols = col0 + 2 * (spot & 127)
        found = []
        for p, q in PHASES:
            inside = (rows + p >= 0) & (rows + p < height_all)
            inside = inside & (cols + q >= 0) & (cols + q < width_all)
            found.append(jnp.where(inside, 1.0, 0.0))
        return found

    for start in range(0, FLAT, CHUNK):
        span = pl.ds(start, CHUNK)
        found = masks(start)
        value = dot(first_w[...], taps1[:, span])
        for n in range(4):
            part = value[n * chans : (n + 1) * chans] + first_b[...]
            maps[pl.ds(n * chans, chans), span] = (jnp.maximum(part, 0.0) * found[n]).astype(bf16)
        value = dot(down_w[...], maps[:, span]) + down_b[...]
        coarse[:, span] = (jnp.maximum(value, 0.0) * found[0]).astype(bf16).astype(f32)
    for s, (dy, dx) in enumerate(SHIFTS):
        taps2[pl.ds(s * chans, chans)] = moved(coarse[...], dy, dx).astype(bf16)
    for start in range(0, FLAT, CHUNK):
        span = pl.ds(start, CHUNK)
        found = masks(start)
        value = dot(mid_w[...], taps2[:, span]) + mid_b[...]
        third = jnp.maximum(value, 0.0).astype(bf16).astype(f32)
        for n in range(4):
            rows = pl.ds(n * chans, chans)
            fourth[rows, span] = (third * found[n] + maps[rows, span].astype(f32)).astype(bf16)
        parts[:, span] = dot(last_w[...], fourth[:, span])
    total = moved(parts[pl.ds(0, 8)], *SHIFTS[0])
    for s in range(1, 9):
        total = total + moved(parts[pl.ds(s * 8, 8)], *SHIFTS[s])
    planes[...] = total
    for y in range(HALO // 2, HALO // 2 + ROWS // 2):
        tile = planes[:, pl.ds(y * 128, 128)]
        for i, j in PHASES:
            for ch in range(2):
                n = (i * 2 + j) * 2 + ch
                inter[j, pl.ds(ch * ROWS + 2 * y - HALO + i, 1)] = tile[n : n + 1]
    e_src = lax.broadcasted_iota(jnp.int32, (256, COLS), 0)
    e_dst = lax.broadcasted_iota(jnp.int32, (256, COLS), 1)
    weave = jnp.where(2 * (e_src & 127) - HALO + (e_src >> 7) == e_dst, 1.0, 0.0).astype(bf16)
    wide = jnp.concatenate([inter[0], inter[1]], axis=1)
    high = wide.astype(bf16)
    low = (wide - high.astype(f32)).astype(bf16)
    woven = dot(high, weave) + dot(low, weave)
    for ch in range(2):
        out[ch] = woven[ch * ROWS : (ch + 1) * ROWS] + b_out[ch]


def denoise(base, meta, w_in, b_in, w_down, b_down, w_mid, b_mid, w_out, b_out):
    chans = w_in.shape[1]
    extended = extended_2(base.astype(bf16), ((TILE_AXES, 1), (("mode",), 2)), HALO)
    first, last = split_tables()
    first_w = jnp.einsum("toc,tcik->iok", w_in, first).reshape(4 * chans, 72)
    last_w = jnp.einsum("tcd,tmp->mcpd", w_out, last).reshape(72, 4 * chans)
    down_w = jnp.transpose(w_down, (1, 0, 2)).reshape(chans, 4 * chans)
    mid_w = jnp.transpose(w_mid, (1, 0, 2)).reshape(chans, 9 * chans)
    return pl.pallas_call(
        denoise_kernel,
        out_shape=jax.ShapeDtypeStruct((2, ROWS, COLS), f32),
        in_specs=[smem_spec(), smem_spec()] + [vmem_spec()] * 8,
        out_specs=vmem_spec(),
        scratch_shapes=[
            pltpu.VMEM((2, 2 * (ROWS + 2 * HALO), 128), f32),
            pltpu.VMEM((8, FLAT), f32),
            pltpu.VMEM((72, FLAT), bf16),
            pltpu.VMEM((4 * chans, FLAT), bf16),
            pltpu.VMEM((chans, FLAT), f32),
            pltpu.VMEM((9 * chans, FLAT), bf16),
            pltpu.VMEM((4 * chans, FLAT), bf16),
            pltpu.VMEM((72, FLAT), f32),
            pltpu.VMEM((2, 2 * ROWS, 128), f32),
        ],
        cost_estimate=pl.CostEstimate(
            flops=4 * 10**9, bytes_accessed=2 * 10**7, transcendentals=0
        ),
        name="denoise",
    )(
        meta,
        b_out,
        extended,
        first_w,
        b_in.reshape(chans, 1),
        down_w,
        b_down.reshape(chans, 1),
        mid_w,
        b_mid.reshape(chans, 1),
        last_w,
    )


def per_device(
    obj_x,
    dual_u,
    probes,
    intensity,
    corners,
    owner,
    w_in,
    b_in,
    w_down,
    b_down,
    w_mid,
    b_mid,
    w_out,
    b_out,
):
    x = lax.axis_index("x")
    z = lax.axis_index("z")
    core = lax.axis_index("core")
    mode = lax.axis_index("mode")
    tiles = NX * NZ * NC
    lanes = jnp.arange(tiles, dtype=jnp.int32)
    owned = owner[None, :] == lanes[:, None]
    by_owner = jnp.sum(jnp.where(owned[None], corners[:, None, :], 0), axis=2)
    place = jnp.where(lanes == 0, x, jnp.where(lanes == 1, z, jnp.where(lanes == 2, core, mode)))
    meta = jnp.concatenate([by_owner, place[None]], axis=0).astype(jnp.int32)

    low = obj_x.astype(bf16).reshape(1, 2 * ROWS, COLS)
    near = lax.all_to_all(jnp.broadcast_to(low, (NZ, 2 * ROWS, COLS)), "z", 0, 0, tiled=True)
    probe0 = probes[0].astype(bf16)
    others = [
        lax.ppermute(probe0, "mode", [(i, (i + k) % NM) for i in range(NM)]) for k in range(1, NM)
    ]
    all_probes = (probe0, *others)
    packed = pl.pallas_call(
        pack_kernel,
        out_shape=jax.ShapeDtypeStruct((NX * NC, HALF, 2 * ROWS, COLS), bf16),
        in_specs=[smem_spec(), vmem_spec()],
        out_specs=vmem_spec(),
        name="pack",
    )(meta, near)
    got = lax.all_to_all(packed, ("x", "core"), 0, 0, tiled=True)
    window = pl.pallas_call(
        window_kernel,
        out_shape=jax.ShapeDtypeStruct((2, PATCH, COLS), bf16),
        in_specs=[smem_spec(), vmem_spec()],
        out_specs=vmem_spec(),
        scratch_shapes=[pltpu.VMEM((2, STRIPS * ROWS, COLS), f32)],
        name="window",
    )(meta, got)
    wins = lax.all_gather(window, "mode", axis=0)
    updates, misfit = pl.pallas_call(
        wave_kernel,
        out_shape=(
            jax.ShapeDtypeStruct((NX * NC, HALF, 2 * ROWS, COLS), bf16),
            jax.ShapeDtypeStruct((1, 1), f32),
        ),
        in_specs=[smem_spec()] + [vmem_spec()] * 7,
        out_specs=(vmem_spec(), vmem_spec()),
        scratch_shapes=[
            pltpu.VMEM((NM, PATCH, 2 * PATCH), f32),
            pltpu.VMEM((2, STRIPS * ROWS, COLS), f32),
        ],
        name="wave",
    )(meta, wins, *all_probes, intensity, dft_table())
    back = lax.all_to_all(updates, ("x", "core"), 0, 0, tiled=True)
    partial = pl.pallas_call(
        gather_kernel,
        out_shape=jax.ShapeDtypeStruct((NZ, 2 * ROWS, COLS), bf16),
        in_specs=[smem_spec(), vmem_spec()],
        out_specs=vmem_spec(),
        scratch_shapes=[pltpu.VMEM((NZ, 2 * ROWS, COLS), f32)],
        name="gather",
    )(meta, back)
    pieces = lax.all_to_all(partial, "z", 0, 0, tiled=True)
    denom = pl.pallas_call(
        weight_kernel,
        out_shape=jax.ShapeDtypeStruct((ROWS, COLS), f32),
        in_specs=[smem_spec()] + [vmem_spec()] * NM,
        out_specs=vmem_spec(),
        scratch_shapes=[pltpu.VMEM((PATCH // COLS + 2, PATCH + 2 * ROWS, COLS), f32)],
        name="weight",
    )(meta, *all_probes)
    base = obj_x + dual_u
    center = denoise(base, meta, w_in, b_in, w_down, b_down, w_mid, b_mid, w_out, b_out)
    aux_next = base - center
    numer = jnp.sum(pieces.astype(f32), axis=0).reshape(2, ROWS, COLS)
    obj_next = (numer + rho_weight * (aux_next - dual_u)) / (denom + rho_weight)
    dual_next = dual_u + obj_next - aux_next
    return (obj_next, aux_next, dual_next, misfit.reshape(1))


def solution(mesh):
    split = Mesh(mesh.devices.reshape(NX, NZ, NC, NM), TILE_AXES + ("mode",))
    grid = P(None, TILE_AXES, "mode")
    return jax.shard_map(
        per_device,
        mesh=split,
        in_specs=(
            grid,
            grid,
            P("mode", None, None, None),
            P(TILE_AXES, None, None),
        )
        + (P(),) * 10,
        out_specs=(grid, grid, grid, P(TILE_AXES)),
        check_vma=False,
    )
```

```python
import math

import jax
import jax.numpy as jnp
import numpy as np
from jax import lax
from jax.experimental import pallas as pl
from jax.experimental.pallas import tpu as pltpu
from jax.sharding import Mesh, PartitionSpec as P

HALO = 6
NX, NZ, NC, NM = 4, 16, 2, 4
PATCH = 256
ROWS = 32
COLS = 128
STRIPS = PATCH // ROWS + 1
HALF = (STRIPS + 1) // 2

rho_weight = 2.0
floor_level = 0.25
f32 = jnp.float32
bf16 = jnp.bfloat16
TILE_AXES = ("x", "z", "core")


def shifted(value, axes, step):
    count = math.prod(lax.axis_size(a) for a in axes)
    pairs = [(i, i + step) for i in range(count) if 0 <= i + step < count]
    return lax.ppermute(value, axes, pairs)


def extended_2(value, sides, width):
    for axes, dim in sides:
        length = value.shape[dim]
        last = lax.slice_in_dim(value, length - width, length, axis=dim)
        first = lax.slice_in_dim(value, 0, width, axis=dim)
        before = shifted(last, axes, 1)
        after = shifted(first, axes, -1)
        value = jnp.concatenate([before, value, after], axis=dim)
    return value


def vmem_spec():
    return pl.BlockSpec(memory_space=pltpu.VMEM)


def smem_spec():
    return pl.BlockSpec(memory_space=pltpu.SMEM)


def ids(meta):
    return meta[2, 0], meta[2, 1], meta[2, 2], meta[2, 3]


def first_strip(s0, core):
    return s0 + ((s0 + core) & 1)


def pack_kernel(meta, near, out):
    _, z, core, _ = ids(meta)
    for target in range(NX * NC):
        tx, tc = target // NC, target % NC
        tile = tx * (NZ * NC) + z * NC + tc
        begin = first_strip(meta[0, tile] // ROWS, core)
        for j in range(HALF):
            slot = ((begin + 2 * j) % (NZ * NC)) // NC
            out[target, j] = near[slot]


def window_kernel(meta, got, out, tall):
    x, z, core, _ = ids(meta)
    row = meta[0, x * (NZ * NC) + z * NC + core]
    s0 = row // ROWS
    for i in range(STRIPS):
        strip = s0 + i
        source = jnp.minimum(strip // (NZ * NC), NX - 1) * NC + (strip & 1)
        block = got[source, i // 2].astype(f32)
        tall[0, pl.ds(i * ROWS, ROWS)] = block[:ROWS]
        tall[1, pl.ds(i * ROWS, ROWS)] = block[ROWS:]
    offset = row - s0 * ROWS
    for plane in range(2):
        out[plane] = tall[plane, pl.ds(offset, PATCH)].astype(bf16)


def dot(a, b):
    return jnp.dot(a, b, preferred_element_type=f32)


def wave_kernel(meta, wins, probe0, probe1, probe2, probe3, intensity, table, out, err, far_all, tall):
    x, z, core, mode = ids(meta)
    mine = x * (NZ * NC) + z * NC + core
    row = meta[0, mine]
    col = meta[1, mine]
    s0 = row // ROWS
    offset = row - s0 * ROWS
    t_re = table[0]
    t_im = table[1]
    t_neg = -t_im
    left = jnp.concatenate(
        [jnp.concatenate([t_re, t_neg], axis=1), jnp.concatenate([t_im, t_re], axis=1)], axis=0
    )
    right = jnp.concatenate(
        [jnp.concatenate([t_re, t_im], axis=1), jnp.concatenate([t_neg, t_re], axis=1)], axis=0
    )
    full = jnp.concatenate(
        [jnp.concatenate([wins[m, p] for m in range(NM)], axis=1) for p in range(2)], axis=0
    )
    src = lax.broadcasted_iota(jnp.int32, (NM * COLS, PATCH), 0)
    dst = lax.broadcasted_iota(jnp.int32, (NM * COLS, PATCH), 1)
    take = jnp.where(src == dst + col, 1.0, 0.0).astype(bf16)
    patch = dot(full, take)
    obj_re = patch[:PATCH]
    obj_im = patch[PATCH:]
    probes = (probe0, probe1, probe2, probe3)
    power = jnp.zeros((PATCH, PATCH), f32)
    for m in range(NM):
        p_re = probes[m][0].astype(f32)
        p_im = probes[m][1].astype(f32)
        wave = jnp.concatenate(
            [(p_re * obj_re - p_im * obj_im).astype(bf16), (p_re * obj_im + p_im * obj_re).astype(bf16)],
            axis=0,
        )
        half = dot(left, wave).astype(bf16)
        far = dot(jnp.concatenate([half[:PATCH], half[PATCH:]], axis=1), right)
        far_all[m] = far
        power = power + far[:, :PATCH] * far[:, :PATCH] + far[:, PATCH:] * far[:, PATCH:]
    measured = jnp.sqrt(intensity[0])
    gap = jnp.sqrt(power) - measured
    err[...] = jnp.sum(gap * gap, keepdims=True) * (1.0 / (PATCH * PATCH))
    scale = measured / jnp.sqrt(jnp.maximum(power, floor_level))
    b_src = lax.broadcasted_iota(jnp.int32, (PATCH, COLS), 0)
    b_dst = lax.broadcasted_iota(jnp.int32, (PATCH, COLS), 1)
    keep = jnp.where(b_src == b_dst + (mode * COLS - col), 1.0, 0.0).astype(bf16)
    k_re = dot(t_re, keep).astype(bf16)
    k_im = dot(t_im, keep).astype(bf16)
    back_right = jnp.concatenate(
        [jnp.concatenate([k_re, -k_im], axis=1), jnp.concatenate([k_im, k_re], axis=1)], axis=0
    )
    sum_re = jnp.zeros((PATCH, COLS), f32)
    sum_im = jnp.zeros((PATCH, COLS), f32)
    for m in range(NM):
        far = far_all[m]
        scaled = jnp.concatenate(
            [(far[:, :PATCH] * scale).astype(bf16), (far[:, PATCH:] * scale).astype(bf16)], axis=1
        )
        half = dot(scaled, back_right).astype(bf16)
        back = dot(right, jnp.concatenate([half[:, :COLS], half[:, COLS:]], axis=0))
        back_re = back[:PATCH]
        back_im = back[PATCH:]
        q_re = dot(probes[m][0], keep)
        q_im = dot(probes[m][1], keep)
        sum_re = sum_re + (q_re * back_re + q_im * back_im)
        sum_im = sum_im + (q_re * back_im - q_im * back_re)
    tall[...] = jnp.zeros(tall.shape, f32)
    tall[0, pl.ds(offset, PATCH)] = sum_re
    tall[1, pl.ds(offset, PATCH)] = sum_im
    out[...] = jnp.zeros(out.shape, bf16)
    for i in range(STRIPS):
        strip = s0 + i
        target = jnp.minimum(strip // (NZ * NC), NX - 1) * NC + (strip & 1)
        piece = [tall[p, pl.ds(i * ROWS, ROWS)] for p in range(2)]
        out[target, i // 2] = jnp.concatenate(piece, axis=0).astype(bf16)


def gather_kernel(meta, got, out, acc):
    _, z, core, _ = ids(meta)
    acc[...] = jnp.zeros(acc.shape, f32)
    for source in range(NX * NC):
        sx, sc = source // NC, source % NC
        begin = first_strip(meta[0, sx * (NZ * NC) + z * NC + sc] // ROWS, core)
        for j in range(HALF):
            slot = ((begin + 2 * j) % (NZ * NC)) // NC
            acc[slot] = acc[slot] + got[source, j].astype(f32)
    out[...] = acc[...].astype(bf16)


def weight_kernel(meta, probe0, probe1, probe2, probe3, out, padded):
    x, z, core, mode = ids(meta)
    row0 = (x * (NZ * NC) + z * NC + core) * ROWS
    col0 = mode * COLS
    total = jnp.zeros((PATCH, PATCH), f32)
    for probe in (probe0, probe1, probe2, probe3):
        p_re = probe[0].astype(f32)
        p_im = probe[1].astype(f32)
        total = total + p_re * p_re + p_im * p_im
    padded[...] = jnp.zeros(padded.shape, f32)
    for half in range(PATCH // COLS):
        padded[1 + half, pl.ds(ROWS, PATCH)] = total[:, half * COLS : (half + 1) * COLS]
    out[...] = jnp.zeros(out.shape, f32)

    def add(k, carry):
        down = row0 - meta[0, k] + ROWS
        over = col0 - meta[1, k] + COLS
        hit = (down > 0) & (down < PATCH + ROWS) & (over > 0) & (over < PATCH + COLS)

        @pl.when(hit)
        def _():
            rows = jnp.concatenate([padded[q, pl.ds(down, ROWS)] for q in range(4)], axis=1)
            moved = pltpu.roll(rows, PATCH + 2 * COLS - over, 1)
            out[...] = out[...] + moved[:, :COLS]

        return carry

    lax.fori_loop(0, meta.shape[1], add, 0)


def dft_table():
    grid = np.arange(PATCH)[:, None] * np.arange(PATCH)[None, :] % PATCH
    angle = 2.0 * np.pi / PATCH * grid
    factor = 1.0 / math.sqrt(PATCH)
    table = np.stack([np.cos(angle) * factor, -np.sin(angle) * factor])
    return jnp.asarray(table.astype(np.float32)).astype(bf16)


CY, CX = (ROWS + 2 * HALO) // 2, (COLS + 2 * HALO) // 2
FLAT = CY * 128
CHUNK = 256
PHASES = ((0, 0), (0, 1), (1, 0), (1, 1))
SHIFTS = tuple((dy, dx) for dy in (-1, 0, 1) for dx in (-1, 0, 1))


def split_tables():
    first = np.zeros((9, 2, 4, 72), np.float32)
    last = np.zeros((9, 36, 4), np.float32)
    for tap in range(9):
        for ij, (i, j) in enumerate(PHASES):
            r, c = i + tap // 3 - 1, j + tap % 3 - 1
            p, q, dy, dx = r & 1, c & 1, r >> 1, c >> 1
            s = (dy + 1) * 3 + dx + 1
            for ch in range(2):
                first[tap, ch, ij, s * 8 + q * 4 + ch * 2 + p] = 1
            last[tap, s * 4 + ij, p * 2 + q] = 1
    return jnp.asarray(first).astype(bf16), jnp.asarray(last).astype(bf16)


def moved(value, dy, dx):
    if dx:
        value = pltpu.roll(value, (-dx) % FLAT, 1)
    if dy == 1:
        value = jnp.concatenate([value[:, 128:], value[:, :128]], axis=1)
    if dy == -1:
        value = jnp.concatenate([value[:, FLAT - 128 :], value[:, : FLAT - 128]], axis=1)
    return value


def denoise_kernel(
    meta,
    b_out,
    ext,
    first_w,
    first_b,
    down_w,
    down_b,
    mid_w,
    mid_b,
    last_w,
    out,
    halves,
    planes,
    taps1,
    maps,
    coarse,
    taps2,
    fourth,
    parts,
    inter,
):
    x, z, core, mode = ids(meta)
    chans = coarse.shape[0]
    height = ROWS + 2 * HALO
    width = COLS + 2 * HALO
    src = lax.broadcasted_iota(jnp.int32, (width, 256), 0)
    dst = lax.broadcasted_iota(jnp.int32, (width, 256), 1)
    lane = dst & 127
    even_odd = jnp.where((src == 2 * lane + (dst >> 7)) & (lane < CX), 1.0, 0.0).astype(bf16)
    for ch in range(2):
        row = dot(ext[ch], even_odd)
        for q in range(2):
            halves[q, pl.ds(ch * height, height)] = row[:, q * 128 : (q + 1) * 128]
    for y in range(CY):
        pieces = [
            halves[q, pl.ds(ch * height + 2 * y, 2)] for q in range(2) for ch in range(2)
        ]
        planes[:, pl.ds(y * 128, 128)] = jnp.concatenate(pieces, axis=0)
    full = planes[...]
    taps1[...] = jnp.concatenate([moved(full, dy, dx) for dy, dx in SHIFTS], axis=0).astype(bf16)

    row0 = (x * (NZ * NC) + z * NC + core) * ROWS - HALO
    col0 = mode * COLS - HALO
    height_all, width_all = NX * NZ * NC * ROWS, NM * COLS

    def masks(start):
        spot = lax.broadcasted_iota(jnp.int32, (1, CHUNK), 1) + start
        rows = row0 + 2 * (spot >> 7)
        cols = col0 + 2 * (spot & 127)
        found = []
        for p, q in PHASES:
            inside = (rows + p >= 0) & (rows + p < height_all)
            inside = inside & (cols + q >= 0) & (cols + q < width_all)
            found.append(jnp.where(inside, 1.0, 0.0))
        return found

    for start in range(0, FLAT, CHUNK):
        span = pl.ds(start, CHUNK)
        found = masks(start)
        value = dot(first_w[...], taps1[:, span])
        for n in range(4):
            part = value[n * chans : (n + 1) * chans] + first_b[...]
            maps[pl.ds(n * chans, chans), span] = (jnp.maximum(part, 0.0) * found[n]).astype(bf16)
        value = dot(down_w[...], maps[:, span]) + down_b[...]
        coarse[:, span] = (jnp.maximum(value, 0.0) * found[0]).astype(bf16).astype(f32)
    for s, (dy, dx) in enumerate(SHIFTS):
        taps2[pl.ds(s * chans, chans)] = moved(coarse[...], dy, dx).astype(bf16)
    for start in range(0, FLAT, CHUNK):
        span = pl.ds(start, CHUNK)
        found = masks(start)
        value = dot(mid_w[...], taps2[:, span]) + mid_b[...]
        third = jnp.maximum(value, 0.0).astype(bf16).astype(f32)
        for n in range(4):
            rows = pl.ds(n * chans, chans)
            fourth[rows, span] = (third * found[n] + maps[rows, span].astype(f32)).astype(bf16)
        parts[:, span] = dot(last_w[...], fourth[:, span])
    total = moved(parts[pl.ds(0, 8)], *SHIFTS[0])
    for s in range(1, 9):
        total = total + moved(parts[pl.ds(s * 8, 8)], *SHIFTS[s])
    planes[...] = total
    for y in range(HALO // 2, HALO // 2 + ROWS // 2):
        tile = planes[:, pl.ds(y * 128, 128)]
        for i, j in PHASES:
            for ch in range(2):
                n = (i * 2 + j) * 2 + ch
                inter[j, pl.ds(ch * ROWS + 2 * y - HALO + i, 1)] = tile[n : n + 1]
    e_src = lax.broadcasted_iota(jnp.int32, (256, COLS), 0)
    e_dst = lax.broadcasted_iota(jnp.int32, (256, COLS), 1)
    weave = jnp.where(2 * (e_src & 127) - HALO + (e_src >> 7) == e_dst, 1.0, 0.0).astype(bf16)
    wide = jnp.concatenate([inter[0], inter[1]], axis=1)
    high = wide.astype(bf16)
    low = (wide - high.astype(f32)).astype(bf16)
    woven = dot(high, weave) + dot(low, weave)
    for ch in range(2):
        out[ch] = woven[ch * ROWS : (ch + 1) * ROWS] + b_out[ch]


def denoise(base, meta, w_in, b_in, w_down, b_down, w_mid, b_mid, w_out, b_out):
    chans = w_in.shape[1]
    extended = extended_2(base.astype(bf16), ((TILE_AXES, 1), (("mode",), 2)), HALO)
    first, last = split_tables()
    first_w = jnp.einsum("toc,tcik->iok", w_in, first).reshape(4 * chans, 72)
    last_w = jnp.einsum("tcd,tmp->mcpd", w_out, last).reshape(72, 4 * chans)
    down_w = jnp.transpose(w_down, (1, 0, 2)).reshape(chans, 4 * chans)
    mid_w = jnp.transpose(w_mid, (1, 0, 2)).reshape(chans, 9 * chans)
    return pl.pallas_call(
        denoise_kernel,
        out_shape=jax.ShapeDtypeStruct((2, ROWS, COLS), f32),
        in_specs=[smem_spec(), smem_spec()] + [vmem_spec()] * 8,
        out_specs=vmem_spec(),
        scratch_shapes=[
            pltpu.VMEM((2, 2 * (ROWS + 2 * HALO), 128), f32),
            pltpu.VMEM((8, FLAT), f32),
            pltpu.VMEM((72, FLAT), bf16),
            pltpu.VMEM((4 * chans, FLAT), bf16),
            pltpu.VMEM((chans, FLAT), f32),
            pltpu.VMEM((9 * chans, FLAT), bf16),
            pltpu.VMEM((4 * chans, FLAT), bf16),
            pltpu.VMEM((72, FLAT), f32),
            pltpu.VMEM((2, 2 * ROWS, 128), f32),
        ],
        cost_estimate=pl.CostEstimate(
            flops=4 * 10**9, bytes_accessed=2 * 10**7, transcendentals=0
        ),
        name="denoise",
    )(
        meta,
        b_out,
        extended,
        first_w,
        b_in.reshape(chans, 1),
        down_w,
        b_down.reshape(chans, 1),
        mid_w,
        b_mid.reshape(chans, 1),
        last_w,
    )


def per_device(
    obj_x,
    dual_u,
    probes,
    intensity,
    corners,
    owner,
    w_in,
    b_in,
    w_down,
    b_down,
    w_mid,
    b_mid,
    w_out,
    b_out,
):
    x = lax.axis_index("x")
    z = lax.axis_index("z")
    core = lax.axis_index("core")
    mode = lax.axis_index("mode")
    tiles = NX * NZ * NC
    lanes = jnp.arange(tiles, dtype=jnp.int32)
    owned = owner[None, :] == lanes[:, None]
    by_owner = jnp.sum(jnp.where(owned[None], corners[:, None, :], 0), axis=2)
    place = jnp.where(lanes == 0, x, jnp.where(lanes == 1, z, jnp.where(lanes == 2, core, mode)))
    meta = jnp.concatenate([by_owner, place[None]], axis=0).astype(jnp.int32)

    low = obj_x.astype(bf16).reshape(1, 2 * ROWS, COLS)
    near = lax.all_to_all(jnp.broadcast_to(low, (NZ, 2 * ROWS, COLS)), "z", 0, 0, tiled=True)
    probe0 = probes[0].astype(bf16)
    others = [
        lax.ppermute(probe0, "mode", [(i, (i + k) % NM) for i in range(NM)])
        for k in range(1, NM)
    ]
    all_probes = (probe0, *others)
    packed = pl.pallas_call(
        pack_kernel,
        out_shape=jax.ShapeDtypeStruct((NX * NC, HALF, 2 * ROWS, COLS), bf16),
        in_specs=[smem_spec(), vmem_spec()],
        out_specs=vmem_spec(),
        name="pack",
    )(meta, near)
    got = lax.all_to_all(packed, ("x", "core"), 0, 0, tiled=True)
    window = pl.pallas_call(
        window_kernel,
        out_shape=jax.ShapeDtypeStruct((2, PATCH, COLS), bf16),
        in_specs=[smem_spec(), vmem_spec()],
        out_specs=vmem_spec(),
        scratch_shapes=[pltpu.VMEM((2, STRIPS * ROWS, COLS), f32)],
        name="window",
    )(meta, got)
    wins = lax.all_to_all(jnp.broadcast_to(window, (NM, *window.shape)), "mode", 0, 0, tiled=True)
    updates, misfit = pl.pallas_call(
        wave_kernel,
        out_shape=(
            jax.ShapeDtypeStruct((NX * NC, HALF, 2 * ROWS, COLS), bf16),
            jax.ShapeDtypeStruct((1, 1), f32),
        ),
        in_specs=[smem_spec()] + [vmem_spec()] * 7,
        out_specs=(vmem_spec(), vmem_spec()),
        scratch_shapes=[
            pltpu.VMEM((NM, PATCH, 2 * PATCH), f32),
            pltpu.VMEM((2, STRIPS * ROWS, COLS), f32),
        ],
        name="wave",
    )(meta, wins, *all_probes, intensity, dft_table())
    back = lax.all_to_all(updates, ("x", "core"), 0, 0, tiled=True)
    partial = pl.pallas_call(
        gather_kernel,
        out_shape=jax.ShapeDtypeStruct((NZ, 2 * ROWS, COLS), bf16),
        in_specs=[smem_spec(), vmem_spec()],
        out_specs=vmem_spec(),
        scratch_shapes=[pltpu.VMEM((NZ, 2 * ROWS, COLS), f32)],
        name="gather",
    )(meta, back)
    pieces = lax.all_to_all(partial, "z", 0, 0, tiled=True)
    denom = pl.pallas_call(
        weight_kernel,
        out_shape=jax.ShapeDtypeStruct((ROWS, COLS), f32),
        in_specs=[smem_spec()] + [vmem_spec()] * NM,
        out_specs=vmem_spec(),
        scratch_shapes=[pltpu.VMEM((PATCH // COLS + 2, PATCH + 2 * ROWS, COLS), f32)],
        name="weight",
    )(meta, *all_probes)
    base = obj_x + dual_u
    center = denoise(base, meta, w_in, b_in, w_down, b_down, w_mid, b_mid, w_out, b_out)
    aux_next = base - center
    numer = jnp.sum(pieces.astype(f32), axis=0).reshape(2, ROWS, COLS)
    obj_next = (numer + rho_weight * (aux_next - dual_u)) / (denom + rho_weight)
    dual_next = dual_u + obj_next - aux_next
    return (obj_next, aux_next, dual_next, misfit.reshape(1))


def solution(mesh):
    split = Mesh(mesh.devices.reshape(NX, NZ, NC, NM), TILE_AXES + ("mode",))
    grid = P(None, TILE_AXES, "mode")
    return jax.shard_map(
        per_device,
        mesh=split,
        in_specs=(
            grid,
            grid,
            P("mode", None, None, None),
            P(TILE_AXES, None, None),
        )
        + (P(),) * 10,
        out_specs=(grid, grid, grid, P(TILE_AXES)),
        check_vma=False,
    )
```

```python
import math

import jax
import jax.numpy as jnp
import numpy as np
from jax import lax
from jax.experimental import pallas as pl
from jax.experimental.pallas import tpu as pltpu
from jax.sharding import Mesh, PartitionSpec as P

HALO = 6
NX, NZ, NC, NM = 4, 16, 2, 4
PATCH = 256
ROWS = 32
COLS = 128
STRIPS = PATCH // ROWS + 1
HALF = (STRIPS + 1) // 2

rho_weight = 2.0
floor_level = 0.25
f32 = jnp.float32
bf16 = jnp.bfloat16
TILE_AXES = ("x", "z", "core")


def shifted(value, axes, step):
    count = math.prod(lax.axis_size(a) for a in axes)
    pairs = [(i, i + step) for i in range(count) if 0 <= i + step < count]
    return lax.ppermute(value, axes, pairs)


def extended_2(value, sides, width):
    for axes, dim in sides:
        length = value.shape[dim]
        last = lax.slice_in_dim(value, length - width, length, axis=dim)
        first = lax.slice_in_dim(value, 0, width, axis=dim)
        before = shifted(last, axes, 1)
        after = shifted(first, axes, -1)
        value = jnp.concatenate([before, value, after], axis=dim)
    return value


def vmem_spec():
    return pl.BlockSpec(memory_space=pltpu.VMEM)


def near_core(*arrays):
    return [pltpu.with_memory_space_constraint(a, pltpu.VMEM) for a in arrays]


def smem_spec():
    return pl.BlockSpec(memory_space=pltpu.SMEM)


def ids(meta):
    return meta[2, 0], meta[2, 1], meta[2, 2], meta[2, 3]


def first_strip(s0, core):
    return s0 + ((s0 + core) & 1)


def spread_kernel(obj, out):
    rows = jnp.concatenate([obj[0], obj[1]], axis=0).astype(bf16)
    for slot in range(NZ):
        out[slot] = rows


def pack_kernel(meta, near, out):
    _, z, core, _ = ids(meta)
    for target in range(NX * NC):
        tx, tc = target // NC, target % NC
        tile = tx * (NZ * NC) + z * NC + tc
        begin = first_strip(meta[0, tile] // ROWS, core)
        for j in range(HALF):
            slot = ((begin + 2 * j) % (NZ * NC)) // NC
            out[target, j] = near[slot]


def window_kernel(meta, got, out, tall):
    x, z, core, _ = ids(meta)
    row = meta[0, x * (NZ * NC) + z * NC + core]
    s0 = row // ROWS
    for i in range(STRIPS):
        strip = s0 + i
        source = jnp.minimum(strip // (NZ * NC), NX - 1) * NC + (strip & 1)
        block = got[source, i // 2].astype(f32)
        tall[0, pl.ds(i * ROWS, ROWS)] = block[:ROWS]
        tall[1, pl.ds(i * ROWS, ROWS)] = block[ROWS:]
    offset = row - s0 * ROWS
    for plane in range(2):
        rows = tall[plane, pl.ds(offset, PATCH)].astype(bf16)
        for peer in range(NM):
            out[peer, plane] = rows


def dot(a, b):
    return jnp.dot(a, b, preferred_element_type=f32)


def wave_kernel(meta, wins, probe0, probe1, probe2, probe3, intensity, table, out, err, far_all, tall):
    x, z, core, mode = ids(meta)
    mine = x * (NZ * NC) + z * NC + core
    row = meta[0, mine]
    col = meta[1, mine]
    s0 = row // ROWS
    offset = row - s0 * ROWS
    t_re = table[0]
    t_im = table[1]
    t_neg = -t_im
    left = jnp.concatenate(
        [jnp.concatenate([t_re, t_neg], axis=1), jnp.concatenate([t_im, t_re], axis=1)], axis=0
    )
    right = jnp.concatenate(
        [jnp.concatenate([t_re, t_im], axis=1), jnp.concatenate([t_neg, t_re], axis=1)], axis=0
    )
    full = jnp.concatenate(
        [jnp.concatenate([wins[m, p] for m in range(NM)], axis=1) for p in range(2)], axis=0
    )
    src = lax.broadcasted_iota(jnp.int32, (NM * COLS, PATCH), 0)
    dst = lax.broadcasted_iota(jnp.int32, (NM * COLS, PATCH), 1)
    take = jnp.where(src == dst + col, 1.0, 0.0).astype(bf16)
    patch = dot(full, take)
    obj_re = patch[:PATCH]
    obj_im = patch[PATCH:]
    probes = (probe0, probe1, probe2, probe3)
    power = jnp.zeros((PATCH, PATCH), f32)
    for m in range(NM):
        p_re = probes[m][0].astype(f32)
        p_im = probes[m][1].astype(f32)
        wave = jnp.concatenate(
            [(p_re * obj_re - p_im * obj_im).astype(bf16), (p_re * obj_im + p_im * obj_re).astype(bf16)],
            axis=0,
        )
        half = dot(left, wave).astype(bf16)
        far = dot(jnp.concatenate([half[:PATCH], half[PATCH:]], axis=1), right)
        far_all[m] = far
        power = power + far[:, :PATCH] * far[:, :PATCH] + far[:, PATCH:] * far[:, PATCH:]
    measured = jnp.sqrt(intensity[0])
    gap = jnp.sqrt(power) - measured
    err[...] = jnp.sum(gap * gap, keepdims=True) * (1.0 / (PATCH * PATCH))
    scale = measured / jnp.sqrt(jnp.maximum(power, floor_level))
    b_src = lax.broadcasted_iota(jnp.int32, (PATCH, COLS), 0)
    b_dst = lax.broadcasted_iota(jnp.int32, (PATCH, COLS), 1)
    keep = jnp.where(b_src == b_dst + (mode * COLS - col), 1.0, 0.0).astype(bf16)
    k_re = dot(t_re, keep).astype(bf16)
    k_im = dot(t_im, keep).astype(bf16)
    back_right = jnp.concatenate(
        [jnp.concatenate([k_re, -k_im], axis=1), jnp.concatenate([k_im, k_re], axis=1)], axis=0
    )
    sum_re = jnp.zeros((PATCH, COLS), f32)
    sum_im = jnp.zeros((PATCH, COLS), f32)
    for m in range(NM):
        far = far_all[m]
        scaled = jnp.concatenate(
            [(far[:, :PATCH] * scale).astype(bf16), (far[:, PATCH:] * scale).astype(bf16)], axis=1
        )
        half = dot(scaled, back_right).astype(bf16)
        back = dot(right, jnp.concatenate([half[:, :COLS], half[:, COLS:]], axis=0))
        back_re = back[:PATCH]
        back_im = back[PATCH:]
        q_re = dot(probes[m][0], keep)
        q_im = dot(probes[m][1], keep)
        sum_re = sum_re + (q_re * back_re + q_im * back_im)
        sum_im = sum_im + (q_re * back_im - q_im * back_re)
    tall[...] = jnp.zeros(tall.shape, f32)
    tall[0, pl.ds(offset, PATCH)] = sum_re
    tall[1, pl.ds(offset, PATCH)] = sum_im
    out[...] = jnp.zeros(out.shape, bf16)
    for i in range(STRIPS):
        strip = s0 + i
        target = jnp.minimum(strip // (NZ * NC), NX - 1) * NC + (strip & 1)
        piece = [tall[p, pl.ds(i * ROWS, ROWS)] for p in range(2)]
        out[target, i // 2] = jnp.concatenate(piece, axis=0).astype(bf16)


def gather_kernel(meta, got, out, acc):
    _, z, core, _ = ids(meta)
    acc[...] = jnp.zeros(acc.shape, f32)
    for source in range(NX * NC):
        sx, sc = source // NC, source % NC
        begin = first_strip(meta[0, sx * (NZ * NC) + z * NC + sc] // ROWS, core)
        for j in range(HALF):
            slot = ((begin + 2 * j) % (NZ * NC)) // NC
            acc[slot] = acc[slot] + got[source, j].astype(f32)
    out[...] = acc[...].astype(bf16)


def weight_kernel(meta, probe0, probe1, probe2, probe3, out, padded):
    x, z, core, mode = ids(meta)
    row0 = (x * (NZ * NC) + z * NC + core) * ROWS
    col0 = mode * COLS
    total = jnp.zeros((PATCH, PATCH), f32)
    for probe in (probe0, probe1, probe2, probe3):
        p_re = probe[0].astype(f32)
        p_im = probe[1].astype(f32)
        total = total + p_re * p_re + p_im * p_im
    padded[...] = jnp.zeros(padded.shape, f32)
    for half in range(PATCH // COLS):
        padded[1 + half, pl.ds(ROWS, PATCH)] = total[:, half * COLS : (half + 1) * COLS]
    out[...] = jnp.zeros(out.shape, f32)

    def add(k, carry):
        down = row0 - meta[0, k] + ROWS
        over = col0 - meta[1, k] + COLS
        hit = (down > 0) & (down < PATCH + ROWS) & (over > 0) & (over < PATCH + COLS)

        @pl.when(hit)
        def _():
            rows = jnp.concatenate([padded[q, pl.ds(down, ROWS)] for q in range(4)], axis=1)
            moved = pltpu.roll(rows, PATCH + 2 * COLS - over, 1)
            out[...] = out[...] + moved[:, :COLS]

        return carry

    lax.fori_loop(0, meta.shape[1], add, 0)


def dft_table():
    grid = np.arange(PATCH)[:, None] * np.arange(PATCH)[None, :] % PATCH
    angle = 2.0 * np.pi / PATCH * grid
    factor = 1.0 / math.sqrt(PATCH)
    table = np.stack([np.cos(angle) * factor, -np.sin(angle) * factor])
    return jnp.asarray(table.astype(np.float32)).astype(bf16)


CY, CX = (ROWS + 2 * HALO) // 2, (COLS + 2 * HALO) // 2
FLAT = CY * 128
CHUNK = 256
PHASES = ((0, 0), (0, 1), (1, 0), (1, 1))
SHIFTS = tuple((dy, dx) for dy in (-1, 0, 1) for dx in (-1, 0, 1))


def split_tables():
    first = np.zeros((9, 2, 4, 72), np.float32)
    last = np.zeros((9, 36, 4), np.float32)
    for tap in range(9):
        for ij, (i, j) in enumerate(PHASES):
            r, c = i + tap // 3 - 1, j + tap % 3 - 1
            p, q, dy, dx = r & 1, c & 1, r >> 1, c >> 1
            s = (dy + 1) * 3 + dx + 1
            for ch in range(2):
                first[tap, ch, ij, s * 8 + q * 4 + ch * 2 + p] = 1
            last[tap, s * 4 + ij, p * 2 + q] = 1
    return jnp.asarray(first).astype(bf16), jnp.asarray(last).astype(bf16)


def moved(value, dy, dx):
    if dx:
        value = pltpu.roll(value, (-dx) % FLAT, 1)
    if dy == 1:
        value = jnp.concatenate([value[:, 128:], value[:, :128]], axis=1)
    if dy == -1:
        value = jnp.concatenate([value[:, FLAT - 128 :], value[:, : FLAT - 128]], axis=1)
    return value


def denoise_kernel(
    meta,
    b_out,
    ext,
    first_w,
    down_w,
    mid_w,
    last_w,
    biases,
    out,
    halves,
    planes,
    taps1,
    maps,
    coarse,
    taps2,
    fourth,
    parts,
    inter,
):
    x, z, core, mode = ids(meta)
    chans = coarse.shape[0]
    height = ROWS + 2 * HALO
    width = COLS + 2 * HALO
    src = lax.broadcasted_iota(jnp.int32, (width, 256), 0)
    dst = lax.broadcasted_iota(jnp.int32, (width, 256), 1)
    lane = dst & 127
    even_odd = jnp.where((src == 2 * lane + (dst >> 7)) & (lane < CX), 1.0, 0.0).astype(bf16)
    for ch in range(2):
        row = dot(ext[ch], even_odd)
        for q in range(2):
            halves[q, pl.ds(ch * height, height)] = row[:, q * 128 : (q + 1) * 128]
    for y in range(CY):
        pieces = [
            halves[q, pl.ds(ch * height + 2 * y, 2)] for q in range(2) for ch in range(2)
        ]
        planes[:, pl.ds(y * 128, 128)] = jnp.concatenate(pieces, axis=0)
    full = planes[...]
    taps1[...] = jnp.concatenate([moved(full, dy, dx) for dy, dx in SHIFTS], axis=0).astype(bf16)

    row0 = (x * (NZ * NC) + z * NC + core) * ROWS - HALO
    col0 = mode * COLS - HALO
    height_all, width_all = NX * NZ * NC * ROWS, NM * COLS

    def masks(start):
        spot = lax.broadcasted_iota(jnp.int32, (1, CHUNK), 1) + start
        rows = row0 + 2 * (spot >> 7)
        cols = col0 + 2 * (spot & 127)
        found = []
        for p, q in PHASES:
            inside = (rows + p >= 0) & (rows + p < height_all)
            inside = inside & (cols + q >= 0) & (cols + q < width_all)
            found.append(jnp.where(inside, 1.0, 0.0))
        return found

    for start in range(0, FLAT, CHUNK):
        span = pl.ds(start, CHUNK)
        found = masks(start)
        value = dot(first_w[...], taps1[:, span])
        for n in range(4):
            part = value[n * chans : (n + 1) * chans] + biases[:, 0:1]
            maps[pl.ds(n * chans, chans), span] = (jnp.maximum(part, 0.0) * found[n]).astype(bf16)
        value = dot(down_w[...], maps[:, span]) + biases[:, 1:2]
        coarse[:, span] = (jnp.maximum(value, 0.0) * found[0]).astype(bf16).astype(f32)
    for s, (dy, dx) in enumerate(SHIFTS):
        taps2[pl.ds(s * chans, chans)] = moved(coarse[...], dy, dx).astype(bf16)
    for start in range(0, FLAT, CHUNK):
        span = pl.ds(start, CHUNK)
        found = masks(start)
        value = dot(mid_w[...], taps2[:, span]) + biases[:, 2:3]
        third = jnp.maximum(value, 0.0).astype(bf16).astype(f32)
        for n in range(4):
            rows = pl.ds(n * chans, chans)
            fourth[rows, span] = (third * found[n] + maps[rows, span].astype(f32)).astype(bf16)
        parts[:, span] = dot(last_w[...], fourth[:, span])
    total = moved(parts[pl.ds(0, 8)], *SHIFTS[0])
    for s in range(1, 9):
        total = total + moved(parts[pl.ds(s * 8, 8)], *SHIFTS[s])
    planes[...] = total
    for y in range(HALO // 2, HALO // 2 + ROWS // 2):
        tile = planes[:, pl.ds(y * 128, 128)]
        for i, j in PHASES:
            for ch in range(2):
                n = (i * 2 + j) * 2 + ch
                inter[j, pl.ds(ch * ROWS + 2 * y - HALO + i, 1)] = tile[n : n + 1]
    e_src = lax.broadcasted_iota(jnp.int32, (256, COLS), 0)
    e_dst = lax.broadcasted_iota(jnp.int32, (256, COLS), 1)
    weave = jnp.where(2 * (e_src & 127) - HALO + (e_src >> 7) == e_dst, 1.0, 0.0).astype(bf16)
    wide = jnp.concatenate([inter[0], inter[1]], axis=1)
    high = wide.astype(bf16)
    low = (wide - high.astype(f32)).astype(bf16)
    woven = dot(high, weave) + dot(low, weave)
    for ch in range(2):
        out[ch] = woven[ch * ROWS : (ch + 1) * ROWS] + b_out[ch]


def denoise(base, meta, w_in, b_in, w_down, b_down, w_mid, b_mid, w_out, b_out):
    chans = w_in.shape[1]
    extended = extended_2(base.astype(bf16), ((TILE_AXES, 1), (("mode",), 2)), HALO)
    first, last = split_tables()
    first_w = jnp.einsum("toc,tcik->iok", w_in, first).reshape(4 * chans, 72)
    last_w = jnp.einsum("tcd,tmp->mcpd", w_out, last).reshape(72, 4 * chans)
    down_w = jnp.transpose(w_down, (1, 0, 2)).reshape(chans, 4 * chans)
    mid_w = jnp.transpose(w_mid, (1, 0, 2)).reshape(chans, 9 * chans)
    return pl.pallas_call(
        denoise_kernel,
        out_shape=jax.ShapeDtypeStruct((2, ROWS, COLS), f32),
        in_specs=[smem_spec(), smem_spec()] + [vmem_spec()] * 6,
        out_specs=vmem_spec(),
        scratch_shapes=[
            pltpu.VMEM((2, 2 * (ROWS + 2 * HALO), 128), f32),
            pltpu.VMEM((8, FLAT), f32),
            pltpu.VMEM((72, FLAT), bf16),
            pltpu.VMEM((4 * chans, FLAT), bf16),
            pltpu.VMEM((chans, FLAT), f32),
            pltpu.VMEM((9 * chans, FLAT), bf16),
            pltpu.VMEM((4 * chans, FLAT), bf16),
            pltpu.VMEM((72, FLAT), f32),
            pltpu.VMEM((2, 2 * ROWS, 128), f32),
        ],
        cost_estimate=pl.CostEstimate(
            flops=4 * 10**9, bytes_accessed=2 * 10**7, transcendentals=0
        ),
        name="denoise",
    )(
        meta,
        b_out,
        extended,
        first_w,
        down_w,
        mid_w,
        last_w,
        jnp.stack([b_in, b_down, b_mid], axis=1),
    )


def per_device(
    obj_x,
    dual_u,
    probes,
    intensity,
    corners,
    owner,
    w_in,
    b_in,
    w_down,
    b_down,
    w_mid,
    b_mid,
    w_out,
    b_out,
):
    x = lax.axis_index("x")
    z = lax.axis_index("z")
    core = lax.axis_index("core")
    mode = lax.axis_index("mode")
    tiles = NX * NZ * NC
    lanes = jnp.arange(tiles, dtype=jnp.int32)
    owned = owner[None, :] == lanes[:, None]
    by_owner = jnp.sum(jnp.where(owned[None], corners[:, None, :], 0), axis=2)
    place = jnp.where(lanes == 0, x, jnp.where(lanes == 1, z, jnp.where(lanes == 2, core, mode)))
    meta = jnp.concatenate([by_owner, place[None]], axis=0).astype(jnp.int32)

    spread = pl.pallas_call(
        spread_kernel,
        out_shape=jax.ShapeDtypeStruct((NZ, 2 * ROWS, COLS), bf16),
        in_specs=[vmem_spec()],
        out_specs=vmem_spec(),
        name="spread",
    )(obj_x)
    near = lax.all_to_all(spread, "z", 0, 0, tiled=True)
    probe0 = probes[0].astype(bf16)
    others = [
        lax.ppermute(probe0, "mode", [(i, (i + k) % NM) for i in range(NM)])
        for k in range(1, NM)
    ]
    all_probes = (probe0, *others)
    packed = pl.pallas_call(
        pack_kernel,
        out_shape=jax.ShapeDtypeStruct((NX * NC, HALF, 2 * ROWS, COLS), bf16),
        in_specs=[smem_spec(), vmem_spec()],
        out_specs=vmem_spec(),
        name="pack",
    )(meta, *near_core(near))
    got = lax.all_to_all(packed, ("x", "core"), 0, 0, tiled=True)
    window = pl.pallas_call(
        window_kernel,
        out_shape=jax.ShapeDtypeStruct((NM, 2, PATCH, COLS), bf16),
        in_specs=[smem_spec(), vmem_spec()],
        out_specs=vmem_spec(),
        scratch_shapes=[pltpu.VMEM((2, STRIPS * ROWS, COLS), f32)],
        name="window",
    )(meta, *near_core(got))
    wins = lax.all_to_all(window, "mode", 0, 0, tiled=True)
    updates, misfit = pl.pallas_call(
        wave_kernel,
        out_shape=(
            jax.ShapeDtypeStruct((NX * NC, HALF, 2 * ROWS, COLS), bf16),
            jax.ShapeDtypeStruct((1, 1), f32),
        ),
        in_specs=[smem_spec()] + [vmem_spec()] * 7,
        out_specs=(vmem_spec(), vmem_spec()),
        scratch_shapes=[
            pltpu.VMEM((NM, PATCH, 2 * PATCH), f32),
            pltpu.VMEM((2, STRIPS * ROWS, COLS), f32),
        ],
        name="wave",
    )(meta, *near_core(wins, *all_probes), intensity, dft_table())
    back = lax.all_to_all(updates, ("x", "core"), 0, 0, tiled=True)
    partial = pl.pallas_call(
        gather_kernel,
        out_shape=jax.ShapeDtypeStruct((NZ, 2 * ROWS, COLS), bf16),
        in_specs=[smem_spec(), vmem_spec()],
        out_specs=vmem_spec(),
        scratch_shapes=[pltpu.VMEM((NZ, 2 * ROWS, COLS), f32)],
        name="gather",
    )(meta, *near_core(back))
    pieces = lax.all_to_all(partial, "z", 0, 0, tiled=True)
    denom = pl.pallas_call(
        weight_kernel,
        out_shape=jax.ShapeDtypeStruct((ROWS, COLS), f32),
        in_specs=[smem_spec()] + [vmem_spec()] * NM,
        out_specs=vmem_spec(),
        scratch_shapes=[pltpu.VMEM((PATCH // COLS + 2, PATCH + 2 * ROWS, COLS), f32)],
        name="weight",
    )(meta, *near_core(*all_probes))
    base = obj_x + dual_u
    center = denoise(base, meta, w_in, b_in, w_down, b_down, w_mid, b_mid, w_out, b_out)
    aux_next = base - center
    numer = jnp.sum(pieces.astype(f32), axis=0).reshape(2, ROWS, COLS)
    obj_next = (numer + rho_weight * (aux_next - dual_u)) / (denom + rho_weight)
    dual_next = dual_u + obj_next - aux_next
    return (obj_next, aux_next, dual_next, misfit.reshape(1))


def solution(mesh):
    split = Mesh(mesh.devices.reshape(NX, NZ, NC, NM), TILE_AXES + ("mode",))
    grid = P(None, TILE_AXES, "mode")
    return jax.shard_map(
        per_device,
        mesh=split,
        in_specs=(
            grid,
            grid,
            P("mode", None, None, None),
            P(TILE_AXES, None, None),
        )
        + (P(),) * 10,
        out_specs=(grid, grid, grid, P(TILE_AXES)),
        check_vma=False,
    )
```

```python
import math

import jax
import jax.numpy as jnp
import numpy as np
from jax import lax
from jax.experimental import pallas as pl
from jax.experimental.pallas import tpu as pltpu
from jax.sharding import Mesh, PartitionSpec as P

HALO = 6
NX, NZ, NC, NM = 4, 16, 2, 4
PATCH = 256
ROWS = 32
COLS = 128
STRIPS = PATCH // ROWS + 1
HALF = PATCH // ROWS // 2

rho_weight = 2.0
floor_level = 0.25
f32 = jnp.float32
bf16 = jnp.bfloat16
TILE_AXES = ("x", "z", "core")


def shifted(value, axes, step):
    count = math.prod(lax.axis_size(a) for a in axes)
    pairs = [(i, i + step) for i in range(count) if 0 <= i + step < count]
    return lax.ppermute(value, axes, pairs)


def extended_2(value, sides, width):
    for axes, dim in sides:
        length = value.shape[dim]
        last = lax.slice_in_dim(value, length - width, length, axis=dim)
        first = lax.slice_in_dim(value, 0, width, axis=dim)
        before = shifted(last, axes, 1)
        after = shifted(first, axes, -1)
        value = jnp.concatenate([before, value, after], axis=dim)
    return value


def vmem_spec():
    return pl.BlockSpec(memory_space=pltpu.VMEM)


def near_core(*arrays):
    return [pltpu.with_memory_space_constraint(a, pltpu.VMEM) for a in arrays]


def any_spec():
    return pl.BlockSpec(memory_space=pl.ANY)


def smem_spec():
    return pl.BlockSpec(memory_space=pltpu.SMEM)


def ids(meta):
    return meta[2, 0], meta[2, 1], meta[2, 2], meta[2, 3]


def first_strip(s0, core):
    return s0 + ((s0 + core) & 1)


def copy_out(held, out, sems, count, same):
    copies = [
        pltpu.make_async_copy(held if same else held.at[n], out.at[n], sems.at[n])
        for n in range(count)
    ]
    for copy in copies:
        copy.start()
    return copies


def spread_kernel(obj, out, held, sems):
    held[...] = jnp.concatenate([obj[0], obj[1]], axis=0).astype(bf16)
    for copy in copy_out(held, out, sems, NZ, True):
        copy.wait()


def row_in_strip():
    return lax.broadcasted_iota(jnp.int32, (2 * ROWS, COLS), 0) & (ROWS - 1)


def z_slot(strip):
    return (strip % (NZ * NC)) // NC


def strips_of(row, core):
    s0 = row // ROWS
    begin = first_strip(s0, core)
    return begin, jnp.where(begin == s0, row - s0 * ROWS, 0)


def pack_kernel(meta, near, out, held, sems):
    _, z, core, _ = ids(meta)
    rows = row_in_strip()
    copies = []
    for target in range(NX * NC):
        tx, tc = target // NC, target % NC
        begin, cut = strips_of(meta[0, tx * (NZ * NC) + z * NC + tc], core)
        late = near[z_slot(begin + 2 * HALF)].astype(f32)
        early = near[z_slot(begin)].astype(f32)
        held[target, 0] = jnp.where(rows < cut, late, early).astype(bf16)
        for j in range(1, HALF):
            held[target, j] = near[z_slot(begin + 2 * j)]
        copy = pltpu.make_async_copy(held.at[target], out.at[target], sems.at[target])
        copy.start()
        copies.append(copy)
    for copy in copies:
        copy.wait()


def window_kernel(meta, got, out, tall, held, sems):
    x, z, core, _ = ids(meta)
    row = meta[0, x * (NZ * NC) + z * NC + core]
    s0 = row // ROWS
    for i in range(STRIPS):
        strip = s0 + i
        source = jnp.minimum(strip // (NZ * NC), NX - 1) * NC + (strip & 1)
        block = got[source, (i // 2) % HALF].astype(f32)
        tall[0, pl.ds(i * ROWS, ROWS)] = block[:ROWS]
        tall[1, pl.ds(i * ROWS, ROWS)] = block[ROWS:]
    offset = row - s0 * ROWS
    for plane in range(2):
        held[plane] = tall[plane, pl.ds(offset, PATCH)].astype(bf16)
    for copy in copy_out(held, out, sems, NM, True):
        copy.wait()


def dot(a, b):
    return jnp.dot(a, b, preferred_element_type=f32)


def wave_kernel(meta, wins, probe0, probe1, probe2, probe3, intensity, table, out, err, far_all, tall):
    x, z, core, mode = ids(meta)
    mine = x * (NZ * NC) + z * NC + core
    row = meta[0, mine]
    col = meta[1, mine]
    s0 = row // ROWS
    offset = row - s0 * ROWS
    t_re = table[0]
    t_im = table[1]
    t_neg = -t_im
    left = jnp.concatenate(
        [jnp.concatenate([t_re, t_neg], axis=1), jnp.concatenate([t_im, t_re], axis=1)], axis=0
    )
    right = jnp.concatenate(
        [jnp.concatenate([t_re, t_im], axis=1), jnp.concatenate([t_neg, t_re], axis=1)], axis=0
    )
    full = jnp.concatenate(
        [jnp.concatenate([wins[m, p] for m in range(NM)], axis=1) for p in range(2)], axis=0
    )
    src = lax.broadcasted_iota(jnp.int32, (NM * COLS, PATCH), 0)
    dst = lax.broadcasted_iota(jnp.int32, (NM * COLS, PATCH), 1)
    take = jnp.where(src == dst + col, 1.0, 0.0).astype(bf16)
    patch = dot(full, take)
    obj_re = patch[:PATCH]
    obj_im = patch[PATCH:]
    probes = (probe0, probe1, probe2, probe3)
    power = jnp.zeros((PATCH, PATCH), f32)
    for m in range(NM):
        p_re = probes[m][0].astype(f32)
        p_im = probes[m][1].astype(f32)
        wave = jnp.concatenate(
            [(p_re * obj_re - p_im * obj_im).astype(bf16), (p_re * obj_im + p_im * obj_re).astype(bf16)],
            axis=0,
        )
        half = dot(left, wave).astype(bf16)
        far = dot(jnp.concatenate([half[:PATCH], half[PATCH:]], axis=1), right)
        far_all[m] = far
        power = power + far[:, :PATCH] * far[:, :PATCH] + far[:, PATCH:] * far[:, PATCH:]
    measured = jnp.sqrt(intensity[0])
    gap = jnp.sqrt(power) - measured
    err[...] = jnp.sum(gap * gap, keepdims=True) * (1.0 / (PATCH * PATCH))
    scale = measured / jnp.sqrt(jnp.maximum(power, floor_level))
    b_src = lax.broadcasted_iota(jnp.int32, (PATCH, COLS), 0)
    b_dst = lax.broadcasted_iota(jnp.int32, (PATCH, COLS), 1)
    keep = jnp.where(b_src == b_dst + (mode * COLS - col), 1.0, 0.0).astype(bf16)
    k_re = dot(t_re, keep).astype(bf16)
    k_im = dot(t_im, keep).astype(bf16)
    back_right = jnp.concatenate(
        [jnp.concatenate([k_re, -k_im], axis=1), jnp.concatenate([k_im, k_re], axis=1)], axis=0
    )
    sum_re = jnp.zeros((PATCH, COLS), f32)
    sum_im = jnp.zeros((PATCH, COLS), f32)
    for m in range(NM):
        far = far_all[m]
        scaled = jnp.concatenate(
            [(far[:, :PATCH] * scale).astype(bf16), (far[:, PATCH:] * scale).astype(bf16)], axis=1
        )
        half = dot(scaled, back_right).astype(bf16)
        back = dot(right, jnp.concatenate([half[:, :COLS], half[:, COLS:]], axis=0))
        back_re = back[:PATCH]
        back_im = back[PATCH:]
        q_re = dot(probes[m][0], keep)
        q_im = dot(probes[m][1], keep)
        sum_re = sum_re + (q_re * back_re + q_im * back_im)
        sum_im = sum_im + (q_re * back_im - q_im * back_re)
    tall[...] = jnp.zeros(tall.shape, f32)
    tall[0, pl.ds(offset, PATCH)] = sum_re
    tall[1, pl.ds(offset, PATCH)] = sum_im
    out[...] = jnp.zeros(out.shape, bf16)
    for i in range(STRIPS):
        strip = s0 + i
        target = jnp.minimum(strip // (NZ * NC), NX - 1) * NC + (strip & 1)
        piece = jnp.concatenate([tall[p, pl.ds(i * ROWS, ROWS)] for p in range(2)], axis=0)
        if i < 2 * HALF:
            out[target, i // 2] = piece.astype(bf16)
        else:
            out[target, 0] = (out[target, 0].astype(f32) + piece).astype(bf16)


def gather_kernel(meta, got, out, acc):
    _, z, core, _ = ids(meta)
    rows = row_in_strip()
    acc[...] = jnp.zeros(acc.shape, f32)
    for source in range(NX * NC):
        sx, sc = source // NC, source % NC
        begin, cut = strips_of(meta[0, sx * (NZ * NC) + z * NC + sc], core)
        both = got[source, 0].astype(f32)
        late, early = z_slot(begin + 2 * HALF), z_slot(begin)
        acc[late] = acc[late] + jnp.where(rows < cut, both, 0.0)
        acc[early] = acc[early] + jnp.where(rows < cut, 0.0, both)
        for j in range(1, HALF):
            slot = z_slot(begin + 2 * j)
            acc[slot] = acc[slot] + got[source, j].astype(f32)
    out[...] = acc[...].astype(bf16)


def weight_kernel(meta, probe0, probe1, probe2, probe3, out, padded):
    x, z, core, mode = ids(meta)
    row0 = (x * (NZ * NC) + z * NC + core) * ROWS
    col0 = mode * COLS
    total = jnp.zeros((PATCH, PATCH), f32)
    for probe in (probe0, probe1, probe2, probe3):
        p_re = probe[0].astype(f32)
        p_im = probe[1].astype(f32)
        total = total + p_re * p_re + p_im * p_im
    padded[...] = jnp.zeros(padded.shape, f32)
    for half in range(PATCH // COLS):
        padded[1 + half, pl.ds(ROWS, PATCH)] = total[:, half * COLS : (half + 1) * COLS]
    out[...] = jnp.zeros(out.shape, f32)

    def add(k, carry):
        down = row0 - meta[0, k] + ROWS
        over = col0 - meta[1, k] + COLS
        hit = (down > 0) & (down < PATCH + ROWS) & (over > 0) & (over < PATCH + COLS)

        @pl.when(hit)
        def _():
            rows = jnp.concatenate([padded[q, pl.ds(down, ROWS)] for q in range(4)], axis=1)
            moved = pltpu.roll(rows, PATCH + 2 * COLS - over, 1)
            out[...] = out[...] + moved[:, :COLS]

        return carry

    lax.fori_loop(0, meta.shape[1], add, 0)


def dft_table():
    grid = np.arange(PATCH)[:, None] * np.arange(PATCH)[None, :] % PATCH
    angle = 2.0 * np.pi / PATCH * grid
    factor = 1.0 / math.sqrt(PATCH)
    table = np.stack([np.cos(angle) * factor, -np.sin(angle) * factor])
    return jnp.asarray(table.astype(np.float32)).astype(bf16)


CY, CX = (ROWS + 2 * HALO) // 2, (COLS + 2 * HALO) // 2
FLAT = CY * 128
CHUNK = 256
PHASES = ((0, 0), (0, 1), (1, 0), (1, 1))
SHIFTS = tuple((dy, dx) for dy in (-1, 0, 1) for dx in (-1, 0, 1))


def split_tables():
    first = np.zeros((9, 2, 4, 72), np.float32)
    last = np.zeros((9, 36, 4), np.float32)
    for tap in range(9):
        for ij, (i, j) in enumerate(PHASES):
            r, c = i + tap // 3 - 1, j + tap % 3 - 1
            p, q, dy, dx = r & 1, c & 1, r >> 1, c >> 1
            s = (dy + 1) * 3 + dx + 1
            for ch in range(2):
                first[tap, ch, ij, s * 8 + q * 4 + ch * 2 + p] = 1
            last[tap, s * 4 + ij, p * 2 + q] = 1
    return jnp.asarray(first).astype(bf16), jnp.asarray(last).astype(bf16)


def moved(value, dy, dx):
    if dx:
        value = pltpu.roll(value, (-dx) % FLAT, 1)
    if dy == 1:
        value = jnp.concatenate([value[:, 128:], value[:, :128]], axis=1)
    if dy == -1:
        value = jnp.concatenate([value[:, FLAT - 128 :], value[:, : FLAT - 128]], axis=1)
    return value


def denoise_kernel(
    meta,
    b_out,
    ext,
    first_w,
    down_w,
    mid_w,
    last_w,
    biases,
    out,
    halves,
    planes,
    taps1,
    maps,
    coarse,
    taps2,
    fourth,
    parts,
    inter,
):
    x, z, core, mode = ids(meta)
    chans = coarse.shape[0]
    height = ROWS + 2 * HALO
    width = COLS + 2 * HALO
    src = lax.broadcasted_iota(jnp.int32, (width, 256), 0)
    dst = lax.broadcasted_iota(jnp.int32, (width, 256), 1)
    lane = dst & 127
    even_odd = jnp.where((src == 2 * lane + (dst >> 7)) & (lane < CX), 1.0, 0.0).astype(bf16)
    for ch in range(2):
        row = dot(ext[ch], even_odd)
        for q in range(2):
            halves[q, pl.ds(ch * height, height)] = row[:, q * 128 : (q + 1) * 128]
    for y in range(CY):
        pieces = [
            halves[q, pl.ds(ch * height + 2 * y, 2)] for q in range(2) for ch in range(2)
        ]
        planes[:, pl.ds(y * 128, 128)] = jnp.concatenate(pieces, axis=0)
    full = planes[...]
    taps1[...] = jnp.concatenate([moved(full, dy, dx) for dy, dx in SHIFTS], axis=0).astype(bf16)

    row0 = (x * (NZ * NC) + z * NC + core) * ROWS - HALO
    col0 = mode * COLS - HALO
    height_all, width_all = NX * NZ * NC * ROWS, NM * COLS

    def masks(start):
        spot = lax.broadcasted_iota(jnp.int32, (1, CHUNK), 1) + start
        rows = row0 + 2 * (spot >> 7)
        cols = col0 + 2 * (spot & 127)
        found = []
        for p, q in PHASES:
            inside = (rows + p >= 0) & (rows + p < height_all)
            inside = inside & (cols + q >= 0) & (cols + q < width_all)
            found.append(jnp.where(inside, 1.0, 0.0))
        return found

    for start in range(0, FLAT, CHUNK):
        span = pl.ds(start, CHUNK)
        found = masks(start)
        value = dot(first_w[...], taps1[:, span])
        for n in range(4):
            part = value[n * chans : (n + 1) * chans] + biases[:, 0:1]
            maps[pl.ds(n * chans, chans), span] = (jnp.maximum(part, 0.0) * found[n]).astype(bf16)
        value = dot(down_w[...], maps[:, span]) + biases[:, 1:2]
        coarse[:, span] = (jnp.maximum(value, 0.0) * found[0]).astype(bf16).astype(f32)
    for s, (dy, dx) in enumerate(SHIFTS):
        taps2[pl.ds(s * chans, chans)] = moved(coarse[...], dy, dx).astype(bf16)
    for start in range(0, FLAT, CHUNK):
        span = pl.ds(start, CHUNK)
        found = masks(start)
        value = dot(mid_w[...], taps2[:, span]) + biases[:, 2:3]
        third = jnp.maximum(value, 0.0).astype(bf16).astype(f32)
        for n in range(4):
            rows = pl.ds(n * chans, chans)
            fourth[rows, span] = (third * found[n] + maps[rows, span].astype(f32)).astype(bf16)
        parts[:, span] = dot(last_w[...], fourth[:, span])
    total = moved(parts[pl.ds(0, 8)], *SHIFTS[0])
    for s in range(1, 9):
        total = total + moved(parts[pl.ds(s * 8, 8)], *SHIFTS[s])
    planes[...] = total
    for y in range(HALO // 2, HALO // 2 + ROWS // 2):
        tile = planes[:, pl.ds(y * 128, 128)]
        for i, j in PHASES:
            for ch in range(2):
                n = (i * 2 + j) * 2 + ch
                inter[j, pl.ds(ch * ROWS + 2 * y - HALO + i, 1)] = tile[n : n + 1]
    e_src = lax.broadcasted_iota(jnp.int32, (256, COLS), 0)
    e_dst = lax.broadcasted_iota(jnp.int32, (256, COLS), 1)
    weave = jnp.where(2 * (e_src & 127) - HALO + (e_src >> 7) == e_dst, 1.0, 0.0).astype(bf16)
    wide = jnp.concatenate([inter[0], inter[1]], axis=1)
    high = wide.astype(bf16)
    low = (wide - high.astype(f32)).astype(bf16)
    woven = dot(high, weave) + dot(low, weave)
    for ch in range(2):
        out[ch] = woven[ch * ROWS : (ch + 1) * ROWS] + b_out[ch]


def denoise(base, meta, w_in, b_in, w_down, b_down, w_mid, b_mid, w_out, b_out):
    chans = w_in.shape[1]
    extended = extended_2(base.astype(bf16), ((TILE_AXES, 1), (("mode",), 2)), HALO)
    first, last = split_tables()
    first_w = jnp.einsum("toc,tcik->iok", w_in, first).reshape(4 * chans, 72)
    last_w = jnp.einsum("tcd,tmp->mcpd", w_out, last).reshape(72, 4 * chans)
    down_w = jnp.transpose(w_down, (1, 0, 2)).reshape(chans, 4 * chans)
    mid_w = jnp.transpose(w_mid, (1, 0, 2)).reshape(chans, 9 * chans)
    return pl.pallas_call(
        denoise_kernel,
        out_shape=jax.ShapeDtypeStruct((2, ROWS, COLS), f32),
        in_specs=[smem_spec(), smem_spec()] + [vmem_spec()] * 6,
        out_specs=vmem_spec(),
        scratch_shapes=[
            pltpu.VMEM((2, 2 * (ROWS + 2 * HALO), 128), f32),
            pltpu.VMEM((8, FLAT), f32),
            pltpu.VMEM((72, FLAT), bf16),
            pltpu.VMEM((4 * chans, FLAT), bf16),
            pltpu.VMEM((chans, FLAT), f32),
            pltpu.VMEM((9 * chans, FLAT), bf16),
            pltpu.VMEM((4 * chans, FLAT), bf16),
            pltpu.VMEM((72, FLAT), f32),
            pltpu.VMEM((2, 2 * ROWS, 128), f32),
        ],
        cost_estimate=pl.CostEstimate(
            flops=4 * 10**9, bytes_accessed=2 * 10**7, transcendentals=0
        ),
        name="denoise",
    )(
        meta,
        b_out,
        extended,
        first_w,
        down_w,
        mid_w,
        last_w,
        jnp.stack([b_in, b_down, b_mid], axis=1),
    )


def per_device(
    obj_x,
    dual_u,
    probes,
    intensity,
    corners,
    owner,
    w_in,
    b_in,
    w_down,
    b_down,
    w_mid,
    b_mid,
    w_out,
    b_out,
):
    x = lax.axis_index("x")
    z = lax.axis_index("z")
    core = lax.axis_index("core")
    mode = lax.axis_index("mode")
    tiles = NX * NZ * NC
    lanes = jnp.arange(tiles, dtype=jnp.int32)
    owned = owner[None, :] == lanes[:, None]
    by_owner = jnp.sum(jnp.where(owned[None], corners[:, None, :], 0), axis=2)
    place = jnp.where(lanes == 0, x, jnp.where(lanes == 1, z, jnp.where(lanes == 2, core, mode)))
    meta = jnp.concatenate([by_owner, place[None]], axis=0).astype(jnp.int32)

    spread = pl.pallas_call(
        spread_kernel,
        out_shape=jax.ShapeDtypeStruct((NZ, 2 * ROWS, COLS), bf16),
        in_specs=[vmem_spec()],
        out_specs=any_spec(),
        scratch_shapes=[pltpu.VMEM((2 * ROWS, COLS), bf16), pltpu.SemaphoreType.DMA((NZ,))],
        name="spread",
    )(obj_x)
    near = lax.all_to_all(spread, "z", 0, 0, tiled=True)
    probe0 = probes[0].astype(bf16)
    others = [
        lax.ppermute(probe0, "mode", [(i, (i + k) % NM) for i in range(NM)])
        for k in range(1, NM)
    ]
    all_probes = (probe0, *others)
    packed = pl.pallas_call(
        pack_kernel,
        out_shape=jax.ShapeDtypeStruct((NX * NC, HALF, 2 * ROWS, COLS), bf16),
        in_specs=[smem_spec(), vmem_spec()],
        out_specs=any_spec(),
        scratch_shapes=[
            pltpu.VMEM((NX * NC, HALF, 2 * ROWS, COLS), bf16),
            pltpu.SemaphoreType.DMA((NX * NC,)),
        ],
        name="pack",
    )(meta, *near_core(near))
    got = lax.all_to_all(packed, ("x", "core"), 0, 0, tiled=True)
    window = pl.pallas_call(
        window_kernel,
        out_shape=jax.ShapeDtypeStruct((NM, 2, PATCH, COLS), bf16),
        in_specs=[smem_spec(), vmem_spec()],
        out_specs=any_spec(),
        scratch_shapes=[
            pltpu.VMEM((2, STRIPS * ROWS, COLS), f32),
            pltpu.VMEM((2, PATCH, COLS), bf16),
            pltpu.SemaphoreType.DMA((NM,)),
        ],
        name="window",
    )(meta, *near_core(got))
    wins = lax.all_to_all(window, "mode", 0, 0, tiled=True)
    updates, misfit = pl.pallas_call(
        wave_kernel,
        out_shape=(
            jax.ShapeDtypeStruct((NX * NC, HALF, 2 * ROWS, COLS), bf16),
            jax.ShapeDtypeStruct((1, 1), f32),
        ),
        in_specs=[smem_spec()] + [vmem_spec()] * 7,
        out_specs=(vmem_spec(), vmem_spec()),
        scratch_shapes=[
            pltpu.VMEM((NM, PATCH, 2 * PATCH), f32),
            pltpu.VMEM((2, STRIPS * ROWS, COLS), f32),
        ],
        name="wave",
    )(meta, *near_core(wins, *all_probes), intensity, dft_table())
    back = lax.all_to_all(updates, ("x", "core"), 0, 0, tiled=True)
    partial = pl.pallas_call(
        gather_kernel,
        out_shape=jax.ShapeDtypeStruct((NZ, 2 * ROWS, COLS), bf16),
        in_specs=[smem_spec(), vmem_spec()],
        out_specs=vmem_spec(),
        scratch_shapes=[pltpu.VMEM((NZ, 2 * ROWS, COLS), f32)],
        name="gather",
    )(meta, *near_core(back))
    pieces = lax.all_to_all(partial, "z", 0, 0, tiled=True)
    denom = pl.pallas_call(
        weight_kernel,
        out_shape=jax.ShapeDtypeStruct((ROWS, COLS), f32),
        in_specs=[smem_spec()] + [vmem_spec()] * NM,
        out_specs=vmem_spec(),
        scratch_shapes=[pltpu.VMEM((PATCH // COLS + 2, PATCH + 2 * ROWS, COLS), f32)],
        name="weight",
    )(meta, *near_core(*all_probes))
    base = obj_x + dual_u
    center = denoise(base, meta, w_in, b_in, w_down, b_down, w_mid, b_mid, w_out, b_out)
    aux_next = base - center
    numer = jnp.sum(pieces.astype(f32), axis=0).reshape(2, ROWS, COLS)
    obj_next = (numer + rho_weight * (aux_next - dual_u)) / (denom + rho_weight)
    dual_next = dual_u + obj_next - aux_next
    return (obj_next, aux_next, dual_next, misfit.reshape(1))


def solution(mesh):
    split = Mesh(mesh.devices.reshape(NX, NZ, NC, NM), TILE_AXES + ("mode",))
    grid = P(None, TILE_AXES, "mode")
    return jax.shard_map(
        per_device,
        mesh=split,
        in_specs=(
            grid,
            grid,
            P("mode", None, None, None),
            P(TILE_AXES, None, None),
        )
        + (P(),) * 10,
        out_specs=(grid, grid, grid, P(TILE_AXES)),
        check_vma=False,
    )
```

```python
import math

import jax
import jax.numpy as jnp
import numpy as np
from jax import lax
from jax.experimental import pallas as pl
from jax.experimental.pallas import tpu as pltpu
from jax.sharding import Mesh, PartitionSpec as P

HALO = 6
NX, NZ, NC, NM = 4, 16, 2, 4
PATCH = 256
ROWS = 32
COLS = 128
STRIPS = PATCH // ROWS + 1
HALF = PATCH // ROWS // 2

rho_weight = 2.0
floor_level = 0.25
f32 = jnp.float32
bf16 = jnp.bfloat16
TILE_AXES = ("x", "z", "core")


def shifted(value, axes, step):
    count = math.prod(lax.axis_size(a) for a in axes)
    pairs = [(i, i + step) for i in range(count) if 0 <= i + step < count]
    return lax.ppermute(value, axes, pairs)


def extended_2(value, sides, width):
    for axes, dim in sides:
        length = value.shape[dim]
        last = lax.slice_in_dim(value, length - width, length, axis=dim)
        first = lax.slice_in_dim(value, 0, width, axis=dim)
        before = shifted(last, axes, 1)
        after = shifted(first, axes, -1)
        value = jnp.concatenate([before, value, after], axis=dim)
    return value


def vmem_spec():
    return pl.BlockSpec(memory_space=pltpu.VMEM)


def near_core(*arrays):
    return [pltpu.with_memory_space_constraint(a, pltpu.VMEM) for a in arrays]


def any_spec():
    return pl.BlockSpec(memory_space=pl.ANY)


def smem_spec():
    return pl.BlockSpec(memory_space=pltpu.SMEM)


def ids(meta):
    return meta[2, 0], meta[2, 1], meta[2, 2], meta[2, 3]


def first_strip(s0, core):
    return s0 + ((s0 + core) & 1)


def copy_out(held, out, sems, count, same):
    copies = [
        pltpu.make_async_copy(held if same else held.at[n], out.at[n], sems.at[n])
        for n in range(count)
    ]
    for copy in copies:
        copy.start()
    return copies


def row_in_strip():
    return lax.broadcasted_iota(jnp.int32, (2 * ROWS, COLS), 0) & (ROWS - 1)


def z_slot(strip):
    return (strip % (NZ * NC)) // NC


def strips_of(row, core):
    s0 = row // ROWS
    begin = first_strip(s0, core)
    return begin, jnp.where(begin == s0, row - s0 * ROWS, 0)


def pack_kernel(meta, near, out, held, sems):
    _, z, core, _ = ids(meta)
    rows = row_in_strip()
    copies = []
    for target in range(NX * NC):
        tx, tc = target // NC, target % NC
        begin, cut = strips_of(meta[0, tx * (NZ * NC) + z * NC + tc], core)
        late = near[z_slot(begin + 2 * HALF)].astype(f32)
        early = near[z_slot(begin)].astype(f32)
        held[target, 0] = jnp.where(rows < cut, late, early).astype(bf16)
        for j in range(1, HALF):
            held[target, j] = near[z_slot(begin + 2 * j)]
        copy = pltpu.make_async_copy(held.at[target], out.at[target], sems.at[target])
        copy.start()
        copies.append(copy)
    for copy in copies:
        copy.wait()


def window_kernel(meta, got, out, tall, held, sems):
    x, z, core, _ = ids(meta)
    row = meta[0, x * (NZ * NC) + z * NC + core]
    s0 = row // ROWS
    for i in range(STRIPS):
        strip = s0 + i
        source = jnp.minimum(strip // (NZ * NC), NX - 1) * NC + (strip & 1)
        block = got[source, (i // 2) % HALF].astype(f32)
        tall[0, pl.ds(i * ROWS, ROWS)] = block[:ROWS]
        tall[1, pl.ds(i * ROWS, ROWS)] = block[ROWS:]
    offset = row - s0 * ROWS
    for plane in range(2):
        held[plane] = tall[plane, pl.ds(offset, PATCH)].astype(bf16)
    for copy in copy_out(held, out, sems, NM, True):
        copy.wait()


def dot(a, b):
    return jnp.dot(a, b, preferred_element_type=f32)


def wave_kernel(
    meta, wins, probe0, probe1, probe2, probe3, side, turn, intensity, table, out, err, far_all, tall
):
    x, z, core, _ = ids(meta)
    mine = x * (NZ * NC) + z * NC + core
    row = meta[0, mine]
    col = meta[1, mine]
    s0 = row // ROWS
    offset = row - s0 * ROWS
    t_re = table[0]
    t_im = table[1]
    t_neg = -t_im
    left = jnp.concatenate(
        [jnp.concatenate([t_re, t_neg], axis=1), jnp.concatenate([t_im, t_re], axis=1)], axis=0
    )
    right = jnp.concatenate(
        [jnp.concatenate([t_re, t_im], axis=1), jnp.concatenate([t_neg, t_re], axis=1)], axis=0
    )
    full = jnp.concatenate(
        [jnp.concatenate([wins[m, p] for m in range(NM)], axis=1) for p in range(2)], axis=0
    )
    src = lax.broadcasted_iota(jnp.int32, (NM * COLS, PATCH), 0)
    dst = lax.broadcasted_iota(jnp.int32, (NM * COLS, PATCH), 1)
    take = jnp.where(src == dst + col, 1.0, 0.0).astype(bf16)
    patch = dot(full, take)
    obj_re = patch[:PATCH]
    obj_im = patch[PATCH:]
    probes = (probe0, probe1, probe2, probe3)
    power = jnp.zeros((PATCH, PATCH), f32)
    for m in range(NM):
        p_re = probes[m][0].astype(f32)
        p_im = probes[m][1].astype(f32)
        wave = jnp.concatenate(
            [(p_re * obj_re - p_im * obj_im).astype(bf16), (p_re * obj_im + p_im * obj_re).astype(bf16)],
            axis=0,
        )
        half = dot(left, wave).astype(bf16)
        far = dot(jnp.concatenate([half[:PATCH], half[PATCH:]], axis=1), right)
        far_all[m] = far
        power = power + far[:, :PATCH] * far[:, :PATCH] + far[:, PATCH:] * far[:, PATCH:]
    measured = jnp.sqrt(intensity[0])
    gap = jnp.sqrt(power) - measured
    err[...] = jnp.sum(gap * gap, keepdims=True) * (1.0 / (PATCH * PATCH))
    scale = measured / jnp.sqrt(jnp.maximum(power, floor_level))
    sums = [jnp.zeros((PATCH, 2 * COLS), f32) for _ in range(2)]
    for pair in range(NM // 2):
        halves = []
        for m in (2 * pair, 2 * pair + 1):
            far = far_all[m]
            scaled = jnp.concatenate(
                [(far[:, :PATCH] * scale).astype(bf16), (far[:, PATCH:] * scale).astype(bf16)],
                axis=1,
            )
            halves.append(dot(scaled, turn[...]).astype(bf16))
        stacked = [
            jnp.concatenate([h[:, p * COLS : (p + 1) * COLS] for h in halves], axis=1)
            for p in range(2)
        ]
        back = dot(right, jnp.concatenate(stacked, axis=0))
        back_re = back[:PATCH]
        back_im = back[PATCH:]
        q_re = side[pair, 0].astype(f32)
        q_im = side[pair, 1].astype(f32)
        sums[0] = sums[0] + (q_re * back_re + q_im * back_im)
        sums[1] = sums[1] + (q_re * back_im - q_im * back_re)
    sum_re, sum_im = [v[:, :COLS] + v[:, COLS:] for v in sums]
    tall[...] = jnp.zeros(tall.shape, f32)
    tall[0, pl.ds(offset, PATCH)] = sum_re
    tall[1, pl.ds(offset, PATCH)] = sum_im
    out[...] = jnp.zeros(out.shape, bf16)
    for i in range(STRIPS):
        strip = s0 + i
        target = jnp.minimum(strip // (NZ * NC), NX - 1) * NC + (strip & 1)
        piece = jnp.concatenate([tall[p, pl.ds(i * ROWS, ROWS)] for p in range(2)], axis=0)
        if i < 2 * HALF:
            out[target, i // 2] = piece.astype(bf16)
        else:
            out[target, 0] = (out[target, 0].astype(f32) + piece).astype(bf16)


def gather_kernel(meta, got, out, acc):
    _, z, core, _ = ids(meta)
    rows = row_in_strip()
    acc[...] = jnp.zeros(acc.shape, f32)
    for source in range(NX * NC):
        sx, sc = source // NC, source % NC
        begin, cut = strips_of(meta[0, sx * (NZ * NC) + z * NC + sc], core)
        both = got[source, 0].astype(f32)
        late, early = z_slot(begin + 2 * HALF), z_slot(begin)
        acc[late] = acc[late] + jnp.where(rows < cut, both, 0.0)
        acc[early] = acc[early] + jnp.where(rows < cut, 0.0, both)
        for j in range(1, HALF):
            slot = z_slot(begin + 2 * j)
            acc[slot] = acc[slot] + got[source, j].astype(f32)
    out[...] = acc[...].astype(bf16)


def weight_kernel(meta, probe0, probe1, probe2, probe3, table, out, side, turn, padded):
    x, z, core, mode = ids(meta)
    row0 = (x * (NZ * NC) + z * NC + core) * ROWS
    col0 = mode * COLS
    probes = (probe0, probe1, probe2, probe3)
    mine = x * (NZ * NC) + z * NC + core
    src = lax.broadcasted_iota(jnp.int32, (PATCH, COLS), 0)
    dst = lax.broadcasted_iota(jnp.int32, (PATCH, COLS), 1)
    keep = jnp.where(src == dst + (col0 - meta[1, mine]), 1.0, 0.0).astype(bf16)
    for m in range(NM):
        for plane in range(2):
            moved_probe = dot(probes[m][plane], keep).astype(bf16)
            side[m // 2, plane, :, pl.ds(m % 2 * COLS, COLS)] = moved_probe
    k_re = dot(table[0], keep).astype(bf16)
    k_im = dot(table[1], keep).astype(bf16)
    turn[...] = jnp.concatenate(
        [jnp.concatenate([k_re, -k_im], axis=1), jnp.concatenate([k_im, k_re], axis=1)], axis=0
    )
    total = jnp.zeros((PATCH, PATCH), f32)
    for probe in probes:
        p_re = probe[0].astype(f32)
        p_im = probe[1].astype(f32)
        total = total + p_re * p_re + p_im * p_im
    padded[...] = jnp.zeros(padded.shape, f32)
    for half in range(PATCH // COLS):
        padded[1 + half, pl.ds(ROWS, PATCH)] = total[:, half * COLS : (half + 1) * COLS]
    out[...] = jnp.zeros(out.shape, f32)

    def add(k, carry):
        down = row0 - meta[0, k] + ROWS
        over = col0 - meta[1, k] + COLS
        hit = (down > 0) & (down < PATCH + ROWS) & (over > 0) & (over < PATCH + COLS)

        @pl.when(hit)
        def _():
            rows = jnp.concatenate([padded[q, pl.ds(down, ROWS)] for q in range(4)], axis=1)
            moved = pltpu.roll(rows, PATCH + 2 * COLS - over, 1)
            out[...] = out[...] + moved[:, :COLS]

        return carry

    lax.fori_loop(0, meta.shape[1], add, 0)


def dft_table():
    grid = np.arange(PATCH)[:, None] * np.arange(PATCH)[None, :] % PATCH
    angle = 2.0 * np.pi / PATCH * grid
    factor = 1.0 / math.sqrt(PATCH)
    table = np.stack([np.cos(angle) * factor, -np.sin(angle) * factor])
    return jnp.asarray(table.astype(np.float32)).astype(bf16)


CY, CX = (ROWS + 2 * HALO) // 2, (COLS + 2 * HALO) // 2
FLAT = CY * 128
CHUNK = 256
PHASES = ((0, 0), (0, 1), (1, 0), (1, 1))
SHIFTS = tuple((dy, dx) for dy in (-1, 0, 1) for dx in (-1, 0, 1))


def split_tables():
    first = np.zeros((9, 2, 4, 72), np.float32)
    last = np.zeros((9, 36, 4), np.float32)
    for tap in range(9):
        for ij, (i, j) in enumerate(PHASES):
            r, c = i + tap // 3 - 1, j + tap % 3 - 1
            p, q, dy, dx = r & 1, c & 1, r >> 1, c >> 1
            s = (dy + 1) * 3 + dx + 1
            for ch in range(2):
                first[tap, ch, ij, s * 8 + q * 4 + ch * 2 + p] = 1
            last[tap, s * 4 + ij, p * 2 + q] = 1
    return jnp.asarray(first).astype(bf16), jnp.asarray(last).astype(bf16)


def moved(value, dy, dx):
    if dx:
        value = pltpu.roll(value, (-dx) % FLAT, 1)
    if dy == 1:
        value = jnp.concatenate([value[:, 128:], value[:, :128]], axis=1)
    if dy == -1:
        value = jnp.concatenate([value[:, FLAT - 128 :], value[:, : FLAT - 128]], axis=1)
    return value


def denoise_kernel(
    meta,
    b_out,
    ext,
    first_w,
    down_w,
    mid_w,
    last_w,
    biases,
    out,
    halves,
    planes,
    taps1,
    maps,
    coarse,
    taps2,
    fourth,
    parts,
    inter,
):
    x, z, core, mode = ids(meta)
    chans = coarse.shape[0]
    height = ROWS + 2 * HALO
    width = COLS + 2 * HALO
    src = lax.broadcasted_iota(jnp.int32, (width, 256), 0)
    dst = lax.broadcasted_iota(jnp.int32, (width, 256), 1)
    lane = dst & 127
    even_odd = jnp.where((src == 2 * lane + (dst >> 7)) & (lane < CX), 1.0, 0.0).astype(bf16)
    for ch in range(2):
        row = dot(ext[ch], even_odd)
        for q in range(2):
            halves[q, pl.ds(ch * height, height)] = row[:, q * 128 : (q + 1) * 128]
    for y in range(CY):
        pieces = [
            halves[q, pl.ds(ch * height + 2 * y, 2)] for q in range(2) for ch in range(2)
        ]
        planes[:, pl.ds(y * 128, 128)] = jnp.concatenate(pieces, axis=0)
    full = planes[...]
    taps1[...] = jnp.concatenate([moved(full, dy, dx) for dy, dx in SHIFTS], axis=0).astype(bf16)

    row0 = (x * (NZ * NC) + z * NC + core) * ROWS - HALO
    col0 = mode * COLS - HALO
    height_all, width_all = NX * NZ * NC * ROWS, NM * COLS

    def masks(start):
        spot = lax.broadcasted_iota(jnp.int32, (1, CHUNK), 1) + start
        rows = row0 + 2 * (spot >> 7)
        cols = col0 + 2 * (spot & 127)
        found = []
        for p, q in PHASES:
            inside = (rows + p >= 0) & (rows + p < height_all)
            inside = inside & (cols + q >= 0) & (cols + q < width_all)
            found.append(jnp.where(inside, 1.0, 0.0))
        return found

    for start in range(0, FLAT, CHUNK):
        span = pl.ds(start, CHUNK)
        found = masks(start)
        value = dot(first_w[...], taps1[:, span])
        for n in range(4):
            part = value[n * chans : (n + 1) * chans] + biases[:, 0:1]
            maps[pl.ds(n * chans, chans), span] = (jnp.maximum(part, 0.0) * found[n]).astype(bf16)
        value = dot(down_w[...], maps[:, span]) + biases[:, 1:2]
        coarse[:, span] = (jnp.maximum(value, 0.0) * found[0]).astype(bf16).astype(f32)
    for s, (dy, dx) in enumerate(SHIFTS):
        taps2[pl.ds(s * chans, chans)] = moved(coarse[...], dy, dx).astype(bf16)
    for start in range(0, FLAT, CHUNK):
        span = pl.ds(start, CHUNK)
        found = masks(start)
        value = dot(mid_w[...], taps2[:, span]) + biases[:, 2:3]
        third = jnp.maximum(value, 0.0).astype(bf16).astype(f32)
        for n in range(4):
            rows = pl.ds(n * chans, chans)
            fourth[rows, span] = (third * found[n] + maps[rows, span].astype(f32)).astype(bf16)
        parts[:, span] = dot(last_w[...], fourth[:, span])
    total = moved(parts[pl.ds(0, 8)], *SHIFTS[0])
    for s in range(1, 9):
        total = total + moved(parts[pl.ds(s * 8, 8)], *SHIFTS[s])
    planes[...] = total
    for y in range(HALO // 2, HALO // 2 + ROWS // 2):
        tile = planes[:, pl.ds(y * 128, 128)]
        for i, j in PHASES:
            for ch in range(2):
                n = (i * 2 + j) * 2 + ch
                inter[j, pl.ds(ch * ROWS + 2 * y - HALO + i, 1)] = tile[n : n + 1]
    e_src = lax.broadcasted_iota(jnp.int32, (256, COLS), 0)
    e_dst = lax.broadcasted_iota(jnp.int32, (256, COLS), 1)
    weave = jnp.where(2 * (e_src & 127) - HALO + (e_src >> 7) == e_dst, 1.0, 0.0).astype(bf16)
    wide = jnp.concatenate([inter[0], inter[1]], axis=1)
    high = wide.astype(bf16)
    low = (wide - high.astype(f32)).astype(bf16)
    woven = dot(high, weave) + dot(low, weave)
    for ch in range(2):
        out[ch] = woven[ch * ROWS : (ch + 1) * ROWS] + b_out[ch]


def denoise(base, meta, w_in, b_in, w_down, b_down, w_mid, b_mid, w_out, b_out):
    chans = w_in.shape[1]
    extended = extended_2(base.astype(bf16), ((TILE_AXES, 1), (("mode",), 2)), HALO)
    first, last = split_tables()
    first_w = jnp.einsum("toc,tcik->iok", w_in, first).reshape(4 * chans, 72)
    last_w = jnp.einsum("tcd,tmp->mcpd", w_out, last).reshape(72, 4 * chans)
    down_w = jnp.transpose(w_down, (1, 0, 2)).reshape(chans, 4 * chans)
    mid_w = jnp.transpose(w_mid, (1, 0, 2)).reshape(chans, 9 * chans)
    return pl.pallas_call(
        denoise_kernel,
        out_shape=jax.ShapeDtypeStruct((2, ROWS, COLS), f32),
        in_specs=[smem_spec(), smem_spec()] + [vmem_spec()] * 6,
        out_specs=vmem_spec(),
        scratch_shapes=[
            pltpu.VMEM((2, 2 * (ROWS + 2 * HALO), 128), f32),
            pltpu.VMEM((8, FLAT), f32),
            pltpu.VMEM((72, FLAT), bf16),
            pltpu.VMEM((4 * chans, FLAT), bf16),
            pltpu.VMEM((chans, FLAT), f32),
            pltpu.VMEM((9 * chans, FLAT), bf16),
            pltpu.VMEM((4 * chans, FLAT), bf16),
            pltpu.VMEM((72, FLAT), f32),
            pltpu.VMEM((2, 2 * ROWS, 128), f32),
        ],
        cost_estimate=pl.CostEstimate(
            flops=4 * 10**9, bytes_accessed=2 * 10**7, transcendentals=0
        ),
        compiler_params=pltpu.CompilerParams(vmem_limit_bytes=24 * 2**20),
        name="denoise",
    )(
        meta,
        b_out,
        extended,
        first_w,
        down_w,
        mid_w,
        last_w,
        jnp.stack([b_in, b_down, b_mid], axis=1),
    )


def per_device(
    obj_x,
    dual_u,
    probes,
    intensity,
    corners,
    owner,
    w_in,
    b_in,
    w_down,
    b_down,
    w_mid,
    b_mid,
    w_out,
    b_out,
):
    x = lax.axis_index("x")
    z = lax.axis_index("z")
    core = lax.axis_index("core")
    mode = lax.axis_index("mode")
    tiles = NX * NZ * NC
    lanes = jnp.arange(tiles, dtype=jnp.int32)
    owned = owner[None, :] == lanes[:, None]
    by_owner = jnp.sum(jnp.where(owned[None], corners[:, None, :], 0), axis=2)
    place = jnp.where(lanes == 0, x, jnp.where(lanes == 1, z, jnp.where(lanes == 2, core, mode)))
    meta = jnp.concatenate([by_owner, place[None]], axis=0).astype(jnp.int32)

    rows = jnp.broadcast_to(obj_x.reshape(1, 2 * ROWS, COLS), (NZ, 2 * ROWS, COLS))
    spread = rows.astype(bf16)
    near = lax.all_to_all(spread, "z", 0, 0, tiled=True)
    probe0 = probes[0].astype(bf16)
    others = [
        lax.ppermute(probe0, "mode", [(i, (i + k) % NM) for i in range(NM)])
        for k in range(1, NM)
    ]
    all_probes = (probe0, *others)
    table = dft_table()
    denom, side, turn = pl.pallas_call(
        weight_kernel,
        out_shape=(
            jax.ShapeDtypeStruct((ROWS, COLS), f32),
            pltpu.VMEM((NM // 2, 2, PATCH, 2 * COLS), bf16),
            pltpu.VMEM((2 * PATCH, 2 * COLS), bf16),
        ),
        in_specs=[smem_spec()] + [vmem_spec()] * (NM + 1),
        out_specs=(vmem_spec(),) * 3,
        scratch_shapes=[pltpu.VMEM((PATCH // COLS + 2, PATCH + 2 * ROWS, COLS), f32)],
        compiler_params=pltpu.CompilerParams(vmem_limit_bytes=12 * 2**20),
        name="weight",
    )(meta, *near_core(*all_probes), table)
    packed = pl.pallas_call(
        pack_kernel,
        out_shape=jax.ShapeDtypeStruct((NX * NC, HALF, 2 * ROWS, COLS), bf16),
        in_specs=[smem_spec(), vmem_spec()],
        out_specs=any_spec(),
        scratch_shapes=[
            pltpu.VMEM((NX * NC, HALF, 2 * ROWS, COLS), bf16),
            pltpu.SemaphoreType.DMA((NX * NC,)),
        ],
        compiler_params=pltpu.CompilerParams(vmem_limit_bytes=8 * 2**20),
        name="pack",
    )(meta, *near_core(near))
    got = lax.all_to_all(packed, ("x", "core"), 0, 0, tiled=True)
    window = pl.pallas_call(
        window_kernel,
        out_shape=jax.ShapeDtypeStruct((NM, 2, PATCH, COLS), bf16),
        in_specs=[smem_spec(), vmem_spec()],
        out_specs=any_spec(),
        scratch_shapes=[
            pltpu.VMEM((2, STRIPS * ROWS, COLS), f32),
            pltpu.VMEM((2, PATCH, COLS), bf16),
            pltpu.SemaphoreType.DMA((NM,)),
        ],
        compiler_params=pltpu.CompilerParams(vmem_limit_bytes=8 * 2**20),
        name="window",
    )(meta, *near_core(got))
    wins = lax.all_to_all(window, "mode", 0, 0, tiled=True)
    updates, misfit = pl.pallas_call(
        wave_kernel,
        out_shape=(
            jax.ShapeDtypeStruct((NX * NC, HALF, 2 * ROWS, COLS), bf16),
            jax.ShapeDtypeStruct((1, 1), f32),
        ),
        in_specs=[smem_spec()] + [vmem_spec()] * 9,
        out_specs=(vmem_spec(), vmem_spec()),
        scratch_shapes=[
            pltpu.VMEM((NM, PATCH, 2 * PATCH), f32),
            pltpu.VMEM((2, STRIPS * ROWS, COLS), f32),
        ],
        compiler_params=pltpu.CompilerParams(vmem_limit_bytes=24 * 2**20),
        name="wave",
    )(meta, *near_core(wins, *all_probes, side, turn, intensity, table))
    back = lax.all_to_all(updates, ("x", "core"), 0, 0, tiled=True)
    partial = pl.pallas_call(
        gather_kernel,
        out_shape=jax.ShapeDtypeStruct((NZ, 2 * ROWS, COLS), bf16),
        in_specs=[smem_spec(), vmem_spec()],
        out_specs=vmem_spec(),
        scratch_shapes=[pltpu.VMEM((NZ, 2 * ROWS, COLS), f32)],
        compiler_params=pltpu.CompilerParams(vmem_limit_bytes=8 * 2**20),
        name="gather",
    )(meta, *near_core(back))
    pieces = lax.all_to_all(partial, "z", 0, 0, tiled=True)
    obj_later = lax.optimization_barrier(obj_x)
    base = obj_later + dual_u
    center = denoise(base, meta, w_in, b_in, w_down, b_down, w_mid, b_mid, w_out, b_out)
    aux_next = base - center
    numer = jnp.sum(pieces.astype(f32), axis=0).reshape(2, ROWS, COLS)
    obj_next = (numer + rho_weight * (aux_next - dual_u)) / (denom + rho_weight)
    dual_next = dual_u + obj_next - aux_next
    return (obj_next, aux_next, dual_next, misfit.reshape(1))


def solution(mesh):
    split = Mesh(mesh.devices.reshape(NX, NZ, NC, NM), TILE_AXES + ("mode",))
    grid = P(None, TILE_AXES, "mode")
    return jax.shard_map(
        per_device,
        mesh=split,
        in_specs=(
            grid,
            grid,
            P("mode", None, None, None),
            P(TILE_AXES, None, None),
        )
        + (P(),) * 10,
        out_specs=(grid, grid, grid, P(TILE_AXES)),
        check_vma=False,
    )
```

```python
import math

import jax
import jax.numpy as jnp
import numpy as np
from jax import lax
from jax.experimental import pallas as pl
from jax.experimental.pallas import tpu as pltpu
from jax.sharding import Mesh, PartitionSpec as P

HALO = 6
NX, NZ, NC, NM = 4, 16, 2, 4
PATCH = 256
ROWS = 32
COLS = 128
STRIPS = PATCH // ROWS + 1
HALF = PATCH // ROWS // 2

rho_weight = 2.0
floor_level = 0.25
f32 = jnp.float32
bf16 = jnp.bfloat16
TILE_AXES = ("x", "z", "core")


def shifted(value, axes, step):
    count = math.prod(lax.axis_size(a) for a in axes)
    pairs = [(i, i + step) for i in range(count) if 0 <= i + step < count]
    return lax.ppermute(value, axes, pairs)


def extended_2(value, sides, width):
    for axes, dim in sides:
        length = value.shape[dim]
        last = lax.slice_in_dim(value, length - width, length, axis=dim)
        first = lax.slice_in_dim(value, 0, width, axis=dim)
        before = shifted(last, axes, 1)
        after = shifted(first, axes, -1)
        value = jnp.concatenate([before, value, after], axis=dim)
    return value


def vmem_spec():
    return pl.BlockSpec(memory_space=pltpu.VMEM)


def near_core(*arrays):
    return [pltpu.with_memory_space_constraint(a, pltpu.VMEM) for a in arrays]


def any_spec():
    return pl.BlockSpec(memory_space=pl.ANY)


def smem_spec():
    return pl.BlockSpec(memory_space=pltpu.SMEM)


def ids(meta):
    return meta[2, 0], meta[2, 1], meta[2, 2], meta[2, 3]


def first_strip(s0, core):
    return s0 + ((s0 + core) & 1)


def copy_out(held, out, sems, count, same):
    copies = [
        pltpu.make_async_copy(held if same else held.at[n], out.at[n], sems.at[n])
        for n in range(count)
    ]
    for copy in copies:
        copy.start()
    return copies


def row_in_strip():
    return lax.broadcasted_iota(jnp.int32, (2 * ROWS, COLS), 0) & (ROWS - 1)


def z_slot(strip):
    return (strip % (NZ * NC)) // NC


def strips_of(row, core):
    s0 = row // ROWS
    begin = first_strip(s0, core)
    return begin, jnp.where(begin == s0, row - s0 * ROWS, 0)


def pack_kernel(meta, near, out, held, sems):
    _, z, core, _ = ids(meta)
    rows = row_in_strip()
    copies = []
    for target in range(NX * NC):
        tx, tc = target // NC, target % NC
        begin, cut = strips_of(meta[0, tx * (NZ * NC) + z * NC + tc], core)
        late = near[z_slot(begin + 2 * HALF)].astype(f32)
        early = near[z_slot(begin)].astype(f32)
        held[target, 0] = jnp.where(rows < cut, late, early).astype(bf16)
        for j in range(1, HALF):
            held[target, j] = near[z_slot(begin + 2 * j)]
        copy = pltpu.make_async_copy(held.at[target], out.at[target], sems.at[target])
        copy.start()
        copies.append(copy)
    for copy in copies:
        copy.wait()


def window_kernel(meta, got, out, tall, held, sems):
    x, z, core, _ = ids(meta)
    row = meta[0, x * (NZ * NC) + z * NC + core]
    s0 = row // ROWS
    for i in range(STRIPS):
        strip = s0 + i
        source = jnp.minimum(strip // (NZ * NC), NX - 1) * NC + (strip & 1)
        block = got[source, (i // 2) % HALF].astype(f32)
        tall[0, pl.ds(i * ROWS, ROWS)] = block[:ROWS]
        tall[1, pl.ds(i * ROWS, ROWS)] = block[ROWS:]
    offset = row - s0 * ROWS
    for plane in range(2):
        held[plane] = tall[plane, pl.ds(offset, PATCH)].astype(bf16)
    for copy in copy_out(held, out, sems, NM, True):
        copy.wait()


def dot(a, b):
    return jnp.dot(a, b, preferred_element_type=f32)


def wave_kernel(
    meta, wins, probe0, probe1, probe2, probe3, side, turn, take, intensity, table, out, err, far_all, tall
):
    x, z, core, _ = ids(meta)
    mine = x * (NZ * NC) + z * NC + core
    row = meta[0, mine]
    s0 = row // ROWS
    offset = row - s0 * ROWS
    t_re = table[0]
    t_im = table[1]
    t_neg = -t_im
    left = jnp.concatenate(
        [jnp.concatenate([t_re, t_neg], axis=1), jnp.concatenate([t_im, t_re], axis=1)], axis=0
    )
    right = jnp.concatenate(
        [jnp.concatenate([t_re, t_im], axis=1), jnp.concatenate([t_neg, t_re], axis=1)], axis=0
    )
    full = jnp.concatenate(
        [jnp.concatenate([wins[m, p] for m in range(NM)], axis=1) for p in range(2)], axis=0
    )
    patch = dot(full, take[...])
    obj_re = patch[:PATCH]
    obj_im = patch[PATCH:]
    probes = (probe0, probe1, probe2, probe3)
    power = jnp.zeros((PATCH, PATCH), f32)
    for m in range(NM):
        p_re = probes[m][0].astype(f32)
        p_im = probes[m][1].astype(f32)
        wave = jnp.concatenate(
            [(p_re * obj_re - p_im * obj_im).astype(bf16), (p_re * obj_im + p_im * obj_re).astype(bf16)],
            axis=0,
        )
        half = dot(left, wave).astype(bf16)
        far = dot(jnp.concatenate([half[:PATCH], half[PATCH:]], axis=1), right)
        far_all[m] = far
        power = power + far[:, :PATCH] * far[:, :PATCH] + far[:, PATCH:] * far[:, PATCH:]
    measured = jnp.sqrt(intensity[0])
    gap = jnp.sqrt(power) - measured
    err[...] = jnp.sum(gap * gap, keepdims=True) * (1.0 / (PATCH * PATCH))
    scale = measured / jnp.sqrt(jnp.maximum(power, floor_level))
    sums = [jnp.zeros((PATCH, 2 * COLS), f32) for _ in range(2)]
    for pair in range(NM // 2):
        halves = []
        for m in (2 * pair, 2 * pair + 1):
            far = far_all[m]
            scaled = jnp.concatenate(
                [(far[:, :PATCH] * scale).astype(bf16), (far[:, PATCH:] * scale).astype(bf16)],
                axis=1,
            )
            halves.append(dot(scaled, turn[...]).astype(bf16))
        stacked = [
            jnp.concatenate([h[:, p * COLS : (p + 1) * COLS] for h in halves], axis=1)
            for p in range(2)
        ]
        back = dot(right, jnp.concatenate(stacked, axis=0))
        back_re = back[:PATCH]
        back_im = back[PATCH:]
        q_re = side[pair, 0].astype(f32)
        q_im = side[pair, 1].astype(f32)
        sums[0] = sums[0] + (q_re * back_re + q_im * back_im)
        sums[1] = sums[1] + (q_re * back_im - q_im * back_re)
    sum_re, sum_im = [v[:, :COLS] + v[:, COLS:] for v in sums]
    tall[...] = jnp.zeros(tall.shape, f32)
    tall[0, pl.ds(offset, PATCH)] = sum_re
    tall[1, pl.ds(offset, PATCH)] = sum_im
    out[...] = jnp.zeros(out.shape, bf16)
    for i in range(STRIPS):
        strip = s0 + i
        target = jnp.minimum(strip // (NZ * NC), NX - 1) * NC + (strip & 1)
        piece = jnp.concatenate([tall[p, pl.ds(i * ROWS, ROWS)] for p in range(2)], axis=0)
        if i < 2 * HALF:
            out[target, i // 2] = piece.astype(bf16)
        else:
            out[target, 0] = (out[target, 0].astype(f32) + piece).astype(bf16)


def gather_kernel(meta, got, out, acc):
    _, z, core, _ = ids(meta)
    rows = row_in_strip()
    acc[...] = jnp.zeros(acc.shape, f32)
    for source in range(NX * NC):
        sx, sc = source // NC, source % NC
        begin, cut = strips_of(meta[0, sx * (NZ * NC) + z * NC + sc], core)
        both = got[source, 0].astype(f32)
        late, early = z_slot(begin + 2 * HALF), z_slot(begin)
        acc[late] = acc[late] + jnp.where(rows < cut, both, 0.0)
        acc[early] = acc[early] + jnp.where(rows < cut, 0.0, both)
        for j in range(1, HALF):
            slot = z_slot(begin + 2 * j)
            acc[slot] = acc[slot] + got[source, j].astype(f32)
    out[...] = acc[...].astype(bf16)


def weight_kernel(meta, probe0, probe1, probe2, probe3, table, out, side, turn, take, padded):
    x, z, core, mode = ids(meta)
    row0 = (x * (NZ * NC) + z * NC + core) * ROWS
    col0 = mode * COLS
    probes = (probe0, probe1, probe2, probe3)
    mine = x * (NZ * NC) + z * NC + core
    src = lax.broadcasted_iota(jnp.int32, (NM * COLS, PATCH), 0)
    dst = lax.broadcasted_iota(jnp.int32, (NM * COLS, PATCH), 1)
    take[...] = jnp.where(src == dst + meta[1, mine], 1.0, 0.0).astype(bf16)
    src = lax.broadcasted_iota(jnp.int32, (PATCH, COLS), 0)
    dst = lax.broadcasted_iota(jnp.int32, (PATCH, COLS), 1)
    keep = jnp.where(src == dst + (col0 - meta[1, mine]), 1.0, 0.0).astype(bf16)
    for m in range(NM):
        for plane in range(2):
            moved_probe = dot(probes[m][plane], keep).astype(bf16)
            side[m // 2, plane, :, pl.ds(m % 2 * COLS, COLS)] = moved_probe
    k_re = dot(table[0], keep).astype(bf16)
    k_im = dot(table[1], keep).astype(bf16)
    turn[...] = jnp.concatenate(
        [jnp.concatenate([k_re, -k_im], axis=1), jnp.concatenate([k_im, k_re], axis=1)], axis=0
    )
    total = jnp.zeros((PATCH, PATCH), f32)
    for probe in probes:
        p_re = probe[0].astype(f32)
        p_im = probe[1].astype(f32)
        total = total + p_re * p_re + p_im * p_im
    padded[...] = jnp.zeros(padded.shape, f32)
    for half in range(PATCH // COLS):
        padded[1 + half, pl.ds(ROWS, PATCH)] = total[:, half * COLS : (half + 1) * COLS]
    out[...] = jnp.zeros(out.shape, f32)

    def add(k, carry):
        down = row0 - meta[0, k] + ROWS
        over = col0 - meta[1, k] + COLS
        hit = (down > 0) & (down < PATCH + ROWS) & (over > 0) & (over < PATCH + COLS)

        @pl.when(hit)
        def _():
            rows = jnp.concatenate([padded[q, pl.ds(down, ROWS)] for q in range(4)], axis=1)
            moved = pltpu.roll(rows, PATCH + 2 * COLS - over, 1)
            out[...] = out[...] + moved[:, :COLS]

        return carry

    lax.fori_loop(0, meta.shape[1], add, 0)


def dft_table():
    grid = np.arange(PATCH)[:, None] * np.arange(PATCH)[None, :] % PATCH
    angle = 2.0 * np.pi / PATCH * grid
    factor = 1.0 / math.sqrt(PATCH)
    table = np.stack([np.cos(angle) * factor, -np.sin(angle) * factor])
    return jnp.asarray(table.astype(np.float32)).astype(bf16)


CY, CX = (ROWS + 2 * HALO) // 2, (COLS + 2 * HALO) // 2
FLAT = CY * 128
CHUNK = 256
PHASES = ((0, 0), (0, 1), (1, 0), (1, 1))
SHIFTS = tuple((dy, dx) for dy in (-1, 0, 1) for dx in (-1, 0, 1))


def split_tables():
    first = np.zeros((9, 2, 4, 72), np.float32)
    last = np.zeros((9, 36, 4), np.float32)
    for tap in range(9):
        for ij, (i, j) in enumerate(PHASES):
            r, c = i + tap // 3 - 1, j + tap % 3 - 1
            p, q, dy, dx = r & 1, c & 1, r >> 1, c >> 1
            s = (dy + 1) * 3 + dx + 1
            for ch in range(2):
                first[tap, ch, ij, s * 8 + q * 4 + ch * 2 + p] = 1
            last[tap, s * 4 + ij, p * 2 + q] = 1
    return jnp.asarray(first).astype(bf16), jnp.asarray(last).astype(bf16)


def moved(value, dy, dx):
    if dx:
        value = pltpu.roll(value, (-dx) % FLAT, 1)
    if dy == 1:
        value = jnp.concatenate([value[:, 128:], value[:, :128]], axis=1)
    if dy == -1:
        value = jnp.concatenate([value[:, FLAT - 128 :], value[:, : FLAT - 128]], axis=1)
    return value


def denoise_kernel(
    meta,
    b_out,
    ext,
    first_w,
    down_w,
    mid_w,
    last_w,
    biases,
    out,
    halves,
    planes,
    taps1,
    maps,
    coarse,
    taps2,
    fourth,
    parts,
    inter,
):
    x, z, core, mode = ids(meta)
    chans = coarse.shape[0]
    height = ROWS + 2 * HALO
    width = COLS + 2 * HALO
    src = lax.broadcasted_iota(jnp.int32, (width, 256), 0)
    dst = lax.broadcasted_iota(jnp.int32, (width, 256), 1)
    lane = dst & 127
    even_odd = jnp.where((src == 2 * lane + (dst >> 7)) & (lane < CX), 1.0, 0.0).astype(bf16)
    for ch in range(2):
        row = dot(ext[ch], even_odd)
        for q in range(2):
            halves[q, pl.ds(ch * height, height)] = row[:, q * 128 : (q + 1) * 128]
    for y in range(CY):
        pieces = [
            halves[q, pl.ds(ch * height + 2 * y, 2)] for q in range(2) for ch in range(2)
        ]
        planes[:, pl.ds(y * 128, 128)] = jnp.concatenate(pieces, axis=0)
    full = planes[...]
    taps1[...] = jnp.concatenate([moved(full, dy, dx) for dy, dx in SHIFTS], axis=0).astype(bf16)

    row0 = (x * (NZ * NC) + z * NC + core) * ROWS - HALO
    col0 = mode * COLS - HALO
    height_all, width_all = NX * NZ * NC * ROWS, NM * COLS

    def masks(start):
        spot = lax.broadcasted_iota(jnp.int32, (1, CHUNK), 1) + start
        rows = row0 + 2 * (spot >> 7)
        cols = col0 + 2 * (spot & 127)
        found = []
        for p, q in PHASES:
            inside = (rows + p >= 0) & (rows + p < height_all)
            inside = inside & (cols + q >= 0) & (cols + q < width_all)
            found.append(jnp.where(inside, 1.0, 0.0))
        return found

    for start in range(0, FLAT, CHUNK):
        span = pl.ds(start, CHUNK)
        found = masks(start)
        value = dot(first_w[...], taps1[:, span])
        for n in range(4):
            part = value[n * chans : (n + 1) * chans] + biases[:, 0:1]
            maps[pl.ds(n * chans, chans), span] = (jnp.maximum(part, 0.0) * found[n]).astype(bf16)
        value = dot(down_w[...], maps[:, span]) + biases[:, 1:2]
        coarse[:, span] = (jnp.maximum(value, 0.0) * found[0]).astype(bf16).astype(f32)
    for s, (dy, dx) in enumerate(SHIFTS):
        taps2[pl.ds(s * chans, chans)] = moved(coarse[...], dy, dx).astype(bf16)
    for start in range(0, FLAT, CHUNK):
        span = pl.ds(start, CHUNK)
        found = masks(start)
        value = dot(mid_w[...], taps2[:, span]) + biases[:, 2:3]
        third = jnp.maximum(value, 0.0).astype(bf16).astype(f32)
        for n in range(4):
            rows = pl.ds(n * chans, chans)
            fourth[rows, span] = (third * found[n] + maps[rows, span].astype(f32)).astype(bf16)
        parts[:, span] = dot(last_w[...], fourth[:, span])
    total = moved(parts[pl.ds(0, 8)], *SHIFTS[0])
    for s in range(1, 9):
        total = total + moved(parts[pl.ds(s * 8, 8)], *SHIFTS[s])
    planes[...] = total
    for y in range(HALO // 2, HALO // 2 + ROWS // 2):
        tile = planes[:, pl.ds(y * 128, 128)]
        for i, j in PHASES:
            for ch in range(2):
                n = (i * 2 + j) * 2 + ch
                inter[j, pl.ds(ch * ROWS + 2 * y - HALO + i, 1)] = tile[n : n + 1]
    e_src = lax.broadcasted_iota(jnp.int32, (256, COLS), 0)
    e_dst = lax.broadcasted_iota(jnp.int32, (256, COLS), 1)
    weave = jnp.where(2 * (e_src & 127) - HALO + (e_src >> 7) == e_dst, 1.0, 0.0).astype(bf16)
    wide = jnp.concatenate([inter[0], inter[1]], axis=1)
    high = wide.astype(bf16)
    low = (wide - high.astype(f32)).astype(bf16)
    woven = dot(high, weave) + dot(low, weave)
    for ch in range(2):
        out[ch] = woven[ch * ROWS : (ch + 1) * ROWS] + b_out[ch]


def denoise(base, meta, w_in, b_in, w_down, b_down, w_mid, b_mid, w_out, b_out):
    chans = w_in.shape[1]
    extended = extended_2(base.astype(bf16), ((TILE_AXES, 1), (("mode",), 2)), HALO)
    first, last = split_tables()
    first_w = jnp.einsum("toc,tcik->iok", w_in, first).reshape(4 * chans, 72)
    last_w = jnp.einsum("tcd,tmp->mcpd", w_out, last).reshape(72, 4 * chans)
    down_w = jnp.transpose(w_down, (1, 0, 2)).reshape(chans, 4 * chans)
    mid_w = jnp.transpose(w_mid, (1, 0, 2)).reshape(chans, 9 * chans)
    return pl.pallas_call(
        denoise_kernel,
        out_shape=jax.ShapeDtypeStruct((2, ROWS, COLS), f32),
        in_specs=[smem_spec(), smem_spec()] + [vmem_spec()] * 6,
        out_specs=vmem_spec(),
        scratch_shapes=[
            pltpu.VMEM((2, 2 * (ROWS + 2 * HALO), 128), f32),
            pltpu.VMEM((8, FLAT), f32),
            pltpu.VMEM((72, FLAT), bf16),
            pltpu.VMEM((4 * chans, FLAT), bf16),
            pltpu.VMEM((chans, FLAT), f32),
            pltpu.VMEM((9 * chans, FLAT), bf16),
            pltpu.VMEM((4 * chans, FLAT), bf16),
            pltpu.VMEM((72, FLAT), f32),
            pltpu.VMEM((2, 2 * ROWS, 128), f32),
        ],
        cost_estimate=pl.CostEstimate(
            flops=4 * 10**9, bytes_accessed=2 * 10**7, transcendentals=0
        ),
        compiler_params=pltpu.CompilerParams(vmem_limit_bytes=24 * 2**20),
        name="denoise",
    )(
        meta,
        b_out,
        extended,
        first_w,
        down_w,
        mid_w,
        last_w,
        jnp.stack([b_in, b_down, b_mid], axis=1),
    )


def per_device(
    obj_x,
    dual_u,
    probes,
    intensity,
    corners,
    owner,
    w_in,
    b_in,
    w_down,
    b_down,
    w_mid,
    b_mid,
    w_out,
    b_out,
):
    x = lax.axis_index("x")
    z = lax.axis_index("z")
    core = lax.axis_index("core")
    mode = lax.axis_index("mode")
    tiles = NX * NZ * NC
    lanes = jnp.arange(tiles, dtype=jnp.int32)
    owned = owner[None, :] == lanes[:, None]
    by_owner = jnp.sum(jnp.where(owned[None], corners[:, None, :], 0), axis=2)
    place = jnp.where(lanes == 0, x, jnp.where(lanes == 1, z, jnp.where(lanes == 2, core, mode)))
    meta = jnp.concatenate([by_owner, place[None]], axis=0).astype(jnp.int32)

    rows = jnp.broadcast_to(obj_x.reshape(1, 2 * ROWS, COLS), (NZ, 2 * ROWS, COLS))
    slots = lax.broadcasted_iota(jnp.int32, rows.shape, 0)
    spread = jnp.where(slots + z >= 0, rows, 0.0).astype(bf16)
    near = lax.all_to_all(spread, "z", 0, 0, tiled=True)
    probe0 = probes[0].astype(bf16)
    others = [
        lax.ppermute(probe0, "mode", [(i, (i + k) % NM) for i in range(NM)])
        for k in range(1, NM)
    ]
    all_probes = (probe0, *others)
    table = dft_table()
    denom, side, turn, take = pl.pallas_call(
        weight_kernel,
        out_shape=(
            jax.ShapeDtypeStruct((ROWS, COLS), f32),
            pltpu.VMEM((NM // 2, 2, PATCH, 2 * COLS), bf16),
            pltpu.VMEM((2 * PATCH, 2 * COLS), bf16),
            pltpu.VMEM((NM * COLS, PATCH), bf16),
        ),
        in_specs=[smem_spec()] + [vmem_spec()] * (NM + 1),
        out_specs=(vmem_spec(),) * 4,
        scratch_shapes=[pltpu.VMEM((PATCH // COLS + 2, PATCH + 2 * ROWS, COLS), f32)],
        compiler_params=pltpu.CompilerParams(vmem_limit_bytes=12 * 2**20),
        name="weight",
    )(meta, *near_core(*all_probes), table)
    packed = pl.pallas_call(
        pack_kernel,
        out_shape=jax.ShapeDtypeStruct((NX * NC, HALF, 2 * ROWS, COLS), bf16),
        in_specs=[smem_spec(), vmem_spec()],
        out_specs=any_spec(),
        scratch_shapes=[
            pltpu.VMEM((NX * NC, HALF, 2 * ROWS, COLS), bf16),
            pltpu.SemaphoreType.DMA((NX * NC,)),
        ],
        compiler_params=pltpu.CompilerParams(vmem_limit_bytes=8 * 2**20),
        name="pack",
    )(meta, *near_core(near))
    got = lax.all_to_all(packed, ("x", "core"), 0, 0, tiled=True)
    window = pl.pallas_call(
        window_kernel,
        out_shape=jax.ShapeDtypeStruct((NM, 2, PATCH, COLS), bf16),
        in_specs=[smem_spec(), vmem_spec()],
        out_specs=any_spec(),
        scratch_shapes=[
            pltpu.VMEM((2, STRIPS * ROWS, COLS), f32),
            pltpu.VMEM((2, PATCH, COLS), bf16),
            pltpu.SemaphoreType.DMA((NM,)),
        ],
        compiler_params=pltpu.CompilerParams(vmem_limit_bytes=8 * 2**20),
        name="window",
    )(meta, *near_core(got))
    wins = lax.all_to_all(window, "mode", 0, 0, tiled=True)
    updates, misfit = pl.pallas_call(
        wave_kernel,
        out_shape=(
            jax.ShapeDtypeStruct((NX * NC, HALF, 2 * ROWS, COLS), bf16),
            jax.ShapeDtypeStruct((1, 1), f32),
        ),
        in_specs=[smem_spec()] + [vmem_spec()] * 10,
        out_specs=(vmem_spec(), vmem_spec()),
        scratch_shapes=[
            pltpu.VMEM((NM, PATCH, 2 * PATCH), f32),
            pltpu.VMEM((2, STRIPS * ROWS, COLS), f32),
        ],
        compiler_params=pltpu.CompilerParams(vmem_limit_bytes=24 * 2**20),
        name="wave",
    )(meta, *near_core(wins, *all_probes, side, turn, take, intensity, table))
    back = lax.all_to_all(updates, ("x", "core"), 0, 0, tiled=True)
    partial = pl.pallas_call(
        gather_kernel,
        out_shape=jax.ShapeDtypeStruct((NZ, 2 * ROWS, COLS), bf16),
        in_specs=[smem_spec(), vmem_spec()],
        out_specs=vmem_spec(),
        scratch_shapes=[pltpu.VMEM((NZ, 2 * ROWS, COLS), f32)],
        compiler_params=pltpu.CompilerParams(vmem_limit_bytes=8 * 2**20),
        name="gather",
    )(meta, *near_core(back))
    pieces = lax.all_to_all(partial, "z", 0, 0, tiled=True)
    obj_later = lax.optimization_barrier(obj_x)
    base = obj_later + dual_u
    center = denoise(base, meta, w_in, b_in, w_down, b_down, w_mid, b_mid, w_out, b_out)
    aux_next = base - center
    numer = jnp.sum(pieces.astype(f32), axis=0).reshape(2, ROWS, COLS)
    obj_next = (numer + rho_weight * (aux_next - dual_u)) / (denom + rho_weight)
    dual_next = dual_u + obj_next - aux_next
    return (obj_next, aux_next, dual_next, misfit.reshape(1))


def solution(mesh):
    split = Mesh(mesh.devices.reshape(NX, NZ, NC, NM), TILE_AXES + ("mode",))
    grid = P(None, TILE_AXES, "mode")
    return jax.shard_map(
        per_device,
        mesh=split,
        in_specs=(
            grid,
            grid,
            P("mode", None, None, None),
            P(TILE_AXES, None, None),
        )
        + (P(),) * 10,
        out_specs=(grid, grid, grid, P(TILE_AXES)),
        check_vma=False,
    )
```

```python
import math

import jax
import jax.numpy as jnp
import numpy as np
from jax import lax
from jax.experimental import pallas as pl
from jax.experimental.pallas import tpu as pltpu
from jax.sharding import Mesh, PartitionSpec as P

HALO = 6
NX, NZ, NC, NM = 4, 8, 4, 4
PATCH = 256
ROWS = 32
COLS = 128
STRIPS = PATCH // ROWS + 1
HALF = PATCH // ROWS // NC

rho_weight = 2.0
floor_level = 0.25
f32 = jnp.float32
bf16 = jnp.bfloat16
TILE_AXES = ("x", "z", "core")


def shifted(value, axes, step):
    count = math.prod(lax.axis_size(a) for a in axes)
    pairs = [(i, i + step) for i in range(count) if 0 <= i + step < count]
    return lax.ppermute(value, axes, pairs)


def extended_2(value, sides, width):
    for axes, dim in sides:
        length = value.shape[dim]
        last = lax.slice_in_dim(value, length - width, length, axis=dim)
        first = lax.slice_in_dim(value, 0, width, axis=dim)
        before = shifted(last, axes, 1)
        after = shifted(first, axes, -1)
        value = jnp.concatenate([before, value, after], axis=dim)
    return value


def vmem_spec():
    return pl.BlockSpec(memory_space=pltpu.VMEM)


def near_core(*arrays):
    return [pltpu.with_memory_space_constraint(a, pltpu.VMEM) for a in arrays]


def any_spec():
    return pl.BlockSpec(memory_space=pl.ANY)


def smem_spec():
    return pl.BlockSpec(memory_space=pltpu.SMEM)


def ids(meta):
    return meta[2, 0], meta[2, 1], meta[2, 2], meta[2, 3]


def first_strip(s0, core):
    return s0 + ((core - s0) & (NC - 1))


def copy_out(held, out, sems, count, same):
    copies = [
        pltpu.make_async_copy(held if same else held.at[n], out.at[n], sems.at[n])
        for n in range(count)
    ]
    for copy in copies:
        copy.start()
    return copies


def row_in_strip():
    return lax.broadcasted_iota(jnp.int32, (2 * ROWS, COLS), 0) & (ROWS - 1)


def z_slot(strip):
    return (strip % (NZ * NC)) // NC


def strips_of(row, core):
    s0 = row // ROWS
    begin = first_strip(s0, core)
    return begin, jnp.where(begin == s0, row - s0 * ROWS, 0)


def pack_kernel(meta, near, out, held, sems):
    _, z, core, _ = ids(meta)
    rows = row_in_strip()
    copies = []
    for target in range(NX * NC):
        tx, tc = target // NC, target % NC
        begin, cut = strips_of(meta[0, tx * (NZ * NC) + z * NC + tc], core)
        late = near[z_slot(begin + NC * HALF)].astype(f32)
        early = near[z_slot(begin)].astype(f32)
        held[target, 0] = jnp.where(rows < cut, late, early).astype(bf16)
        for j in range(1, HALF):
            held[target, j] = near[z_slot(begin + NC * j)]
        copy = pltpu.make_async_copy(held.at[target], out.at[target], sems.at[target])
        copy.start()
        copies.append(copy)
    for copy in copies:
        copy.wait()


def window_kernel(meta, got, out, tall, held, sems):
    x, z, core, _ = ids(meta)
    row = meta[0, x * (NZ * NC) + z * NC + core]
    s0 = row // ROWS
    for i in range(STRIPS):
        strip = s0 + i
        source = jnp.minimum(strip // (NZ * NC), NX - 1) * NC + (strip & (NC - 1))
        block = got[source, (i // NC) % HALF].astype(f32)
        tall[0, pl.ds(i * ROWS, ROWS)] = block[:ROWS]
        tall[1, pl.ds(i * ROWS, ROWS)] = block[ROWS:]
    offset = row - s0 * ROWS
    for plane in range(2):
        held[plane] = tall[plane, pl.ds(offset, PATCH)].astype(bf16)
    for copy in copy_out(held, out, sems, NM, True):
        copy.wait()


def dot(a, b):
    return jnp.dot(a, b, preferred_element_type=f32)


def wave_kernel(
    meta, wins, probe0, probe1, probe2, probe3, side, turn, take, intensity, table, out, err, far_all, tall
):
    x, z, core, _ = ids(meta)
    mine = x * (NZ * NC) + z * NC + core
    row = meta[0, mine]
    s0 = row // ROWS
    offset = row - s0 * ROWS
    t_re = table[0]
    t_im = table[1]
    t_neg = -t_im
    left = jnp.concatenate(
        [jnp.concatenate([t_re, t_neg], axis=1), jnp.concatenate([t_im, t_re], axis=1)], axis=0
    )
    right = jnp.concatenate(
        [jnp.concatenate([t_re, t_im], axis=1), jnp.concatenate([t_neg, t_re], axis=1)], axis=0
    )
    full = jnp.concatenate(
        [jnp.concatenate([wins[m, p] for m in range(NM)], axis=1) for p in range(2)], axis=0
    )
    patch = dot(full, take[...])
    obj_re = patch[:PATCH]
    obj_im = patch[PATCH:]
    probes = (probe0, probe1, probe2, probe3)
    power = jnp.zeros((PATCH, PATCH), f32)
    for m in range(NM):
        p_re = probes[m][0].astype(f32)
        p_im = probes[m][1].astype(f32)
        wave = jnp.concatenate(
            [(p_re * obj_re - p_im * obj_im).astype(bf16), (p_re * obj_im + p_im * obj_re).astype(bf16)],
            axis=0,
        )
        half = dot(left, wave).astype(bf16)
        far = dot(jnp.concatenate([half[:PATCH], half[PATCH:]], axis=1), right)
        far_all[m] = far
        power = power + far[:, :PATCH] * far[:, :PATCH] + far[:, PATCH:] * far[:, PATCH:]
    measured = jnp.sqrt(intensity[0])
    gap = jnp.sqrt(power) - measured
    err[...] = jnp.sum(gap * gap, keepdims=True) * (1.0 / (PATCH * PATCH))
    scale = measured / jnp.sqrt(jnp.maximum(power, floor_level))
    sums = [jnp.zeros((PATCH, 2 * COLS), f32) for _ in range(2)]
    for pair in range(NM // 2):
        halves = []
        for m in (2 * pair, 2 * pair + 1):
            far = far_all[m]
            scaled = jnp.concatenate(
                [(far[:, :PATCH] * scale).astype(bf16), (far[:, PATCH:] * scale).astype(bf16)],
                axis=1,
            )
            halves.append(dot(scaled, turn[...]).astype(bf16))
        stacked = [
            jnp.concatenate([h[:, p * COLS : (p + 1) * COLS] for h in halves], axis=1)
            for p in range(2)
        ]
        back = dot(right, jnp.concatenate(stacked, axis=0))
        back_re = back[:PATCH]
        back_im = back[PATCH:]
        q_re = side[pair, 0].astype(f32)
        q_im = side[pair, 1].astype(f32)
        sums[0] = sums[0] + (q_re * back_re + q_im * back_im)
        sums[1] = sums[1] + (q_re * back_im - q_im * back_re)
    sum_re, sum_im = [v[:, :COLS] + v[:, COLS:] for v in sums]
    tall[...] = jnp.zeros(tall.shape, f32)
    tall[0, pl.ds(offset, PATCH)] = sum_re
    tall[1, pl.ds(offset, PATCH)] = sum_im
    out[...] = jnp.zeros(out.shape, bf16)
    for i in range(STRIPS):
        strip = s0 + i
        target = jnp.minimum(strip // (NZ * NC), NX - 1) * NC + (strip & (NC - 1))
        piece = jnp.concatenate([tall[p, pl.ds(i * ROWS, ROWS)] for p in range(2)], axis=0)
        if i < NC * HALF:
            out[target, i // NC] = piece.astype(bf16)
        else:
            out[target, 0] = (out[target, 0].astype(f32) + piece).astype(bf16)


def gather_kernel(meta, got, out, acc):
    _, z, core, _ = ids(meta)
    rows = row_in_strip()
    acc[...] = jnp.zeros(acc.shape, f32)
    for source in range(NX * NC):
        sx, sc = source // NC, source % NC
        begin, cut = strips_of(meta[0, sx * (NZ * NC) + z * NC + sc], core)
        both = got[source, 0].astype(f32)
        late, early = z_slot(begin + NC * HALF), z_slot(begin)
        acc[late] = acc[late] + jnp.where(rows < cut, both, 0.0)
        acc[early] = acc[early] + jnp.where(rows < cut, 0.0, both)
        for j in range(1, HALF):
            slot = z_slot(begin + NC * j)
            acc[slot] = acc[slot] + got[source, j].astype(f32)
    out[...] = acc[...].astype(bf16)


def weight_kernel(meta, probe0, probe1, probe2, probe3, table, out, side, turn, take, padded):
    x, z, core, mode = ids(meta)
    row0 = (x * (NZ * NC) + z * NC + core) * ROWS
    col0 = mode * COLS
    probes = (probe0, probe1, probe2, probe3)
    mine = x * (NZ * NC) + z * NC + core
    src = lax.broadcasted_iota(jnp.int32, (NM * COLS, PATCH), 0)
    dst = lax.broadcasted_iota(jnp.int32, (NM * COLS, PATCH), 1)
    take[...] = jnp.where(src == dst + meta[1, mine], 1.0, 0.0).astype(bf16)
    src = lax.broadcasted_iota(jnp.int32, (PATCH, COLS), 0)
    dst = lax.broadcasted_iota(jnp.int32, (PATCH, COLS), 1)
    keep = jnp.where(src == dst + (col0 - meta[1, mine]), 1.0, 0.0).astype(bf16)
    for m in range(NM):
        for plane in range(2):
            moved_probe = dot(probes[m][plane], keep).astype(bf16)
            side[m // 2, plane, :, pl.ds(m % 2 * COLS, COLS)] = moved_probe
    k_re = dot(table[0], keep).astype(bf16)
    k_im = dot(table[1], keep).astype(bf16)
    turn[...] = jnp.concatenate(
        [jnp.concatenate([k_re, -k_im], axis=1), jnp.concatenate([k_im, k_re], axis=1)], axis=0
    )
    total = jnp.zeros((PATCH, PATCH), f32)
    for probe in probes:
        p_re = probe[0].astype(f32)
        p_im = probe[1].astype(f32)
        total = total + p_re * p_re + p_im * p_im
    padded[...] = jnp.zeros(padded.shape, f32)
    for half in range(PATCH // COLS):
        padded[1 + half, pl.ds(ROWS, PATCH)] = total[:, half * COLS : (half + 1) * COLS]
    out[...] = jnp.zeros(out.shape, f32)

    def add(k, carry):
        down = row0 - meta[0, k] + ROWS
        over = col0 - meta[1, k] + COLS
        hit = (down > 0) & (down < PATCH + ROWS) & (over > 0) & (over < PATCH + COLS)

        @pl.when(hit)
        def _():
            rows = jnp.concatenate([padded[q, pl.ds(down, ROWS)] for q in range(4)], axis=1)
            moved = pltpu.roll(rows, PATCH + 2 * COLS - over, 1)
            out[...] = out[...] + moved[:, :COLS]

        return carry

    lax.fori_loop(0, meta.shape[1], add, 0)


def dft_table():
    grid = np.arange(PATCH)[:, None] * np.arange(PATCH)[None, :] % PATCH
    angle = 2.0 * np.pi / PATCH * grid
    factor = 1.0 / math.sqrt(PATCH)
    table = np.stack([np.cos(angle) * factor, -np.sin(angle) * factor])
    return jnp.asarray(table.astype(np.float32)).astype(bf16)


CY, CX = (ROWS + 2 * HALO) // 2, (COLS + 2 * HALO) // 2
FLAT = CY * 128
CHUNK = 256
PHASES = ((0, 0), (0, 1), (1, 0), (1, 1))
SHIFTS = tuple((dy, dx) for dy in (-1, 0, 1) for dx in (-1, 0, 1))


def split_tables():
    first = np.zeros((9, 2, 4, 72), np.float32)
    last = np.zeros((9, 36, 4), np.float32)
    for tap in range(9):
        for ij, (i, j) in enumerate(PHASES):
            r, c = i + tap // 3 - 1, j + tap % 3 - 1
            p, q, dy, dx = r & 1, c & 1, r >> 1, c >> 1
            s = (dy + 1) * 3 + dx + 1
            for ch in range(2):
                first[tap, ch, ij, s * 8 + q * 4 + ch * 2 + p] = 1
            last[tap, s * 4 + ij, p * 2 + q] = 1
    return jnp.asarray(first).astype(bf16), jnp.asarray(last).astype(bf16)


def moved(value, dy, dx):
    if dx:
        value = pltpu.roll(value, (-dx) % FLAT, 1)
    if dy == 1:
        value = jnp.concatenate([value[:, 128:], value[:, :128]], axis=1)
    if dy == -1:
        value = jnp.concatenate([value[:, FLAT - 128 :], value[:, : FLAT - 128]], axis=1)
    return value


def denoise_kernel(
    meta,
    b_out,
    ext,
    first_w,
    down_w,
    mid_w,
    last_w,
    biases,
    out,
    halves,
    planes,
    taps1,
    maps,
    coarse,
    taps2,
    fourth,
    parts,
    inter,
):
    x, z, core, mode = ids(meta)
    chans = coarse.shape[0]
    height = ROWS + 2 * HALO
    width = COLS + 2 * HALO
    src = lax.broadcasted_iota(jnp.int32, (width, 256), 0)
    dst = lax.broadcasted_iota(jnp.int32, (width, 256), 1)
    lane = dst & 127
    even_odd = jnp.where((src == 2 * lane + (dst >> 7)) & (lane < CX), 1.0, 0.0).astype(bf16)
    for ch in range(2):
        row = dot(ext[ch], even_odd)
        for q in range(2):
            halves[q, pl.ds(ch * height, height)] = row[:, q * 128 : (q + 1) * 128]
    for y in range(CY):
        pieces = [
            halves[q, pl.ds(ch * height + 2 * y, 2)] for q in range(2) for ch in range(2)
        ]
        planes[:, pl.ds(y * 128, 128)] = jnp.concatenate(pieces, axis=0)
    full = planes[...]
    taps1[...] = jnp.concatenate([moved(full, dy, dx) for dy, dx in SHIFTS], axis=0).astype(bf16)

    row0 = (x * (NZ * NC) + z * NC + core) * ROWS - HALO
    col0 = mode * COLS - HALO
    height_all, width_all = NX * NZ * NC * ROWS, NM * COLS

    def masks(start):
        spot = lax.broadcasted_iota(jnp.int32, (1, CHUNK), 1) + start
        rows = row0 + 2 * (spot >> 7)
        cols = col0 + 2 * (spot & 127)
        found = []
        for p, q in PHASES:
            inside = (rows + p >= 0) & (rows + p < height_all)
            inside = inside & (cols + q >= 0) & (cols + q < width_all)
            found.append(jnp.where(inside, 1.0, 0.0))
        return found

    for start in range(0, FLAT, CHUNK):
        span = pl.ds(start, CHUNK)
        found = masks(start)
        value = dot(first_w[...], taps1[:, span])
        for n in range(4):
            part = value[n * chans : (n + 1) * chans] + biases[:, 0:1]
            maps[pl.ds(n * chans, chans), span] = (jnp.maximum(part, 0.0) * found[n]).astype(bf16)
        value = dot(down_w[...], maps[:, span]) + biases[:, 1:2]
        coarse[:, span] = (jnp.maximum(value, 0.0) * found[0]).astype(bf16).astype(f32)
    for s, (dy, dx) in enumerate(SHIFTS):
        taps2[pl.ds(s * chans, chans)] = moved(coarse[...], dy, dx).astype(bf16)
    for start in range(0, FLAT, CHUNK):
        span = pl.ds(start, CHUNK)
        found = masks(start)
        value = dot(mid_w[...], taps2[:, span]) + biases[:, 2:3]
        third = jnp.maximum(value, 0.0).astype(bf16).astype(f32)
        for n in range(4):
            rows = pl.ds(n * chans, chans)
            fourth[rows, span] = (third * found[n] + maps[rows, span].astype(f32)).astype(bf16)
        parts[:, span] = dot(last_w[...], fourth[:, span])
    total = moved(parts[pl.ds(0, 8)], *SHIFTS[0])
    for s in range(1, 9):
        total = total + moved(parts[pl.ds(s * 8, 8)], *SHIFTS[s])
    planes[...] = total
    for y in range(HALO // 2, HALO // 2 + ROWS // 2):
        tile = planes[:, pl.ds(y * 128, 128)]
        for i, j in PHASES:
            for ch in range(2):
                n = (i * 2 + j) * 2 + ch
                inter[j, pl.ds(ch * ROWS + 2 * y - HALO + i, 1)] = tile[n : n + 1]
    e_src = lax.broadcasted_iota(jnp.int32, (256, COLS), 0)
    e_dst = lax.broadcasted_iota(jnp.int32, (256, COLS), 1)
    weave = jnp.where(2 * (e_src & 127) - HALO + (e_src >> 7) == e_dst, 1.0, 0.0).astype(bf16)
    wide = jnp.concatenate([inter[0], inter[1]], axis=1)
    high = wide.astype(bf16)
    low = (wide - high.astype(f32)).astype(bf16)
    woven = dot(high, weave) + dot(low, weave)
    for ch in range(2):
        out[ch] = woven[ch * ROWS : (ch + 1) * ROWS] + b_out[ch]


def denoise(base, meta, w_in, b_in, w_down, b_down, w_mid, b_mid, w_out, b_out):
    chans = w_in.shape[1]
    extended = extended_2(base.astype(bf16), ((TILE_AXES, 1), (("mode",), 2)), HALO)
    first, last = split_tables()
    first_w = jnp.einsum("toc,tcik->iok", w_in, first).reshape(4 * chans, 72)
    last_w = jnp.einsum("tcd,tmp->mcpd", w_out, last).reshape(72, 4 * chans)
    down_w = jnp.transpose(w_down, (1, 0, 2)).reshape(chans, 4 * chans)
    mid_w = jnp.transpose(w_mid, (1, 0, 2)).reshape(chans, 9 * chans)
    return pl.pallas_call(
        denoise_kernel,
        out_shape=jax.ShapeDtypeStruct((2, ROWS, COLS), f32),
        in_specs=[smem_spec(), smem_spec()] + [vmem_spec()] * 6,
        out_specs=vmem_spec(),
        scratch_shapes=[
            pltpu.VMEM((2, 2 * (ROWS + 2 * HALO), 128), f32),
            pltpu.VMEM((8, FLAT), f32),
            pltpu.VMEM((72, FLAT), bf16),
            pltpu.VMEM((4 * chans, FLAT), bf16),
            pltpu.VMEM((chans, FLAT), f32),
            pltpu.VMEM((9 * chans, FLAT), bf16),
            pltpu.VMEM((4 * chans, FLAT), bf16),
            pltpu.VMEM((72, FLAT), f32),
            pltpu.VMEM((2, 2 * ROWS, 128), f32),
        ],
        cost_estimate=pl.CostEstimate(
            flops=4 * 10**9, bytes_accessed=2 * 10**7, transcendentals=0
        ),
        compiler_params=pltpu.CompilerParams(vmem_limit_bytes=24 * 2**20),
        name="denoise",
    )(
        meta,
        b_out,
        extended,
        first_w,
        down_w,
        mid_w,
        last_w,
        jnp.stack([b_in, b_down, b_mid], axis=1),
    )


def per_device(
    obj_x,
    dual_u,
    probes,
    intensity,
    corners,
    owner,
    w_in,
    b_in,
    w_down,
    b_down,
    w_mid,
    b_mid,
    w_out,
    b_out,
):
    x = lax.axis_index("x")
    z = lax.axis_index("z")
    core = lax.axis_index("core")
    mode = lax.axis_index("mode")
    tiles = NX * NZ * NC
    lanes = jnp.arange(tiles, dtype=jnp.int32)
    owned = owner[None, :] == lanes[:, None]
    by_owner = jnp.sum(jnp.where(owned[None], corners[:, None, :], 0), axis=2)
    place = jnp.where(lanes == 0, x, jnp.where(lanes == 1, z, jnp.where(lanes == 2, core, mode)))
    meta = jnp.concatenate([by_owner, place[None]], axis=0).astype(jnp.int32)

    rows = jnp.broadcast_to(obj_x.reshape(1, 2 * ROWS, COLS), (NZ, 2 * ROWS, COLS))
    spread = rows.astype(bf16)
    near = lax.all_to_all(spread, "z", 0, 0, tiled=True)
    probe0 = probes[0].astype(bf16)
    others = [
        lax.ppermute(probe0, "mode", [(i, (i + k) % NM) for i in range(NM)])
        for k in range(1, NM)
    ]
    all_probes = (probe0, *others)
    table = dft_table()
    denom, side, turn, take = pl.pallas_call(
        weight_kernel,
        out_shape=(
            jax.ShapeDtypeStruct((ROWS, COLS), f32),
            pltpu.VMEM((NM // 2, 2, PATCH, 2 * COLS), bf16),
            pltpu.VMEM((2 * PATCH, 2 * COLS), bf16),
            pltpu.VMEM((NM * COLS, PATCH), bf16),
        ),
        in_specs=[smem_spec()] + [vmem_spec()] * (NM + 1),
        out_specs=(vmem_spec(),) * 4,
        scratch_shapes=[pltpu.VMEM((PATCH // COLS + 2, PATCH + 2 * ROWS, COLS), f32)],
        compiler_params=pltpu.CompilerParams(vmem_limit_bytes=12 * 2**20),
        name="weight",
    )(meta, *near_core(*all_probes), table)
    packed = pl.pallas_call(
        pack_kernel,
        out_shape=jax.ShapeDtypeStruct((NX * NC, HALF, 2 * ROWS, COLS), bf16),
        in_specs=[smem_spec(), vmem_spec()],
        out_specs=any_spec(),
        scratch_shapes=[
            pltpu.VMEM((NX * NC, HALF, 2 * ROWS, COLS), bf16),
            pltpu.SemaphoreType.DMA((NX * NC,)),
        ],
        compiler_params=pltpu.CompilerParams(vmem_limit_bytes=8 * 2**20),
        name="pack",
    )(meta, *near_core(near))
    got = lax.all_to_all(packed, ("x", "core"), 0, 0, tiled=True)
    window = pl.pallas_call(
        window_kernel,
        out_shape=jax.ShapeDtypeStruct((NM, 2, PATCH, COLS), bf16),
        in_specs=[smem_spec(), vmem_spec()],
        out_specs=any_spec(),
        scratch_shapes=[
            pltpu.VMEM((2, STRIPS * ROWS, COLS), f32),
            pltpu.VMEM((2, PATCH, COLS), bf16),
            pltpu.SemaphoreType.DMA((NM,)),
        ],
        compiler_params=pltpu.CompilerParams(vmem_limit_bytes=8 * 2**20),
        name="window",
    )(meta, *near_core(got))
    wins = lax.all_to_all(window, "mode", 0, 0, tiled=True)
    updates, misfit = pl.pallas_call(
        wave_kernel,
        out_shape=(
            jax.ShapeDtypeStruct((NX * NC, HALF, 2 * ROWS, COLS), bf16),
            jax.ShapeDtypeStruct((1, 1), f32),
        ),
        in_specs=[smem_spec()] + [vmem_spec()] * 10,
        out_specs=(vmem_spec(), vmem_spec()),
        scratch_shapes=[
            pltpu.VMEM((NM, PATCH, 2 * PATCH), f32),
            pltpu.VMEM((2, STRIPS * ROWS, COLS), f32),
        ],
        compiler_params=pltpu.CompilerParams(vmem_limit_bytes=24 * 2**20),
        name="wave",
    )(meta, *near_core(wins, *all_probes, side, turn, take, intensity, table))
    back = lax.all_to_all(updates, ("x", "core"), 0, 0, tiled=True)
    partial = pl.pallas_call(
        gather_kernel,
        out_shape=jax.ShapeDtypeStruct((NZ, 2 * ROWS, COLS), bf16),
        in_specs=[smem_spec(), vmem_spec()],
        out_specs=vmem_spec(),
        scratch_shapes=[pltpu.VMEM((NZ, 2 * ROWS, COLS), f32)],
        compiler_params=pltpu.CompilerParams(vmem_limit_bytes=8 * 2**20),
        name="gather",
    )(meta, *near_core(back))
    pieces = lax.all_to_all(partial, "z", 0, 0, tiled=True)
    obj_later = lax.optimization_barrier(obj_x)
    base = obj_later + dual_u
    center = denoise(base, meta, w_in, b_in, w_down, b_down, w_mid, b_mid, w_out, b_out)
    aux_next = base - center
    numer = jnp.sum(pieces.astype(f32), axis=0).reshape(2, ROWS, COLS)
    obj_next = (numer + rho_weight * (aux_next - dual_u)) / (denom + rho_weight)
    dual_next = dual_u + obj_next - aux_next
    return (obj_next, aux_next, dual_next, misfit.reshape(1))


def solution(mesh):
    split = Mesh(mesh.devices.reshape(NX, NZ, NC, NM), TILE_AXES + ("mode",))
    grid = P(None, TILE_AXES, "mode")
    return jax.shard_map(
        per_device,
        mesh=split,
        in_specs=(
            grid,
            grid,
            P("mode", None, None, None),
            P(TILE_AXES, None, None),
        )
        + (P(),) * 10,
        out_specs=(grid, grid, grid, P(TILE_AXES)),
        check_vma=False,
    )
```

```python
import math

import jax
import jax.numpy as jnp
import numpy as np
from jax import lax
from jax.experimental import pallas as pl
from jax.experimental.pallas import tpu as pltpu
from jax.sharding import Mesh, PartitionSpec as P

HALO = 6
NX, PER_X, NM = 4, 32, 4
OUT, BACK = 4, 2
PATCH = 256
ROWS = 32
COLS = 128
STRIPS = PATCH // ROWS + 1
SPAN = PATCH // ROWS

rho_weight = 2.0
floor_level = 0.25
f32 = jnp.float32
bf16 = jnp.bfloat16
TILE_AXES = ("x", "zq", "zp", "core")


def shifted(value, axes, step):
    count = math.prod(lax.axis_size(a) for a in axes)
    pairs = [(i, i + step) for i in range(count) if 0 <= i + step < count]
    return lax.ppermute(value, axes, pairs)


def extended_2(value, sides, width):
    for axes, dim in sides:
        length = value.shape[dim]
        last = lax.slice_in_dim(value, length - width, length, axis=dim)
        first = lax.slice_in_dim(value, 0, width, axis=dim)
        before = shifted(last, axes, 1)
        after = shifted(first, axes, -1)
        value = jnp.concatenate([before, value, after], axis=dim)
    return value


def vmem_spec():
    return pl.BlockSpec(memory_space=pltpu.VMEM)


def near_core(*arrays):
    return [pltpu.with_memory_space_constraint(a, pltpu.VMEM) for a in arrays]


def any_spec():
    return pl.BlockSpec(memory_space=pl.ANY)


def smem_spec():
    return pl.BlockSpec(memory_space=pltpu.SMEM)


def ids(meta):
    return meta[2, 0], meta[2, 1], meta[2, 2]


def first_strip(s0, core, step):
    return s0 + ((core - s0) & (step - 1))


def copy_out(held, out, sems, count, same):
    copies = [
        pltpu.make_async_copy(held if same else held.at[n], out.at[n], sems.at[n])
        for n in range(count)
    ]
    for copy in copies:
        copy.start()
    return copies


def row_in_strip():
    return lax.broadcasted_iota(jnp.int32, (2 * ROWS, COLS), 0) & (ROWS - 1)


def z_slot(strip, step):
    return (strip % PER_X) // step


def strips_of(row, core, step):
    s0 = row // ROWS
    begin = first_strip(s0, core, step)
    return begin, jnp.where(begin == s0, row - s0 * ROWS, 0)


def pack_kernel(meta, near, out, held, sems):
    _, spot, _ = ids(meta)
    z, core = spot // OUT, spot % OUT
    rows = row_in_strip()
    copies = []
    for target in range(NX * OUT):
        tx, tc = target // OUT, target % OUT
        begin, cut = strips_of(meta[0, tx * PER_X + z * OUT + tc], core, OUT)
        late = near[z_slot(begin + SPAN, OUT)].astype(f32)
        early = near[z_slot(begin, OUT)].astype(f32)
        held[target, 0] = jnp.where(rows < cut, late, early).astype(bf16)
        for j in range(1, SPAN // OUT):
            held[target, j] = near[z_slot(begin + OUT * j, OUT)]
        copy = pltpu.make_async_copy(held.at[target], out.at[target], sems.at[target])
        copy.start()
        copies.append(copy)
    for copy in copies:
        copy.wait()


def window_kernel(meta, got, out, tall, held, sems):
    x, spot, _ = ids(meta)
    row = meta[0, x * PER_X + spot]
    s0 = row // ROWS
    for i in range(STRIPS):
        strip = s0 + i
        source = jnp.minimum(strip // PER_X, NX - 1) * OUT + (strip & (OUT - 1))
        block = got[source, i % SPAN // OUT].astype(f32)
        tall[0, pl.ds(i * ROWS, ROWS)] = block[:ROWS]
        tall[1, pl.ds(i * ROWS, ROWS)] = block[ROWS:]
    offset = row - s0 * ROWS
    for plane in range(2):
        held[plane] = tall[plane, pl.ds(offset, PATCH)].astype(bf16)
    for copy in copy_out(held, out, sems, NM, True):
        copy.wait()


def dot(a, b):
    return jnp.dot(a, b, preferred_element_type=f32)


def wave_kernel(
    meta, wins, probe0, probe1, probe2, probe3, side, turn, take, intensity, table, out, err, far_all, tall
):
    x, spot, _ = ids(meta)
    mine = x * PER_X + spot
    row = meta[0, mine]
    s0 = row // ROWS
    offset = row - s0 * ROWS
    t_re = table[0]
    t_im = table[1]
    t_neg = -t_im
    left = jnp.concatenate(
        [jnp.concatenate([t_re, t_neg], axis=1), jnp.concatenate([t_im, t_re], axis=1)], axis=0
    )
    right = jnp.concatenate(
        [jnp.concatenate([t_re, t_im], axis=1), jnp.concatenate([t_neg, t_re], axis=1)], axis=0
    )
    full = jnp.concatenate(
        [jnp.concatenate([wins[m, p] for m in range(NM)], axis=1) for p in range(2)], axis=0
    )
    patch = dot(full, take[...])
    obj_re = patch[:PATCH]
    obj_im = patch[PATCH:]
    probes = (probe0, probe1, probe2, probe3)
    power = jnp.zeros((PATCH, PATCH), f32)
    for m in range(NM):
        p_re = probes[m][0].astype(f32)
        p_im = probes[m][1].astype(f32)
        wave = jnp.concatenate(
            [(p_re * obj_re - p_im * obj_im).astype(bf16), (p_re * obj_im + p_im * obj_re).astype(bf16)],
            axis=0,
        )
        half = dot(left, wave).astype(bf16)
        far = dot(jnp.concatenate([half[:PATCH], half[PATCH:]], axis=1), right)
        far_all[m] = far
        power = power + far[:, :PATCH] * far[:, :PATCH] + far[:, PATCH:] * far[:, PATCH:]
    measured = jnp.sqrt(intensity[0])
    gap = jnp.sqrt(power) - measured
    err[...] = jnp.sum(gap * gap, keepdims=True) * (1.0 / (PATCH * PATCH))
    scale = measured / jnp.sqrt(jnp.maximum(power, floor_level))
    sums = [jnp.zeros((PATCH, 2 * COLS), f32) for _ in range(2)]
    for pair in range(NM // 2):
        halves = []
        for m in (2 * pair, 2 * pair + 1):
            far = far_all[m]
            scaled = jnp.concatenate(
                [(far[:, :PATCH] * scale).astype(bf16), (far[:, PATCH:] * scale).astype(bf16)],
                axis=1,
            )
            halves.append(dot(scaled, turn[...]).astype(bf16))
        stacked = [
            jnp.concatenate([h[:, p * COLS : (p + 1) * COLS] for h in halves], axis=1)
            for p in range(2)
        ]
        back = dot(right, jnp.concatenate(stacked, axis=0))
        back_re = back[:PATCH]
        back_im = back[PATCH:]
        q_re = side[pair, 0].astype(f32)
        q_im = side[pair, 1].astype(f32)
        sums[0] = sums[0] + (q_re * back_re + q_im * back_im)
        sums[1] = sums[1] + (q_re * back_im - q_im * back_re)
    sum_re, sum_im = [v[:, :COLS] + v[:, COLS:] for v in sums]
    tall[...] = jnp.zeros(tall.shape, f32)
    tall[0, pl.ds(offset, PATCH)] = sum_re
    tall[1, pl.ds(offset, PATCH)] = sum_im
    out[...] = jnp.zeros(out.shape, bf16)
    for i in range(STRIPS):
        strip = s0 + i
        target = jnp.minimum(strip // PER_X, NX - 1) * BACK + (strip & (BACK - 1))
        piece = jnp.concatenate([tall[p, pl.ds(i * ROWS, ROWS)] for p in range(2)], axis=0)
        if i < SPAN:
            out[target, i // BACK] = piece.astype(bf16)
        else:
            out[target, 0] = (out[target, 0].astype(f32) + piece).astype(bf16)


def gather_kernel(meta, got, out, acc):
    _, spot, _ = ids(meta)
    z, core = spot // BACK, spot % BACK
    rows = row_in_strip()
    acc[...] = jnp.zeros(acc.shape, f32)
    for source in range(NX * BACK):
        sx, sc = source // BACK, source % BACK
        begin, cut = strips_of(meta[0, sx * PER_X + z * BACK + sc], core, BACK)
        both = got[source, 0].astype(f32)
        late, early = z_slot(begin + SPAN, BACK), z_slot(begin, BACK)
        acc[late] = acc[late] + jnp.where(rows < cut, both, 0.0)
        acc[early] = acc[early] + jnp.where(rows < cut, 0.0, both)
        for j in range(1, SPAN // BACK):
            slot = z_slot(begin + BACK * j, BACK)
            acc[slot] = acc[slot] + got[source, j].astype(f32)
    out[...] = acc[...].astype(bf16)


def weight_kernel(meta, probe0, probe1, probe2, probe3, table, out, side, turn, take, padded):
    x, spot, mode = ids(meta)
    mine = x * PER_X + spot
    row0 = mine * ROWS
    col0 = mode * COLS
    probes = (probe0, probe1, probe2, probe3)
    src = lax.broadcasted_iota(jnp.int32, (NM * COLS, PATCH), 0)
    dst = lax.broadcasted_iota(jnp.int32, (NM * COLS, PATCH), 1)
    take[...] = jnp.where(src == dst + meta[1, mine], 1.0, 0.0).astype(bf16)
    src = lax.broadcasted_iota(jnp.int32, (PATCH, COLS), 0)
    dst = lax.broadcasted_iota(jnp.int32, (PATCH, COLS), 1)
    keep = jnp.where(src == dst + (col0 - meta[1, mine]), 1.0, 0.0).astype(bf16)
    for m in range(NM):
        for plane in range(2):
            moved_probe = dot(probes[m][plane], keep).astype(bf16)
            side[m // 2, plane, :, pl.ds(m % 2 * COLS, COLS)] = moved_probe
    k_re = dot(table[0], keep).astype(bf16)
    k_im = dot(table[1], keep).astype(bf16)
    turn[...] = jnp.concatenate(
        [jnp.concatenate([k_re, -k_im], axis=1), jnp.concatenate([k_im, k_re], axis=1)], axis=0
    )
    total = jnp.zeros((PATCH, PATCH), f32)
    for probe in probes:
        p_re = probe[0].astype(f32)
        p_im = probe[1].astype(f32)
        total = total + p_re * p_re + p_im * p_im
    padded[...] = jnp.zeros(padded.shape, f32)
    for half in range(PATCH // COLS):
        padded[1 + half, pl.ds(ROWS, PATCH)] = total[:, half * COLS : (half + 1) * COLS]
    out[...] = jnp.zeros(out.shape, f32)

    def add(k, carry):
        down = row0 - meta[0, k] + ROWS
        over = col0 - meta[1, k] + COLS
        hit = (down > 0) & (down < PATCH + ROWS) & (over > 0) & (over < PATCH + COLS)

        @pl.when(hit)
        def _():
            rows = jnp.concatenate([padded[q, pl.ds(down, ROWS)] for q in range(4)], axis=1)
            moved = pltpu.roll(rows, PATCH + 2 * COLS - over, 1)
            out[...] = out[...] + moved[:, :COLS]

        return carry

    lax.fori_loop(0, meta.shape[1], add, 0)


def dft_table():
    grid = np.arange(PATCH)[:, None] * np.arange(PATCH)[None, :] % PATCH
    angle = 2.0 * np.pi / PATCH * grid
    factor = 1.0 / math.sqrt(PATCH)
    table = np.stack([np.cos(angle) * factor, -np.sin(angle) * factor])
    return jnp.asarray(table.astype(np.float32)).astype(bf16)


CY, CX = (ROWS + 2 * HALO) // 2, (COLS + 2 * HALO) // 2
FLAT = CY * 128
CHUNK = 256
PHASES = ((0, 0), (0, 1), (1, 0), (1, 1))
SHIFTS = tuple((dy, dx) for dy in (-1, 0, 1) for dx in (-1, 0, 1))


def split_tables():
    first = np.zeros((9, 2, 4, 72), np.float32)
    last = np.zeros((9, 36, 4), np.float32)
    for tap in range(9):
        for ij, (i, j) in enumerate(PHASES):
            r, c = i + tap // 3 - 1, j + tap % 3 - 1
            p, q, dy, dx = r & 1, c & 1, r >> 1, c >> 1
            s = (dy + 1) * 3 + dx + 1
            for ch in range(2):
                first[tap, ch, ij, s * 8 + q * 4 + ch * 2 + p] = 1
            last[tap, s * 4 + ij, p * 2 + q] = 1
    return jnp.asarray(first).astype(bf16), jnp.asarray(last).astype(bf16)


def moved(value, dy, dx):
    if dx:
        value = pltpu.roll(value, (-dx) % FLAT, 1)
    if dy == 1:
        value = jnp.concatenate([value[:, 128:], value[:, :128]], axis=1)
    if dy == -1:
        value = jnp.concatenate([value[:, FLAT - 128 :], value[:, : FLAT - 128]], axis=1)
    return value


def denoise_kernel(
    meta,
    b_out,
    ext,
    first_w,
    down_w,
    mid_w,
    last_w,
    biases,
    out,
    halves,
    planes,
    taps1,
    maps,
    coarse,
    taps2,
    fourth,
    parts,
    inter,
):
    x, spot, mode = ids(meta)
    chans = coarse.shape[0]
    height = ROWS + 2 * HALO
    width = COLS + 2 * HALO
    src = lax.broadcasted_iota(jnp.int32, (width, 256), 0)
    dst = lax.broadcasted_iota(jnp.int32, (width, 256), 1)
    lane = dst & 127
    even_odd = jnp.where((src == 2 * lane + (dst >> 7)) & (lane < CX), 1.0, 0.0).astype(bf16)
    for ch in range(2):
        row = dot(ext[ch], even_odd)
        for q in range(2):
            halves[q, pl.ds(ch * height, height)] = row[:, q * 128 : (q + 1) * 128]
    for y in range(CY):
        pieces = [
            halves[q, pl.ds(ch * height + 2 * y, 2)] for q in range(2) for ch in range(2)
        ]
        planes[:, pl.ds(y * 128, 128)] = jnp.concatenate(pieces, axis=0)
    full = planes[...]
    taps1[...] = jnp.concatenate([moved(full, dy, dx) for dy, dx in SHIFTS], axis=0).astype(bf16)

    row0 = (x * PER_X + spot) * ROWS - HALO
    col0 = mode * COLS - HALO
    height_all, width_all = NX * PER_X * ROWS, NM * COLS

    def masks(start):
        cell = lax.broadcasted_iota(jnp.int32, (1, CHUNK), 1) + start
        rows = row0 + 2 * (cell >> 7)
        cols = col0 + 2 * (cell & 127)
        found = []
        for p, q in PHASES:
            inside = (rows + p >= 0) & (rows + p < height_all)
            inside = inside & (cols + q >= 0) & (cols + q < width_all)
            found.append(jnp.where(inside, 1.0, 0.0))
        return found

    for start in range(0, FLAT, CHUNK):
        span = pl.ds(start, CHUNK)
        found = masks(start)
        value = dot(first_w[...], taps1[:, span])
        for n in range(4):
            part = value[n * chans : (n + 1) * chans] + biases[:, 0:1]
            maps[pl.ds(n * chans, chans), span] = (jnp.maximum(part, 0.0) * found[n]).astype(bf16)
        value = dot(down_w[...], maps[:, span]) + biases[:, 1:2]
        coarse[:, span] = (jnp.maximum(value, 0.0) * found[0]).astype(bf16).astype(f32)
    for s, (dy, dx) in enumerate(SHIFTS):
        taps2[pl.ds(s * chans, chans)] = moved(coarse[...], dy, dx).astype(bf16)
    for start in range(0, FLAT, CHUNK):
        span = pl.ds(start, CHUNK)
        found = masks(start)
        value = dot(mid_w[...], taps2[:, span]) + biases[:, 2:3]
        third = jnp.maximum(value, 0.0).astype(bf16).astype(f32)
        for n in range(4):
            rows = pl.ds(n * chans, chans)
            fourth[rows, span] = (third * found[n] + maps[rows, span].astype(f32)).astype(bf16)
        parts[:, span] = dot(last_w[...], fourth[:, span])
    total = moved(parts[pl.ds(0, 8)], *SHIFTS[0])
    for s in range(1, 9):
        total = total + moved(parts[pl.ds(s * 8, 8)], *SHIFTS[s])
    planes[...] = total
    for y in range(HALO // 2, HALO // 2 + ROWS // 2):
        tile = planes[:, pl.ds(y * 128, 128)]
        for i, j in PHASES:
            for ch in range(2):
                n = (i * 2 + j) * 2 + ch
                inter[j, pl.ds(ch * ROWS + 2 * y - HALO + i, 1)] = tile[n : n + 1]
    e_src = lax.broadcasted_iota(jnp.int32, (256, COLS), 0)
    e_dst = lax.broadcasted_iota(jnp.int32, (256, COLS), 1)
    weave = jnp.where(2 * (e_src & 127) - HALO + (e_src >> 7) == e_dst, 1.0, 0.0).astype(bf16)
    wide = jnp.concatenate([inter[0], inter[1]], axis=1)
    high = wide.astype(bf16)
    low = (wide - high.astype(f32)).astype(bf16)
    woven = dot(high, weave) + dot(low, weave)
    for ch in range(2):
        out[ch] = woven[ch * ROWS : (ch + 1) * ROWS] + b_out[ch]


def denoise(base, meta, w_in, b_in, w_down, b_down, w_mid, b_mid, w_out, b_out):
    chans = w_in.shape[1]
    extended = extended_2(base.astype(bf16), ((TILE_AXES, 1), (("mode",), 2)), HALO)
    first, last = split_tables()
    first_w = jnp.einsum("toc,tcik->iok", w_in, first).reshape(4 * chans, 72)
    last_w = jnp.einsum("tcd,tmp->mcpd", w_out, last).reshape(72, 4 * chans)
    down_w = jnp.transpose(w_down, (1, 0, 2)).reshape(chans, 4 * chans)
    mid_w = jnp.transpose(w_mid, (1, 0, 2)).reshape(chans, 9 * chans)
    return pl.pallas_call(
        denoise_kernel,
        out_shape=jax.ShapeDtypeStruct((2, ROWS, COLS), f32),
        in_specs=[smem_spec(), smem_spec()] + [vmem_spec()] * 6,
        out_specs=vmem_spec(),
        scratch_shapes=[
            pltpu.VMEM((2, 2 * (ROWS + 2 * HALO), 128), f32),
            pltpu.VMEM((8, FLAT), f32),
            pltpu.VMEM((72, FLAT), bf16),
            pltpu.VMEM((4 * chans, FLAT), bf16),
            pltpu.VMEM((chans, FLAT), f32),
            pltpu.VMEM((9 * chans, FLAT), bf16),
            pltpu.VMEM((4 * chans, FLAT), bf16),
            pltpu.VMEM((72, FLAT), f32),
            pltpu.VMEM((2, 2 * ROWS, 128), f32),
        ],
        cost_estimate=pl.CostEstimate(
            flops=4 * 10**9, bytes_accessed=2 * 10**7, transcendentals=0
        ),
        compiler_params=pltpu.CompilerParams(vmem_limit_bytes=24 * 2**20),
        name="denoise",
    )(
        meta,
        b_out,
        extended,
        first_w,
        down_w,
        mid_w,
        last_w,
        jnp.stack([b_in, b_down, b_mid], axis=1),
    )


def per_device(
    obj_x,
    dual_u,
    probes,
    intensity,
    corners,
    owner,
    w_in,
    b_in,
    w_down,
    b_down,
    w_mid,
    b_mid,
    w_out,
    b_out,
):
    x = lax.axis_index("x")
    spot = lax.axis_index(TILE_AXES[1:])
    mode = lax.axis_index("mode")
    tiles = NX * PER_X
    lanes = jnp.arange(tiles, dtype=jnp.int32)
    owned = owner[None, :] == lanes[:, None]
    by_owner = jnp.sum(jnp.where(owned[None], corners[:, None, :], 0), axis=2)
    place = jnp.where(lanes == 0, x, jnp.where(lanes == 1, spot, mode))
    meta = jnp.concatenate([by_owner, place[None]], axis=0).astype(jnp.int32)

    rows = jnp.broadcast_to(obj_x.reshape(1, 2 * ROWS, COLS), (PER_X // OUT, 2 * ROWS, COLS))
    spread = rows.astype(bf16)
    near = lax.all_to_all(spread, "zq", 0, 0, tiled=True)
    probe0 = probes[0].astype(bf16)
    probe1, probe3 = [
        lax.ppermute(probe0, "mode", [(i, (i + k) % NM) for i in range(NM)]) for k in (1, 3)
    ]
    probe2 = lax.ppermute(probe0, "mode", [(i, (i + 2) % NM) for i in range(NM)])
    all_probes = (probe0, probe1, probe2, probe3)
    table = dft_table()
    denom, side, turn, take = pl.pallas_call(
        weight_kernel,
        out_shape=(
            jax.ShapeDtypeStruct((ROWS, COLS), f32),
            pltpu.VMEM((NM // 2, 2, PATCH, 2 * COLS), bf16),
            pltpu.VMEM((2 * PATCH, 2 * COLS), bf16),
            pltpu.VMEM((NM * COLS, PATCH), bf16),
        ),
        in_specs=[smem_spec()] + [vmem_spec()] * (NM + 1),
        out_specs=(vmem_spec(),) * 4,
        scratch_shapes=[pltpu.VMEM((PATCH // COLS + 2, PATCH + 2 * ROWS, COLS), f32)],
        compiler_params=pltpu.CompilerParams(vmem_limit_bytes=12 * 2**20),
        name="weight",
    )(meta, *near_core(*all_probes), table)
    packed = pl.pallas_call(
        pack_kernel,
        out_shape=jax.ShapeDtypeStruct((NX * OUT, SPAN // OUT, 2 * ROWS, COLS), bf16),
        in_specs=[smem_spec(), vmem_spec()],
        out_specs=any_spec(),
        scratch_shapes=[
            pltpu.VMEM((NX * OUT, SPAN // OUT, 2 * ROWS, COLS), bf16),
            pltpu.SemaphoreType.DMA((NX * OUT,)),
        ],
        compiler_params=pltpu.CompilerParams(vmem_limit_bytes=8 * 2**20),
        name="pack",
    )(meta, *near_core(near))
    got = lax.all_to_all(packed, ("x", "zp", "core"), 0, 0, tiled=True)
    window = pl.pallas_call(
        window_kernel,
        out_shape=jax.ShapeDtypeStruct((NM, 2, PATCH, COLS), bf16),
        in_specs=[smem_spec(), vmem_spec()],
        out_specs=any_spec(),
        scratch_shapes=[
            pltpu.VMEM((2, STRIPS * ROWS, COLS), f32),
            pltpu.VMEM((2, PATCH, COLS), bf16),
            pltpu.SemaphoreType.DMA((NM,)),
        ],
        compiler_params=pltpu.CompilerParams(vmem_limit_bytes=8 * 2**20),
        name="window",
    )(meta, *near_core(got))
    wins = lax.all_to_all(window, "mode", 0, 0, tiled=True)
    updates, misfit = pl.pallas_call(
        wave_kernel,
        out_shape=(
            jax.ShapeDtypeStruct((NX * BACK, SPAN // BACK, 2 * ROWS, COLS), bf16),
            jax.ShapeDtypeStruct((1, 1), f32),
        ),
        in_specs=[smem_spec()] + [vmem_spec()] * 10,
        out_specs=(vmem_spec(), vmem_spec()),
        scratch_shapes=[
            pltpu.VMEM((NM, PATCH, 2 * PATCH), f32),
            pltpu.VMEM((2, STRIPS * ROWS, COLS), f32),
        ],
        compiler_params=pltpu.CompilerParams(vmem_limit_bytes=24 * 2**20),
        name="wave",
    )(meta, *near_core(wins, *all_probes, side, turn, take, intensity, table))
    back = lax.all_to_all(updates, ("x", "core"), 0, 0, tiled=True)
    partial = pl.pallas_call(
        gather_kernel,
        out_shape=jax.ShapeDtypeStruct((PER_X // BACK, 2 * ROWS, COLS), bf16),
        in_specs=[smem_spec(), vmem_spec()],
        out_specs=vmem_spec(),
        scratch_shapes=[pltpu.VMEM((PER_X // BACK, 2 * ROWS, COLS), f32)],
        compiler_params=pltpu.CompilerParams(vmem_limit_bytes=8 * 2**20),
        name="gather",
    )(meta, *near_core(back))
    pieces = lax.all_to_all(partial, ("zq", "zp"), 0, 0, tiled=True)
    obj_later = lax.optimization_barrier(obj_x)
    base = obj_later + dual_u
    center = denoise(base, meta, w_in, b_in, w_down, b_down, w_mid, b_mid, w_out, b_out)
    aux_next = base - center
    numer = jnp.sum(pieces.astype(f32), axis=0).reshape(2, ROWS, COLS)
    obj_next = (numer + rho_weight * (aux_next - dual_u)) / (denom + rho_weight)
    dual_next = dual_u + obj_next - aux_next
    return (obj_next, aux_next, dual_next, misfit.reshape(1))


def solution(mesh):
    split = Mesh(mesh.devices.reshape(NX, PER_X // OUT, OUT // 2, 2, NM), TILE_AXES + ("mode",))
    grid = P(None, TILE_AXES, "mode")
    return jax.shard_map(
        per_device,
        mesh=split,
        in_specs=(
            grid,
            grid,
            P("mode", None, None, None),
            P(TILE_AXES, None, None),
        )
        + (P(),) * 10,
        out_specs=(grid, grid, grid, P(TILE_AXES)),
        check_vma=False,
    )
```
